32 devices in a mesh: rows: 8 (over z, x), scene: 4 (over y, core).
Axes of the slice: x: 2, y: 2, z: 4, core: 2. Of those that a mesh axis runs over, the one named last changes fastest.
Arguments:
- points: bfloat16 [32, 9, 32, 6144], P('scene', None, None, 'rows'), may hold values from -8 to 8
- pillar_counts: int32 [32, 6144], P('scene', 'rows'), may hold values from 0 to 32, as said below
- pillar_pixels: int32 [32, 6144], P('scene', 'rows'), may hold values from 0 to 8191, as said below
- point_weight: bfloat16 [9, 64], replicated, may hold values from -2 to 2
- point_master: float32 [9, 64], replicated, may hold values from -2 to 2
- point_states: float32 [3, 9, 64], replicated, as said below
- norm_weight: bfloat16 [4, 64], replicated, may hold values from -1.5 to 1.5, as said below
- norm_master: float32 [4, 64], replicated, may hold values from -1.5 to 1.5, as said below
- norm_states: float32 [3, 4, 64], replicated, as said below
- kernel_weight: bfloat16 [576, 64], P('rows'), may hold values from -0.25 to 0.25
- kernel_master: float32 [576, 64], P('rows'), may hold values from -0.25 to 0.25
- kernel_states: float32 [3, 576, 64], P(None, 'rows'), as said below
- step_count: int32 [1], replicated, may hold values from 1 to 20
- cotangent: bfloat16 [64, 32, 64, 256], P('rows', 'scene'), may hold values from -6 to 6
Outputs:
- result: bfloat16 [64, 32, 64, 256], P('rows', 'scene')
- point_master_new: float32 [9, 64], replicated
- point_states_new: float32 [2, 9, 64], replicated
- point_average_new: float32 [9, 64], replicated
- point_copy: bfloat16 [9, 64], replicated
- norm_master_new: float32 [4, 64], replicated
- norm_states_new: float32 [2, 4, 64], replicated
- norm_average_new: float32 [4, 64], replicated
- norm_copy: bfloat16 [4, 64], replicated
- kernel_master_new: float32 [576, 64], P('rows')
- kernel_states_new: float32 [2, 576, 64], P(None, 'rows')
- kernel_average_new: float32 [576, 64], P('rows')
- kernel_copy: bfloat16 [576, 64], P('rows')
The draws below stay inside these ranges and needn't reach their ends.
Inputs may be any that keep to these rules, and one draw needn't show every extreme that they name: `pillar_counts`: within each device's list of 768 slots the live pillars (count 1 or more) come first and the others have count 0; the first slot of every list holds 32 points; some device's list is live in every slot in every draw. `pillar_pixels`: A slot's cell is its row within the device's 16 rows times 512 plus its column; the cells of one device's list are distinct; the first 48 slots of each list lie in the device's last row and no other slot does; the first slot holds the device's last cell. `norm_weight`: rows 0 and 2 are gains, rows 1 and 3 biases. `norm_master`: rows 0 and 2 are gains, rows 1 and 3 biases. `point_states`: second moments are positive. `norm_states`: second moments are positive. `kernel_states`: second moments are positive.
All inputs are finite; a program needn't handle non-finite values.
Results may differ from the reference program's by a relative error of at most 0.002.
The reference program's roundings to bfloat16 on the way count: a program that leaves them out, or rounds other values in their place, can miss the bound.
Values may be sent and summed in bfloat16 or wider, within the bound.
No kernel may reach another device: no remote copies, remote signals or barrier semaphores. Data moves between devices by JAX's collectives and lax.ppermute only.
A program may use at most 256 MiB of HBM per device.

```python
import math
import jax
import jax.numpy as jnp
from jax import lax

CHANNELS = 64
FEATURES = 9
POINTS = 32
COLUMNS = 512
ROWS_DEV = 16
PIL_DEV = 768
SCENES = 32
CANVAS_ROWS = 128
PILLARS = 6144
OUT_ROWS = 64
OUT_COLUMNS = 256
EDGE_SLOTS = 48


def pixel_root():
    return float(SCENES * OUT_ROWS * OUT_COLUMNS) ** 0.5


def pillar_root():
    return float(SCENES * PILLARS * 0.6) ** 0.5


def norm_like(key):
    key_gain, key_bias = jax.random.split(key)
    gains = 1.0 + 0.15 * jax.random.uniform(key_gain, (2, CHANNELS), jnp.float32, -1.0, 1.0)
    biases = 0.3 * jnp.clip(jax.random.normal(key_bias, (2, CHANNELS), jnp.float32), -4.0, 4.0)
    return jnp.stack([gains[0], biases[0], gains[1], biases[1]])


def state_stack(key, array_shape, grad_size, average):
    key_first, key_second = jax.random.split(key)
    first = jnp.clip(jax.random.normal(key_first, array_shape, jnp.float32), -5.0, 5.0) * (0.111 * grad_size)
    second = grad_size * grad_size * 0.001 * jnp.exp(jax.random.uniform(key_second, array_shape, jnp.float32, 0.0, math.log(4.0)))
    return jnp.stack([first, second, average])


def draw_points(key, part):
    array_shape = (SCENES, FEATURES, POINTS, PILLARS)
    values = jnp.clip(jax.random.normal(key, array_shape, jnp.float32), -4.0, 4.0)
    return values.astype(jnp.bfloat16)


def draw_pillar_counts(key, part):
    slab_total = PILLARS // PIL_DEV
    key_live, key_power, key_extra = jax.random.split(jax.random.fold_in(key, 11), 3)
    slab_ids = jnp.arange(slab_total)
    base_live = PIL_DEV // 4 + (PIL_DEV - PIL_DEV // 4) * slab_ids // max(slab_total - 1, 1)
    live_slots = base_live[None, :] - jax.random.randint(key_live, (SCENES, slab_total), 0, PIL_DEV // 8 + 1)
    live_slots = jnp.clip(live_slots, 1, PIL_DEV)
    live_slots = jnp.where(slab_ids[None, :] == slab_total - 1, PIL_DEV, live_slots)
    powers = jax.random.randint(key_power, (SCENES, slab_total, PIL_DEV), 0, 6)
    extra_points = jax.random.randint(key_extra, (SCENES, slab_total, PIL_DEV), 0, jnp.left_shift(jnp.int32(1), powers))
    counts = jnp.minimum(1 + extra_points, POINTS)
    slot_index = jnp.arange(PIL_DEV)
    counts = jnp.where(slot_index[None, None, :] == 0, POINTS, counts)
    counts = jnp.where(slot_index[None, None, :] < live_slots[:, :, None], counts, 0)
    return counts.reshape(SCENES, PILLARS).astype(jnp.int32)


def draw_pillar_pixels(key, part):
    slab_total = PILLARS // PIL_DEV
    group_total = SCENES * slab_total
    upper_cells = (ROWS_DEV - 1) * COLUMNS
    key_edge, key_rest = jax.random.split(jax.random.fold_in(key, 12))
    edge_keys = jax.random.split(key_edge, group_total)
    rest_keys = jax.random.split(key_rest, group_total)

    def edge_order(single_key):
        return jax.random.permutation(single_key, COLUMNS)

    def rest_order(single_key):
        return jax.random.permutation(single_key, upper_cells)
    edge_columns = jax.vmap(edge_order)(edge_keys).astype(jnp.int32)
    last_column = COLUMNS - 1
    where_last = jnp.argmax(edge_columns == last_column, axis=1)
    rank_index = jnp.arange(COLUMNS)[None, :]
    first_column = edge_columns[:, :1]
    swapped = jnp.where(rank_index == where_last[:, None], first_column, edge_columns)
    swapped = jnp.where(rank_index == 0, last_column, swapped)
    edge_cells = swapped[:, :EDGE_SLOTS] + upper_cells
    rest_cells = jax.vmap(rest_order)(rest_keys).astype(jnp.int32)[:, :PIL_DEV - EDGE_SLOTS]
    joined = jnp.concatenate([edge_cells, rest_cells], axis=1)
    return joined.reshape(SCENES, PILLARS).astype(jnp.int32)


def draw_point_states(key, part):
    key_state, key_avg = jax.random.split(jax.random.fold_in(key, 13))
    average = jax.random.normal(key_avg, (FEATURES, CHANNELS), jnp.float32) * FEATURES ** (-0.5)
    return state_stack(key_state, (FEATURES, CHANNELS), pillar_root(), average)


def draw_norm_weight(key, part):
    return norm_like(jax.random.fold_in(key, 14)).astype(jnp.bfloat16)


def draw_norm_master(key, part):
    return norm_like(jax.random.fold_in(key, 15))


def draw_norm_states(key, part):
    key_state, key_avg = jax.random.split(jax.random.fold_in(key, 16))
    return state_stack(key_state, (4, CHANNELS), max(pixel_root(), pillar_root()), norm_like(key_avg))


def draw_kernel_states(key, part):
    key_state, key_avg = jax.random.split(jax.random.fold_in(key, 17))
    average = jax.random.normal(key_avg, (9 * CHANNELS, CHANNELS), jnp.float32) * (9 * CHANNELS) ** (-0.5)
    return state_stack(key_state, (9 * CHANNELS, CHANNELS), 0.7 * pixel_root(), average)


def steps_of(rng, extent, pieces, least, high):
    factor_of, own = 1.0, jax.random.fold_in(rng, 6)
    for dim, shards_of in pieces:
        draws = jnp.exp(jax.random.uniform(jax.random.fold_in(own, dim), (shards_of,), jnp.float32, least / len(pieces), high / len(pieces)))
        factor_of = factor_of * jnp.repeat(draws, extent[dim] // shards_of).reshape([-1 if axis == dim else 1 for axis in range(len(extent))])
    return factor_of


def centred(rng, shape, scale, limit, cuts=(), held_as=jnp.bfloat16):
    drawn = jax.random.normal(rng, shape, jnp.float32) * scale
    if len(cuts) > 0:
        drawn = steps_of(rng, shape, cuts, -0.22, 0.18) * drawn
    return jnp.clip(drawn, min=-limit, max=limit).astype(held_as)


def setup_inputs(seed: int = 0) -> dict:
    arg_keys = jax.random.split(jax.random.key(seed), 15)
    points = draw_points(jax.random.fold_in(arg_keys[14], 71), 0)
    pillar_counts = draw_pillar_counts(jax.random.fold_in(arg_keys[14], 71), 0)
    pillar_pixels = draw_pillar_pixels(jax.random.fold_in(arg_keys[14], 71), 0)
    point_weight = centred(arg_keys[3], (FEATURES, CHANNELS), FEATURES ** -0.5, 2.0)
    point_master = centred(arg_keys[4], (FEATURES, CHANNELS), FEATURES ** -0.5, 2.0, (), jnp.float32)
    point_states = draw_point_states(jax.random.fold_in(arg_keys[14], 71), 0)
    norm_weight = draw_norm_weight(jax.random.fold_in(arg_keys[14], 71), 0)
    norm_master = draw_norm_master(jax.random.fold_in(arg_keys[14], 71), 0)
    norm_states = draw_norm_states(jax.random.fold_in(arg_keys[14], 71), 0)
    kernel_weight = centred(arg_keys[9], (9 * CHANNELS, CHANNELS), (9 * CHANNELS) ** -0.5, 0.25, ((0, 8),))
    kernel_master = centred(arg_keys[10], (9 * CHANNELS, CHANNELS), (9 * CHANNELS) ** -0.5, 0.25, ((0, 8),), jnp.float32)
    kernel_states = draw_kernel_states(jax.random.fold_in(arg_keys[14], 71), 0)
    step_count = jax.random.randint(arg_keys[12], (1,), 1, 21).astype(jnp.int32)
    cotangent = centred(arg_keys[13], (OUT_ROWS, SCENES, CHANNELS, OUT_COLUMNS), 1.0, 6.0, ((0, 8), (1, 4)))
    return dict(points=points, pillar_counts=pillar_counts, pillar_pixels=pillar_pixels, point_weight=point_weight, point_master=point_master, point_states=point_states, norm_weight=norm_weight, norm_master=norm_master, norm_states=norm_states, kernel_weight=kernel_weight, kernel_master=kernel_master, kernel_states=kernel_states, step_count=step_count, cotangent=cotangent)


@jax.custom_vjp
def low(v):
    return lax.optimization_barrier(v.astype(jnp.bfloat16)).astype(jnp.float32)

@jax.custom_vjp
def low_back(v):
    return v

def low_keep(v):
    return (low(v), None)

def low_pass(kept, grad):
    return (grad,)

def back_keep(v):
    return (v, None)

def back_low(kept, grad):
    return (low(grad),)
low.defvjp(low_keep, low_pass)
low_back.defvjp(back_keep, back_low)
beta_one = 0.9
beta_two = 0.999
adam_eps = 1e-08
decay_rate = 0.01
average_keep = 0.99
norm_eps = 1e-05
rate_points = 0.3
rate_norms = 0.2
rate_kernel = 0.04

def adam_step(master, states, gradient, step_count, step_rate):
    moment = beta_one * states[0] + (1.0 - beta_one) * gradient
    second = beta_two * states[1] + (1.0 - beta_two) * gradient * gradient
    steps_done = step_count[0].astype(jnp.float32)
    first_fix = 1.0 - beta_one ** steps_done
    second_fix = 1.0 - beta_two ** steps_done
    fresh = master - step_rate * (moment / first_fix / (jnp.sqrt(second / second_fix) + adam_eps) + decay_rate * master)
    average = average_keep * states[2] + (1.0 - average_keep) * fresh
    return (fresh, jnp.stack([moment, second]), average, fresh.astype(jnp.bfloat16))

def reference(points, pillar_counts, pillar_pixels, point_weight, point_master, point_states, norm_weight, norm_master, norm_states, kernel_weight, kernel_master, kernel_states, step_count, cotangent):
    points_f = points.astype(jnp.float32)
    live_mask = (jnp.arange(POINTS)[None, :, None] < pillar_counts[:, None, :]).astype(jnp.float32)[:, None]
    slab_index = jnp.arange(PILLARS) // PIL_DEV
    row_at = (slab_index[None, :] * ROWS_DEV + pillar_pixels // COLUMNS).astype(jnp.int32)
    column_at = (pillar_pixels % COLUMNS).astype(jnp.int32)
    scene_at = jnp.broadcast_to(jnp.arange(SCENES)[:, None], pillar_pixels.shape).astype(jnp.int32)
    highest = lax.Precision.HIGHEST
    cells_all = float(OUT_ROWS * SCENES * OUT_COLUMNS)

    def forward(weight_points, weight_norm_values, weight_kernel):
        lifted_features = jnp.einsum('sinp,ic->scnp', points_f, weight_points, precision=highest)
        total_count = jnp.sum(live_mask)
        point_batch_mean = lax.optimization_barrier(jnp.sum(lifted_features * live_mask, axis=(0, 2, 3))) / total_count
        var_points = lax.optimization_barrier(jnp.sum(lifted_features * lifted_features * live_mask, axis=(0, 2, 3))) / total_count - point_batch_mean * point_batch_mean
        inverse_point_std = lax.rsqrt(var_points + norm_eps)
        normalized_points = (lifted_features - point_batch_mean[None, :, None, None]) * inverse_point_std[None, :, None, None]
        points_before_norm = weight_norm_values[0][None, :, None, None] * normalized_points + weight_norm_values[1][None, :, None, None]
        activated = jax.nn.relu(points_before_norm) * live_mask
        pooled = low(lax.optimization_barrier(jnp.max(activated, axis=2)))
        canvas = jnp.zeros((CANVAS_ROWS, SCENES, CHANNELS, COLUMNS), jnp.float32)
        canvas = canvas.at[row_at, scene_at, :, column_at].set(jnp.transpose(pooled, (0, 2, 1)))
        canvas = low_back(canvas)
        image_in = jnp.transpose(canvas, (1, 2, 0, 3))
        kernel_oihw = jnp.transpose(weight_kernel.reshape(3, 3, CHANNELS, CHANNELS), (3, 2, 0, 1))
        convolved_output = lax.conv_general_dilated(image_in, kernel_oihw, (2, 2), ((1, 1), (1, 1)), dimension_numbers=('NCHW', 'OIHW', 'NCHW'), precision=highest)
        convolved_output = low_back(jnp.transpose(convolved_output, (2, 0, 1, 3)))
        conv_batch_mean = lax.optimization_barrier(jnp.sum(convolved_output, axis=(0, 1, 3))) / cells_all
        var_conv = lax.optimization_barrier(jnp.sum(convolved_output * convolved_output, axis=(0, 1, 3))) / cells_all - conv_batch_mean * conv_batch_mean
        inverse_conv_std = lax.rsqrt(var_conv + norm_eps)
        normalized_conv = (convolved_output - conv_batch_mean[None, None, :, None]) * inverse_conv_std[None, None, :, None]
        conv_before_norm = weight_norm_values[2][None, None, :, None] * normalized_conv + weight_norm_values[3][None, None, :, None]
        return jax.nn.relu(conv_before_norm)
    output, pullback = jax.vjp(forward, point_weight.astype(jnp.float32), norm_weight.astype(jnp.float32), kernel_weight.astype(jnp.float32))
    point_grad, norm_grad, kernel_grad = pullback(cotangent.astype(jnp.float32))
    point_new, point_states_new, point_average_new, point_copy = adam_step(point_master, point_states, point_grad, step_count, rate_points)
    norm_new, norm_states_new, norm_average_new, norm_copy = adam_step(norm_master, norm_states, norm_grad, step_count, rate_norms)
    kernel_new, kernel_states_new, kernel_average_new, kernel_copy = adam_step(kernel_master, kernel_states, kernel_grad, step_count, rate_kernel)
    return (output.astype(jnp.bfloat16), point_new, point_states_new, point_average_new, point_copy, norm_new, norm_states_new, norm_average_new, norm_copy, kernel_new, kernel_states_new, kernel_average_new, kernel_copy)
```

```python
import functools

import jax
import jax.numpy as jnp
from jax import lax
from jax.experimental import pallas as pl
from jax.experimental.pallas import tpu as pltpu
from jax.sharding import PartitionSpec as P

beta_one = 0.9
beta_two = 0.999
adam_eps = 1e-08
decay_rate = 0.01
average_keep = 0.99
norm_eps = 1e-05
rate_points = 0.3
rate_norms = 0.2
rate_kernel = 0.04

EDGE = 48
BIG = 1e30
PACK = 16
PAD = 8
f32 = jnp.float32
bf16 = jnp.bfloat16


def iota(shape, dim):
    return lax.broadcasted_iota(jnp.int32, shape, dim)


def dot_nn(a, b):
    return lax.dot_general(a, b, (((1,), (0,)), ((), ())), preferred_element_type=f32)


def dot_nt(a, b):
    return lax.dot_general(a, b, (((1,), (1,)), ((), ())), preferred_element_type=f32)


def dot_tn(a, b):
    return lax.dot_general(a, b, (((0,), (0,)), ((), ())), preferred_element_type=f32)


def split3(x):
    a = x.astype(bf16)
    r = x - a.astype(f32)
    b = r.astype(bf16)
    c = (r - b.astype(f32)).astype(bf16)
    return a, b, c


def column(row, size):
    full = jnp.broadcast_to(row, (128, 128))
    return jnp.transpose(full)[:size]


def wide(row):
    return jnp.concatenate([row, jnp.zeros_like(row)], axis=1)


def lift_tables(weights, table):
    channels = weights.shape[1]
    cols = table.shape[1]
    spread = (iota((16, cols), 1) // PACK == iota((16, cols), 0)).astype(f32).astype(bf16)
    base = dot_tn(weights, spread)
    slot = iota(base.shape, 1) % PACK
    for n in range(PACK):
        table[n * channels : (n + 1) * channels, :] = jnp.where(slot == n, base, 0.0).astype(bf16)


def lift_inputs(points, count, half):
    feats = points.shape[0]
    size = points.shape[2]
    pts = points[:, half * PACK : (half + 1) * PACK, :]
    live = (iota((PACK, size), 0) + half * PACK < count).astype(f32)
    low = live.astype(bf16)
    dead = ((live - 1.0) * BIG).astype(bf16)
    kept = (pts * low[None]).reshape(feats * PACK, size)
    return jnp.concatenate([kept, low, dead], axis=0)


def lift_body(points, counts, pixels, weights, plain, z, edge, stats, moments, table, gram):
    s = pl.program_id(0)
    channels = weights.shape[1]
    feats = points.shape[1]
    depth = points.shape[2]
    size = points.shape[3]
    rows = (feats + 1) * PACK

    @pl.when(s == 0)
    def _():
        lift_tables(weights[...], table)
        gram[...] = jnp.zeros_like(gram)
        edge[...] = jnp.zeros_like(edge)

    count = counts[pl.ds(s, 1), :]
    tile = 256
    quads = PACK // 4
    best = [None] * (size // tile)
    total = None
    for half in range(depth // PACK):
        xin = lift_inputs(points.at[0], count, half)
        part = dot_nt(xin[:rows], xin[:rows])
        total = part if total is None else total + part
        for q in range(quads):
            lhs = table[q * 4 * channels : (q + 1) * 4 * channels, :]
            for t in range(size // tile):
                l = dot_nn(lhs, xin[:, t * tile : (t + 1) * tile])
                m = jnp.maximum(
                    jnp.maximum(l[:channels], l[channels : 2 * channels]),
                    jnp.maximum(l[2 * channels : 3 * channels], l[3 * channels :]),
                )
                best[t] = m if best[t] is None else jnp.maximum(best[t], m)
    gram[...] += total
    for t in range(size // tile):
        z[0, :, t * tile : (t + 1) * tile] = best[t]

    lanes = edge.shape[1]
    pix = pixels[pl.ds(s, 1), :][:, :128].astype(f32)
    flag = jnp.where(iota((8, 128), 0) == 0, pix, 1.0)
    head = jnp.concatenate([best[0][:, :128], flag], axis=0)
    head = jnp.concatenate([head, jnp.zeros((channels + 8, lanes - 128), f32)], axis=1)
    head = pltpu.roll(head, s * EDGE, axis=1)
    lane = iota((channels + 8, lanes), 1)
    edge[...] = jnp.where((lane >= s * EDGE) & (lane < (s + 1) * EDGE), head, edge[...])

    @pl.when(s == pl.num_programs(0) - 1)
    def _():
        g = gram[...]
        g = jnp.where(iota(g.shape, 0) % PACK == iota(g.shape, 1) % PACK, g, 0.0)
        pick = (iota((rows, 128), 0) // PACK == iota((rows, 128), 1)).astype(f32).astype(bf16)
        pick_t = (iota((16, rows), 1) // PACK == iota((16, rows), 0)).astype(f32).astype(bf16)
        a, b, c = split3(g)
        y = dot_nn(a, pick) + (dot_nn(b, pick) + dot_nn(c, pick))
        a, b, c = split3(y)
        m = dot_nn(pick_t, a) + (dot_nn(pick_t, b) + dot_nn(pick_t, c))
        moments[...] = m
        w = plain[...]
        a, b, c = split3(m[:, :16])
        aw = dot_nn(a, w) + (dot_nn(b, w) + dot_nn(c, w))
        two = jnp.sum(aw * w.astype(f32), axis=0, keepdims=True)
        one = aw[feats : feats + 1]
        row = jnp.concatenate([one, two, m[feats : feats + 1]], axis=1)
        stats[...] = jnp.broadcast_to(row, stats.shape)


def lift(points, counts, pixels, weights, plain, peers):
    scenes, feats, depth, size = points.shape
    channels = weights.shape[1]
    cols = (feats + 2) * PACK
    rows = (feats + 1) * PACK
    lanes = scenes * EDGE
    return pl.pallas_call(
        lift_body,
        grid=(scenes,),
        in_specs=[
            pl.BlockSpec((1, feats, depth, size), lambda s: (s, 0, 0, 0)),
            pl.BlockSpec((scenes, size), lambda s: (0, 0)),
            pl.BlockSpec((scenes, size), lambda s: (0, 0)),
            pl.BlockSpec((16, channels), lambda s: (0, 0)),
            pl.BlockSpec((16, channels), lambda s: (0, 0)),
        ],
        out_specs=[
            pl.BlockSpec((1, channels, size), lambda s: (s, 0, 0)),
            pl.BlockSpec((channels + 8, lanes), lambda s: (0, 0)),
            pl.BlockSpec((peers, 256), lambda s: (0, 0)),
            pl.BlockSpec((16, 128), lambda s: (0, 0)),
        ],
        out_shape=[
            jax.ShapeDtypeStruct((scenes, channels, size), f32),
            jax.ShapeDtypeStruct((channels + 8, lanes), f32),
            jax.ShapeDtypeStruct((peers, 256), f32),
            jax.ShapeDtypeStruct((16, 128), f32),
        ],
        scratch_shapes=[
            pltpu.VMEM((PACK * channels, cols), bf16),
            pltpu.VMEM((rows, rows), f32),
        ],
        name="lift",
    )(points, counts, pixels, weights, plain)


def conv_body(idx, stats, z, edge, norm, taps, conv, pooled, sums, params, rows_t, grid, carry, acc):
    s = pl.program_id(0)
    channels = z.shape[1]
    size = z.shape[2]
    out_rows = conv.shape[1]
    wide_cols = conv.shape[3]
    block = wide_cols + PAD
    half = (2 * out_rows + 1) * block

    @pl.when(s == 0)
    def _():
        tot = jnp.sum(stats[:, :256], axis=0, keepdims=True)
        count = tot[:, 137:138]
        mean = tot[:, :channels] / count
        inv = lax.rsqrt(tot[:, channels : 2 * channels] / count - mean * mean + norm_eps)
        params[0] = column(wide(mean), channels)
        params[1] = column(wide(inv), channels)
        nw = norm[...].astype(f32)
        params[2] = column(wide(nw[0:1]), channels)
        params[3] = column(wide(nw[1:2]), channels)
        grid[...] = jnp.zeros_like(grid)
        acc[...] = jnp.zeros_like(acc)

    def pool(x, ok):
        gain = params[2][:, :1]
        sign = jnp.where(gain > 0, 1.0, jnp.where(gain < 0, -1.0, 0.0))
        pre = gain * ((x * sign - params[0][:, :1]) * params[1][:, :1]) + params[3][:, :1]
        return jnp.where(ok, jnp.maximum(pre, 0.0), 0.0).astype(bf16)

    zs = z[0]
    own = pool(zs, zs > -0.5 * BIG)
    lanes = edge.shape[1]
    moved = pltpu.roll(edge[...], (lanes - s * EDGE) % lanes, axis=1)[:, :128]
    ze = moved[:channels]
    ok = (ze > -0.5 * BIG) & (moved[channels + 1 : channels + 2] > 0.5) & (iota((channels, 128), 1) < EDGE)
    far = pool(ze, ok)
    both = jnp.concatenate([own, far], axis=1)
    pooled[0] = both
    wf = both.astype(f32)
    rows_t[...] = jnp.transpose(jnp.concatenate([wf, wf], axis=0))

    step = 16

    def place(i, _):
        for j in range(step):
            p = i * step + j
            grid[pl.ds(idx[0, 0, p], 1), :] = rows_t[pl.ds(p, 1), :]
        return 0

    lax.fori_loop(0, (size + EDGE) // step, place, 0)

    low = iota((wide_cols, 128), 1) < channels

    def window(h):
        base = h * block + PAD
        even = grid[pl.ds(base, wide_cols), :]
        odd = grid[pl.ds(half + base, wide_cols), :]
        prev = grid[pl.ds(half + base - 1, wide_cols), :]
        both = jnp.where(low, even, odd)
        return jnp.concatenate([both, prev], axis=1).astype(bf16)

    def clear(h):
        base = pl.multiple_of(h * block + PAD, 8)
        grid[pl.ds(base, wide_cols), :] = jnp.zeros((wide_cols, 128), f32)
        grid[pl.ds(pl.multiple_of(half + base, 8), wide_cols), :] = jnp.zeros((wide_cols, 128), f32)

    carry[...] = dot_nt(taps[:channels], window(0))
    clear(0)

    def one_row(r, _):
        mid = dot_nt(taps[channels : 2 * channels], window(2 * r + 1))
        last = window(2 * r + 2)
        out = carry[...] + mid + dot_nt(taps[2 * channels :], last)
        carry[...] = dot_nt(taps[:channels], last)
        clear(2 * r + 1)
        clear(2 * r + 2)
        conv[0, r] = out
        square = out * out
        for t in range(wide_cols // 128):
            acc[:channels] += out[:, t * 128 : (t + 1) * 128]
            acc[channels:] += square[:, t * 128 : (t + 1) * 128]
        return 0

    lax.fori_loop(0, out_rows, one_row, 0)

    @pl.when(s == pl.num_programs(0) - 1)
    def _():
        row = jnp.sum(jnp.transpose(acc[...]), axis=0, keepdims=True)
        sums[...] = jnp.broadcast_to(row, sums.shape)


def convolve(idx, stats, z, edge, norm, taps, out_rows, wide_cols):
    scenes, channels, size = z.shape
    peers = stats.shape[0]
    lanes = edge.shape[1]
    block = wide_cols + PAD
    half = (2 * out_rows + 1) * block
    return pl.pallas_call(
        conv_body,
        grid=(scenes,),
        in_specs=[
            pl.BlockSpec((1, 1, idx.shape[2]), lambda s: (s, 0, 0), memory_space=pltpu.SMEM),
            pl.BlockSpec(stats.shape, lambda s: (0, 0)),
            pl.BlockSpec((1, channels, size), lambda s: (s, 0, 0)),
            pl.BlockSpec((channels + 8, lanes), lambda s: (0, 0)),
            pl.BlockSpec((4, channels), lambda s: (0, 0)),
            pl.BlockSpec((3 * channels, 4 * channels), lambda s: (0, 0)),
        ],
        out_specs=[
            pl.BlockSpec((1, out_rows, channels, wide_cols), lambda s: (s, 0, 0, 0)),
            pl.BlockSpec((1, channels, size + 128), lambda s: (s, 0, 0)),
            pl.BlockSpec((peers, 128), lambda s: (0, 0)),
        ],
        out_shape=[
            jax.ShapeDtypeStruct((scenes, out_rows, channels, wide_cols), f32),
            jax.ShapeDtypeStruct((scenes, channels, size + 128), bf16),
            jax.ShapeDtypeStruct((peers, 128), f32),
        ],
        scratch_shapes=[
            pltpu.VMEM((4, channels, 128), f32),
            pltpu.VMEM((size + 128, 128), f32),
            pltpu.VMEM((2 * half, 128), f32),
            pltpu.VMEM((channels, wide_cols), f32),
            pltpu.VMEM((2 * channels, 128), f32),
        ],
        name="convolve",
    )(idx, stats, z, edge, norm, taps)


def conv_params(cells, stats, norm, params):
    channels = params.shape[1]
    tot = jnp.sum(stats[...], axis=0, keepdims=True)
    mean = tot[:, :channels] / cells
    inv = lax.rsqrt(tot[:, channels:] / cells - mean * mean + norm_eps)
    nw = norm[...].astype(f32)
    params[0] = column(wide(mean), channels)
    params[1] = column(wide(inv), channels)
    params[2] = column(wide(nw[2:3]), channels)
    params[3] = column(wide(nw[3:4]), channels)


def norm_body(cells, stats, conv, cot, norm, result, sums, params, acc):
    s = pl.program_id(0)
    channels = conv.shape[2]

    @pl.when(s == 0)
    def _():
        conv_params(cells, stats, norm, params)
        acc[...] = jnp.zeros_like(acc)

    bias = jnp.zeros((channels, 128), f32)
    gain = jnp.zeros((channels, 128), f32)
    for r in range(conv.shape[1]):
        xhat = (conv[0, r] - params[0][:, :1]) * params[1][:, :1]
        pre = params[2][:, :1] * xhat + params[3][:, :1]
        result[r, 0] = jnp.maximum(pre, 0.0).astype(bf16)
        back = jnp.where(pre > 0, cot[r, 0].astype(f32), 0.0)
        prod = back * xhat
        for t in range(conv.shape[3] // 128):
            bias = bias + back[:, t * 128 : (t + 1) * 128]
            gain = gain + prod[:, t * 128 : (t + 1) * 128]
    acc[:channels] += bias
    acc[channels:] += gain

    @pl.when(s == pl.num_programs(0) - 1)
    def _():
        row = jnp.sum(jnp.transpose(acc[...]), axis=0, keepdims=True)
        sums[...] = jnp.broadcast_to(row, sums.shape)


def normalize(cells, stats, conv, cot, norm):
    scenes, out_rows, channels, wide_cols = conv.shape
    peers = stats.shape[0]
    return pl.pallas_call(
        functools.partial(norm_body, cells),
        grid=(scenes,),
        in_specs=[
            pl.BlockSpec((peers, 128), lambda s: (0, 0)),
            pl.BlockSpec((1, out_rows, channels, wide_cols), lambda s: (s, 0, 0, 0)),
            pl.BlockSpec((out_rows, 1, channels, wide_cols), lambda s: (0, s, 0, 0)),
            pl.BlockSpec((4, channels), lambda s: (0, 0)),
        ],
        out_specs=[
            pl.BlockSpec((out_rows, 1, channels, wide_cols), lambda s: (0, s, 0, 0)),
            pl.BlockSpec((peers, 128), lambda s: (0, 0)),
        ],
        out_shape=[
            jax.ShapeDtypeStruct((out_rows, scenes, channels, wide_cols), bf16),
            jax.ShapeDtypeStruct((peers, 128), f32),
        ],
        scratch_shapes=[pltpu.VMEM((4, channels, 128), f32), pltpu.VMEM((2 * channels, 128), f32)],
        name="normalize",
    )(stats, conv, cot, norm)


def grad_body(
    cells, idx, stats, sums, conv, cot, norm, pooled, phase, taps, slots, slots_far, kgrad, params, field, left, right, acc
):
    s = pl.program_id(0)
    channels = conv.shape[2]
    out_rows = conv.shape[1]
    cols = conv.shape[3]
    size = slots.shape[2]

    @pl.when(s == 0)
    def _():
        conv_params(cells, stats, norm, params)
        tot = jnp.sum(sums[...], axis=0, keepdims=True)
        params[4] = column(wide(tot[:, :channels]), channels)
        params[5] = column(wide(tot[:, channels:]), channels)
        params[6] = params[2] * params[1] / cells
        field[...] = jnp.zeros_like(field)
        left[...] = jnp.zeros_like(left)
        right[...] = jnp.zeros_like(right)
        acc[...] = jnp.zeros_like(acc)
        slots_far[...] = jnp.zeros_like(slots_far)

    inside = iota((channels, cols), 1) < cols - 1
    for r in range(out_rows):
        xhat = (conv[0, r] - params[0][:, :1]) * params[1][:, :1]
        pre = params[2][:, :1] * xhat + params[3][:, :1]
        back = jnp.where(pre > 0, cot[r, 0].astype(f32), 0.0)
        grad = params[6][:, :1] * (cells * back - params[4][:, :1] - xhat * params[5][:, :1])
        grad = grad.astype(bf16).astype(f32)
        after = jnp.where(inside, pltpu.roll(grad, cols - 1, axis=1), 0.0)
        field[(r + 1) * cols : (r + 2) * cols, :] = jnp.transpose(jnp.concatenate([grad, after], axis=0))

    step = 16

    def take(i, _):
        for j in range(step):
            p = i * step + j
            k = idx[0, 0, p]
            left[pl.ds(p, 1), :] = field[pl.ds(k, 1), :]
            right[pl.ds(p, 1), :] = field[pl.ds(k + cols, 1), :]
        return 0

    lax.fori_loop(0, (size + EDGE) // step, take, 0)

    total = None
    start = 0
    while start < size + 128:
        tile = min(256, size + 128 - start)
        part = jnp.concatenate([left[start : start + tile], right[start : start + tile]], axis=1).astype(bf16)
        ph = phase[0, :, start : start + tile]
        out = dot_nt(taps[...], part)
        value = jnp.where(
            ph < 2,
            jnp.where(ph == 0, out[:channels], out[channels : 2 * channels]),
            jnp.where(ph == 2, out[2 * channels : 3 * channels], out[3 * channels :]),
        )
        if start < size:
            slots[0, :, start : start + tile] = value
        else:
            lanes = slots_far.shape[1]
            far = jnp.concatenate([value, jnp.zeros((channels, lanes - 128), f32)], axis=1)
            far = pltpu.roll(far, s * EDGE, axis=1)
            lane = iota((channels, lanes), 1)
            slots_far[...] = jnp.where((lane >= s * EDGE) & (lane < (s + 1) * EDGE), far, slots_far[...])
        pf = pooled[0, :, start : start + tile].astype(f32)
        split = jnp.concatenate([jnp.where(ph == k, pf, 0.0) for k in range(4)], axis=0).astype(bf16)
        prod = dot_nn(split, part)
        total = prod if total is None else total + prod
        start += tile
    acc[...] += total

    @pl.when(s == pl.num_programs(0) - 1)
    def _():
        full = acc[...]
        for a in range(3):
            for b in range(3):
                hp, dr = ((1, 1), (0, 0), (1, 0))[a]
                up, dw = ((1, 1), (0, 0), (1, 0))[b]
                row, col = hp * 2 + up, dr * 2 + dw
                tap = 3 * a + b
                kgrad[tap * channels : (tap + 1) * channels, :] = full[
                    row * channels : (row + 1) * channels, col * channels : (col + 1) * channels
                ]


def gradients(cells, idx, stats, sums, conv, cot, norm, pooled, phase, taps):
    scenes, out_rows, channels, wide_cols = conv.shape
    peers = stats.shape[0]
    size = pooled.shape[2] - 128
    lanes = scenes * EDGE
    return pl.pallas_call(
        functools.partial(grad_body, cells),
        grid=(scenes,),
        in_specs=[
            pl.BlockSpec((1, 1, idx.shape[2]), lambda s: (s, 0, 0), memory_space=pltpu.SMEM),
            pl.BlockSpec((peers, 128), lambda s: (0, 0)),
            pl.BlockSpec((peers, 128), lambda s: (0, 0)),
            pl.BlockSpec((1, out_rows, channels, wide_cols), lambda s: (s, 0, 0, 0)),
            pl.BlockSpec((out_rows, 1, channels, wide_cols), lambda s: (0, s, 0, 0)),
            pl.BlockSpec((4, channels), lambda s: (0, 0)),
            pl.BlockSpec((1, channels, size + 128), lambda s: (s, 0, 0)),
            pl.BlockSpec((1, 1, size + 128), lambda s: (s, 0, 0)),
            pl.BlockSpec((4 * channels, 4 * channels), lambda s: (0, 0)),
        ],
        out_specs=[
            pl.BlockSpec((1, channels, size), lambda s: (s, 0, 0)),
            pl.BlockSpec((channels, lanes), lambda s: (0, 0)),
            pl.BlockSpec((9 * channels, channels), lambda s: (0, 0)),
        ],
        out_shape=[
            jax.ShapeDtypeStruct((scenes, channels, size), f32),
            jax.ShapeDtypeStruct((channels, lanes), f32),
            jax.ShapeDtypeStruct((9 * channels, channels), f32),
        ],
        scratch_shapes=[
            pltpu.VMEM((7, channels, 128), f32),
            pltpu.VMEM(((out_rows + 2) * wide_cols, 128), f32),
            pltpu.VMEM((size + 128, 128), f32),
            pltpu.VMEM((size + 128, 128), f32),
            pltpu.VMEM((4 * channels, 4 * channels), f32),
        ],
        name="gradients",
    )(idx, stats, sums, conv, cot, norm, pooled, phase, taps)


def unlift_body(points, counts, weights, z, pooled, slots, slots_far, out, table, acc, mult):
    s = pl.program_id(0)
    channels = weights.shape[1]
    feats = points.shape[1]
    depth = points.shape[2]
    size = points.shape[3]
    cols = (feats + 2) * PACK
    rows = (feats + 1) * PACK

    @pl.when(s == 0)
    def _():
        lift_tables(weights[...], table)
        acc[...] = jnp.zeros_like(acc)

    count = counts[pl.ds(s, 1), :]
    tile = 256
    quads = PACK // 4
    zs = z[0]
    live = zs > -0.5 * BIG
    zs = jnp.where(live, zs, BIG)
    lanes = slots_far.shape[1]
    far = pltpu.roll(slots_far[...], (lanes - s * EDGE) % lanes, axis=1)[:, :128]
    far = jnp.where(iota((channels, 128), 1) < EDGE, far, 0.0)
    raw = slots[0]
    raw = jnp.concatenate([raw[:, :128] + far, raw[:, 128:]], axis=1)
    grad = jnp.where(pooled[0].astype(f32) > 0, raw.astype(bf16).astype(f32), 0.0)

    def visit(fn):
        for half in range(depth // PACK):
            xin = lift_inputs(points.at[0], count, half)
            for q in range(quads):
                lhs = table[q * 4 * channels : (q + 1) * 4 * channels, :]
                pieces = []
                for t in range(size // tile):
                    l = dot_nn(lhs, xin[:, t * tile : (t + 1) * tile])
                    sub = []
                    for k in range(4):
                        sub.append(fn(t, l[k * channels : (k + 1) * channels] == zs[:, t * tile : (t + 1) * tile]))
                    pieces.append(jnp.concatenate(sub, axis=0))
                yield q, xin[:rows], jnp.concatenate(pieces, axis=1)

    def fold(q, prod):
        slot = iota((channels, rows), 1) % PACK
        part = None
        for k in range(4):
            one = jnp.where(slot == q * 4 + k, prod[k * channels : (k + 1) * channels], 0.0)
            part = one if part is None else part + one
        return part

    ties = [jnp.zeros((channels, tile), f32) for _ in range(size // tile)]

    def first(t, win):
        ties[t] = ties[t] + jnp.where(win, 1.0, 0.0)
        return jnp.where(win, grad[:, t * tile : (t + 1) * tile], 0.0)

    total = None
    for q, xin, value in visit(first):
        part = fold(q, dot_nt(value.astype(bf16), xin))
        total = part if total is None else total + part
    acc[...] += total
    most = ties[0]
    for t in range(1, size // tile):
        most = jnp.maximum(most, ties[t])
    for t in range(size // tile):
        mult[:, t * tile : (t + 1) * tile] = ties[t]

    @pl.when(jnp.max(most) > 1.5)
    def _():
        scaled = jnp.where(mult[...] > 1.5, grad / jnp.maximum(mult[...], 1.0) - grad, 0.0)

        def second(t, win):
            return jnp.where(win, scaled[:, t * tile : (t + 1) * tile], 0.0)

        more = None
        for q, xin, value in visit(second):
            a, b, c = split3(value)
            part = fold(q, dot_nt(a, xin) + (dot_nt(b, xin) + dot_nt(c, xin)))
            more = part if more is None else more + part
        acc[...] += more

    @pl.when(s == pl.num_programs(0) - 1)
    def _():
        pick_t = (iota((16, rows), 1) // PACK == iota((16, rows), 0)).astype(f32).astype(bf16)
        a, b, c = split3(acc[...])
        out[...] = dot_nt(pick_t, a) + (dot_nt(pick_t, b) + dot_nt(pick_t, c))


def unlift(points, counts, weights, z, pooled, slots, slots_far):
    scenes, feats, depth, size = points.shape
    channels = weights.shape[1]
    cols = (feats + 2) * PACK
    rows = (feats + 1) * PACK
    lanes = scenes * EDGE
    return pl.pallas_call(
        unlift_body,
        grid=(scenes,),
        in_specs=[
            pl.BlockSpec((1, feats, depth, size), lambda s: (s, 0, 0, 0)),
            pl.BlockSpec((scenes, size), lambda s: (0, 0)),
            pl.BlockSpec((16, channels), lambda s: (0, 0)),
            pl.BlockSpec((1, channels, size), lambda s: (s, 0, 0)),
            pl.BlockSpec((1, channels, size), lambda s: (s, 0, 0)),
            pl.BlockSpec((1, channels, size), lambda s: (s, 0, 0)),
            pl.BlockSpec((channels, lanes), lambda s: (0, 0)),
        ],
        out_specs=pl.BlockSpec((16, channels), lambda s: (0, 0)),
        out_shape=jax.ShapeDtypeStruct((16, channels), f32),
        scratch_shapes=[
            pltpu.VMEM((PACK * channels, cols), bf16),
            pltpu.VMEM((channels, rows), f32),
            pltpu.VMEM((channels, size), f32),
        ],
        name="unlift",
    )(points, counts, weights, z, pooled, slots, slots_far)


def adam_step(master, states, gradient, step_count, step_rate):
    moment = beta_one * states[0] + (1.0 - beta_one) * gradient
    second = beta_two * states[1] + (1.0 - beta_two) * gradient * gradient
    steps_done = step_count[0].astype(jnp.float32)
    first_fix = 1.0 - beta_one**steps_done
    second_fix = 1.0 - beta_two**steps_done
    fresh = master - step_rate * (
        moment / first_fix / (jnp.sqrt(second / second_fix) + adam_eps) + decay_rate * master
    )
    average = average_keep * states[2] + (1.0 - average_keep) * fresh
    return (fresh, jnp.stack([moment, second]), average, fresh.astype(jnp.bfloat16))


def shifted(x, by):
    length = lax.axis_size("rows")
    pairs = [(i, i + by) for i in range(length) if 0 <= i + by < length]
    return lax.ppermute(x, "rows", pairs)


def exchange(x):
    return lax.all_to_all(x, ("rows", "scene"), 0, 0, tiled=True)


def scene_sum(x):
    length = lax.axis_size("scene")
    if length & (length - 1):
        return lax.psum(x, "scene")
    by = 1
    while by < length:
        x = x + lax.ppermute(x, "scene", [(i, i ^ by) for i in range(length)])
        by *= 2
    return x


def body(
    points,
    pillar_counts,
    pillar_pixels,
    point_weight,
    point_master,
    point_states,
    norm_weight,
    norm_master,
    norm_states,
    kernel_weight,
    kernel_master,
    kernel_states,
    step_count,
    cotangent,
):
    feats = points.shape[1]
    size = points.shape[3]
    out_rows, scenes, channels, out_cols = cotangent.shape
    cols = 2 * out_cols
    row_devices = lax.axis_size("rows")
    scene_devices = lax.axis_size("scene")
    peers = row_devices * scene_devices
    cells = float(out_rows * scenes * out_cols * peers)
    own = kernel_weight.shape[0]
    share = own * channels
    cut = scene_devices if share % (scene_devices * 128) == 0 else 1
    mine = lax.axis_index("scene") if cut > 1 else 0

    def my_part(flat):
        return lax.dynamic_index_in_dim(flat.reshape(-1, cut, share // cut), mine, 1, keepdims=False)

    gain_row = norm_weight[0:1].astype(f32)
    sign = jnp.sign(gain_row)
    plain = jnp.zeros((16, channels), f32).at[:feats].set(point_weight.astype(f32))
    signed = (plain * sign).at[feats + 1].set(1.0).astype(bf16)
    plain = plain.astype(bf16)

    z, edge, stats, moments = lift(points, pillar_counts, pillar_pixels, signed, plain, peers)
    edge = shifted(edge, 1)
    kpart = my_part(kernel_weight.astype(f32).reshape(1, share))
    got = exchange(jnp.concatenate([stats, jnp.broadcast_to(kpart, (peers, share // cut))], axis=1))
    stats = got[:, :256]
    kern = got[:, 256:].reshape(row_devices, scene_devices, share // cut)
    if cut == 1:
        kern = kern[:, :1]
    kern = kern.reshape(3, 3, channels, channels)

    far_pixels = edge[channels].reshape(scenes, EDGE).astype(jnp.int32)
    far_row = jnp.full((scenes, EDGE), -1, jnp.int32)
    row_at = jnp.concatenate([pillar_pixels // cols, far_row], axis=1)
    col_at = jnp.concatenate([pillar_pixels % cols, far_pixels % cols], axis=1)
    odd_col = col_at % 2
    at = col_at // 2
    place_at = odd_col * ((2 * out_rows + 1) * (out_cols + PAD)) + (row_at + 1) * (out_cols + PAD) + PAD + at
    take_at = ((row_at + 2) // 2) * out_cols + at
    phase = (row_at % 2) * 2 + odd_col
    phase = jnp.pad(phase, ((0, 0), (0, 128 - EDGE)))

    back_taps = jnp.transpose(kern, (0, 3, 1, 2))
    zero = jnp.zeros((3, channels, channels), f32)
    fore = jnp.stack([back_taps[:, :, 1], back_taps[:, :, 2], back_taps[:, :, 0], zero], axis=2)
    fore = fore.reshape(3 * channels, 4 * channels).astype(bf16)
    blocks = []
    none = jnp.zeros((channels, channels), f32)
    tap_of = ((1, None), (2, 0))
    for hp in range(2):
        for up in range(2):
            line = []
            for dr in range(2):
                for dw in range(2):
                    a, b = tap_of[hp][dr], tap_of[up][dw]
                    line.append(none if a is None or b is None else kern[a, b])
            blocks.append(jnp.concatenate(line, axis=1))
    aft = jnp.concatenate(blocks, axis=0).astype(bf16)

    conv, pooled, sums = convolve(place_at[:, None], stats, z, edge, norm_weight, fore, out_rows, out_cols)
    conv_stats = exchange(sums)
    result, sums = normalize(cells, conv_stats, conv, cotangent, norm_weight)
    grad_sums = exchange(sums)
    slots, slots_far, kgrad = gradients(
        cells, take_at[:, None], conv_stats, grad_sums, conv, cotangent, norm_weight, pooled, phase[:, None], aft
    )
    slots_far = shifted(slots_far, -1)
    kgrad = scene_sum(kgrad)
    cross = unlift(points, pillar_counts, signed, z, pooled, slots, slots_far)

    kpart = my_part(kgrad.reshape(row_devices, share))
    kpart = jnp.broadcast_to(kpart[:, None], (row_devices, scene_devices, share // cut)).reshape(peers, -1)
    rest = jnp.concatenate([cross[: feats + 1].reshape(-1), moments[: feats + 1, :16].reshape(-1)])
    pad = -rest.shape[0] % 128
    rest = jnp.broadcast_to(jnp.pad(rest, (0, pad))[None], (peers, rest.shape[0] + pad))
    got = exchange(jnp.concatenate([kpart, rest], axis=1))
    kernel_own = jnp.sum(got[:, : share // cut].reshape(row_devices, scene_devices, share // cut), axis=0)
    if cut == 1:
        kernel_own = kernel_own[:1]
    kernel_own = kernel_own.reshape(own, channels)
    rest = jnp.sum(got[:, share // cut :], axis=0)
    cross = rest[: (feats + 1) * channels].reshape(feats + 1, channels)
    moments = rest[(feats + 1) * channels : (feats + 1) * (channels + 16)].reshape(feats + 1, 16)[:, : feats + 1]

    weight = point_weight.astype(f32)
    total = moments[feats, feats]
    firsts = moments[:feats, feats]
    mixed = jnp.sum(moments[:feats, :feats, None] * weight[None], axis=1)
    mean = jnp.sum(firsts[:, None] * weight, axis=0) / total
    inv = lax.rsqrt(jnp.sum(mixed * weight, axis=0) / total - mean * mean + norm_eps)
    bias_p = cross[feats]
    gain_p = inv * (jnp.sum(weight * cross[:feats], axis=0) - mean * bias_p)
    spread = inv * (mixed - firsts[:, None] * mean)
    point_total = (norm_weight[0].astype(f32) * inv) * (
        cross[:feats] - (firsts[:, None] * bias_p + spread * gain_p) / total
    )
    both = jnp.sum(grad_sums, axis=0)
    norm_grad = jnp.stack([gain_p, bias_p, both[channels:], both[:channels]])

    outs = [result]
    outs += adam_step(point_master, point_states, point_total, step_count, rate_points)
    outs += adam_step(norm_master, norm_states, norm_grad, step_count, rate_norms)
    outs += adam_step(kernel_master, kernel_states, kernel_own, step_count, rate_kernel)
    return tuple(outs)


def solution(mesh):
    placed = (
        P("scene", None, None, "rows"),
        P("scene", "rows"),
        P("scene", "rows"),
        P(),
        P(),
        P(),
        P(),
        P(),
        P(),
        P("rows", None),
        P("rows", None),
        P(None, "rows", None),
        P(),
        P("rows", "scene", None, None),
    )
    return jax.shard_map(
        body,
        mesh=mesh,
        in_specs=placed,
        out_specs=(
            P("rows", "scene", None, None),
            P(),
            P(),
            P(),
            P(),
            P(),
            P(),
            P(),
            P(),
            P("rows", None),
            P(None, "rows", None),
            P("rows", None),
            P("rows", None),
        ),
        check_vma=False,
    )
```

```python
import functools

import jax
import jax.numpy as jnp
from jax import lax
from jax.experimental import pallas as pl
from jax.experimental.pallas import tpu as pltpu
from jax.sharding import PartitionSpec as P

beta_one = 0.9
beta_two = 0.999
adam_eps = 1e-08
decay_rate = 0.01
average_keep = 0.99
norm_eps = 1e-05
rate_points = 0.3
rate_norms = 0.2
rate_kernel = 0.04

EDGE = 48
BIG = 1e30
PACK = 16
TILE = 256
LANES = 128
f32 = jnp.float32
bf16 = jnp.bfloat16


def iota(shape, dim):
    return lax.broadcasted_iota(jnp.int32, shape, dim)


def dot_nn(a, b):
    return lax.dot_general(a, b, (((1,), (0,)), ((), ())), preferred_element_type=f32)


def dot_nt(a, b):
    return lax.dot_general(a, b, (((1,), (1,)), ((), ())), preferred_element_type=f32)


def dot_tn(a, b):
    return lax.dot_general(a, b, (((0,), (0,)), ((), ())), preferred_element_type=f32)


def split3(x):
    a = x.astype(bf16)
    r = x - a.astype(f32)
    b = r.astype(bf16)
    c = (r - b.astype(f32)).astype(bf16)
    return a, b, c


def exact_left(x, y):
    a, b, c = split3(x)
    return dot_nn(a, y) + (dot_nn(b, y) + dot_nn(c, y))


def exact_right(x, y):
    a, b, c = split3(y)
    return dot_nn(x, a) + (dot_nn(x, b) + dot_nn(x, c))


def swap_halves(x):
    return pltpu.roll(x, x.shape[1] // 2, axis=1)


def twice(row):
    return jnp.concatenate([row, row], axis=1)


def one_hot_rows(rows, cols):
    return (iota((rows, cols), 0) // PACK == iota((rows, cols), 1)).astype(f32).astype(bf16)


def one_hot_cols(rows, cols):
    return (iota((rows, cols), 1) // PACK == iota((rows, cols), 0)).astype(f32).astype(bf16)


def lift_table(weight, norm, table):
    feats, channels = weight.shape
    rows = table.shape[0]
    gain = norm[0:1, :].astype(f32)
    sign = jnp.where(gain > 0, 1.0, jnp.where(gain < 0, -1.0, 0.0))
    signed = weight[...].astype(f32) * sign
    full = jnp.concatenate([signed, jnp.zeros((1, channels), f32), jnp.ones((1, channels), f32)], axis=0)
    full = jnp.concatenate([full, jnp.zeros((16 - feats - 2, channels), f32)], axis=0)
    base = dot_nn(one_hot_rows(rows, 16), twice(full).astype(bf16))
    slot = iota(base.shape, 0) % PACK
    half = iota(base.shape, 1) // channels
    for m in range(PACK // 2):
        table[:, m * LANES : (m + 1) * LANES] = jnp.where(slot == 2 * m + half, base, 0.0).astype(bf16)


def lift_inputs(points, count, half):
    feats = points.shape[0]
    size = points.shape[2]
    pts = points[:, half * PACK : (half + 1) * PACK, :]
    live = (iota((PACK, size), 0) + half * PACK < count).astype(f32)
    low = live.astype(bf16)
    dead = ((live - 1.0) * BIG).astype(bf16)
    kept = (pts * low[None]).reshape(feats * PACK, size)
    return jnp.concatenate([kept, low, dead], axis=0)


def lift_body(mine, points, counts, pixels, weight, norm, kernel, z, edge, payload, moments, table, gram, best, wide):
    s = pl.program_id(0)
    scenes = pl.num_programs(0)
    feats, channels = weight.shape
    depth = points.shape[2]
    size = points.shape[3]
    rows = (feats + 1) * PACK

    @pl.when(s == 0)
    def _():
        lift_table(weight, norm, table)
        gram[...] = jnp.zeros_like(gram)
        edge[...] = jnp.zeros_like(edge)
        wide[...] = kernel[...].astype(f32)

    count = counts[pl.ds(s, 1), :]
    tiles = size // TILE
    total = None
    for half in range(depth // PACK):
        xin = lift_inputs(points.at[0], count, half)
        part = dot_nt(xin[:rows], xin[:rows])
        total = part if total is None else total + part
        turned = [jnp.transpose(xin[:, t * TILE : (t + 1) * TILE]) for t in range(tiles)]
        for q in range(PACK // 4):
            rhs = table[:, q * 256 : (q + 1) * 256]
            for t in range(tiles):
                l = dot_nn(turned[t], rhs)
                m = jnp.maximum(l[:, :LANES], l[:, LANES:])
                at = slice(t * TILE, (t + 1) * TILE)
                if half == 0 and q == 0:
                    best[at, :] = m
                elif half == depth // PACK - 1 and q == PACK // 4 - 1:
                    m = jnp.maximum(best[at, :], m)
                    m = jnp.maximum(m, swap_halves(m))
                    z[0, at, :] = m
                else:
                    best[at, :] = jnp.maximum(best[at, :], m)
    gram[...] += total

    lower = iota((EDGE, LANES), 1) < channels
    spot = pl.ds(pl.multiple_of((s % (scenes // 2)) * EDGE, 8), EDGE)
    first = s < scenes // 2
    edge[spot, :] = jnp.where(lower == first, z[0, :EDGE, :], edge[spot, :])

    @pl.when(s == scenes - 1)
    def _():
        count_rows = edge.shape[0] - 2 * scenes
        edge[count_rows : count_rows + scenes, :] = pixels[:, :LANES].astype(f32)
        edge[count_rows + scenes :, :] = jnp.ones((scenes, LANES), f32)
        g = gram[...]
        g = jnp.where(iota(g.shape, 0) % PACK == iota(g.shape, 1) % PACK, g, 0.0)
        y = exact_left(g, one_hot_rows(rows, LANES))
        m = exact_right(one_hot_cols(16, rows), y)
        moments[...] = m
        w = jnp.concatenate([weight[...].astype(f32), jnp.zeros((16 - feats, channels), f32)], axis=0)
        aw = exact_left(m[:, :16], w.astype(bf16))
        two = jnp.sum(aw * w, axis=0, keepdims=True)
        one = aw[feats : feats + 1]
        pieces = [one, two, m[feats : feats + 1]]
        share = (payload.shape[1] - 256) // channels
        for j in range(share):
            pieces.append(wide[pl.ds(mine[0, 0] * share + j, 1), :])
        payload[...] = jnp.broadcast_to(jnp.concatenate(pieces, axis=1), payload.shape)


def lift(mine, points, counts, pixels, weight, norm, kernel, peers, share):
    scenes, feats, depth, size = points.shape
    channels = weight.shape[1]
    full = (feats + 2) * PACK
    rows = (feats + 1) * PACK
    edge_rows = scenes // 2 * EDGE + 2 * scenes
    fixed = lambda s: (0, 0)
    return pl.pallas_call(
        lift_body,
        grid=(scenes,),
        in_specs=[
            pl.BlockSpec((1, 1), fixed, memory_space=pltpu.SMEM),
            pl.BlockSpec((1, feats, depth, size), lambda s: (s, 0, 0, 0)),
            pl.BlockSpec((scenes, size), fixed),
            pl.BlockSpec((scenes, size), fixed),
            pl.BlockSpec(weight.shape, fixed),
            pl.BlockSpec(norm.shape, fixed),
            pl.BlockSpec(kernel.shape, fixed),
        ],
        out_specs=[
            pl.BlockSpec((1, size, LANES), lambda s: (s, 0, 0)),
            pl.BlockSpec((edge_rows, LANES), fixed),
            pl.BlockSpec((peers, 256 + share), fixed),
            pl.BlockSpec((16, LANES), fixed),
        ],
        out_shape=[
            jax.ShapeDtypeStruct((scenes, size, LANES), f32),
            jax.ShapeDtypeStruct((edge_rows, LANES), f32),
            jax.ShapeDtypeStruct((peers, 256 + share), f32),
            jax.ShapeDtypeStruct((16, LANES), f32),
        ],
        scratch_shapes=[
            pltpu.VMEM((full, PACK * channels), bf16),
            pltpu.VMEM((rows, rows), f32),
            pltpu.VMEM((size, LANES), f32),
            pltpu.VMEM(kernel.shape, f32),
        ],
        name="lift",
    )(mine, points, counts, pixels, weight, norm, kernel)


def gather_kernel(got, kern, devices, parts):
    channels = kern.shape[1]
    share = kern.shape[0] // devices // parts
    peers = got.shape[0]
    for j in range(share):
        lanes = slice(256 + j * channels, 256 + (j + 1) * channels)
        if parts > 1:
            kern[pl.ds(j, peers, stride=share), :] = got[:, lanes]
        else:
            for r in range(devices):
                at = r * (peers // devices)
                kern[r * share + j : r * share + j + 1, :] = got[at : at + 1, lanes]


def tap(kern, a, b):
    channels = kern.shape[1]
    if a is None or b is None:
        return jnp.zeros((channels, channels), f32)
    return kern[(3 * a + b) * channels : (3 * a + b + 1) * channels, :]


def edge_rows_of(block, s, scenes, lower):
    spot = pl.ds(pl.multiple_of((s % (scenes // 2)) * EDGE, 8), EDGE)
    rows = jnp.where(lower == (s < scenes // 2), block[spot, :], 0.0)
    return rows + swap_halves(rows)


def conv_body(
    devices, parts, pix, far_pix, got, z, edge, norm, conv, pooled, sums, kernel, params, source, kern, taps, grid_a, grid_b, side, acc
):
    i = pl.program_id(0)
    scenes = pl.num_programs(0) - 1
    s = jnp.minimum(i, scenes - 1)
    channels = norm.shape[1]
    size = z.shape[1]
    pairs = conv.shape[1]
    out_cols = conv.shape[2]
    cols = 2 * out_cols
    last_row = (4 * pairs - 1) * cols
    strip = out_cols + 8

    @pl.when(i == 0)
    def _():
        tot = jnp.sum(got[:, :256], axis=0, keepdims=True)
        count = tot[:, 2 * channels + 9 : 2 * channels + 10]
        mean = tot[:, :channels] / count
        inv = lax.rsqrt(tot[:, channels : 2 * channels] / count - mean * mean + norm_eps)
        nw = norm[...].astype(f32)
        gain = nw[0:1]
        sign = jnp.where(gain > 0, 1.0, jnp.where(gain < 0, -1.0, 0.0))
        params[0:1] = twice(mean)
        params[1:2] = twice(inv)
        params[2:3] = twice(gain)
        params[3:4] = twice(nw[1:2])
        params[4:5] = twice(sign)
        gather_kernel(got, kern, devices, parts)
        kernel[...] = kern[...].astype(bf16)
        for w, (low, high) in enumerate(((0, None), (1, None), (2, 0), (None, 1), (None, 2))):
            none = tap(kern, None, None)
            top = jnp.concatenate([tap(kern, low, 1), tap(kern, high, 1), none, none], axis=1)
            end = jnp.concatenate(
                [tap(kern, low, 2), tap(kern, high, 2), tap(kern, low, 0), tap(kern, high, 0)], axis=1
            )
            taps[w] = jnp.concatenate([top, end], axis=0).astype(bf16)
        source[...] = jnp.zeros_like(source)
        grid_a[...] = jnp.zeros_like(grid_a)
        grid_b[...] = jnp.zeros_like(grid_b)
        side[...] = jnp.zeros_like(side)
        acc[...] = jnp.zeros_like(acc)

    def pool(x, ok):
        pre = params[2:3] * ((x * params[4:5] - params[0:1]) * params[1:2]) + params[3:4]
        return jnp.where(ok, jnp.maximum(pre, 0.0), 0.0).astype(bf16)

    def work(dst, src):
        zs = z[0]
        own = pool(zs, zs > -0.5 * BIG)
        pooled[0, :size] = own
        source[:size] = own.astype(f32)
        far = edge_rows_of(edge, s, scenes, iota((EDGE, LANES), 1) < channels)
        flag = edge[edge.shape[0] - scenes : edge.shape[0] - scenes + 1, :]
        far = pool(far, (far > -0.5 * BIG) & (flag > 0.5))
        pooled[0, size:] = jnp.concatenate([far, jnp.zeros((LANES - EDGE, LANES), bf16)], axis=0)
        source[size : size + EDGE] = far.astype(f32)

        for p in range(size):
            dst[pl.ds(pix[s, p] + (8 + cols), 1), :] = source[p : p + 1, :]
        for p in range(EDGE):
            at = jnp.maximum(far_pix[s, p], last_row)
            dst[pl.ds(at + (8 - last_row), 1), :] = source[size + p : size + p + 1, :]

        left = iota((out_cols, LANES), 1) < channels

        def window(h):
            base = 8 + (h + 1) * cols
            even = src[pl.ds(base, out_cols, stride=2), :]
            odd = src[pl.ds(base + 1, out_cols, stride=2), :]
            return jnp.where(left, even, odd).astype(bf16)

        held = window(-1)
        for j in range(pairs):
            out = dot_nn(held, taps[0])
            for w in range(1, 5):
                held = window(4 * j - 1 + w)
                out = out + dot_nn(held, taps[w])
            side[j * strip + 8 : (j + 1) * strip, :] = out[:, LANES:]
            value = out[:, :LANES] + side[j * strip + 7 : j * strip + 7 + out_cols, :]
            conv[0, j] = value
            acc[0:8] += jnp.sum(value.reshape(out_cols // 8, 8, LANES), axis=0)
            acc[8:16] += jnp.sum((value * value).reshape(out_cols // 8, 8, LANES), axis=0)
        src[...] = jnp.zeros_like(src)

    @pl.when(i % 2 == 0)
    def _():
        work(grid_a, grid_b)

    @pl.when(i % 2 == 1)
    def _():
        work(grid_b, grid_a)

    @pl.when(i == scenes)
    def _():
        sums[...] = jnp.broadcast_to(both_sums(acc, channels), sums.shape)


def both_sums(acc, channels):
    one = jnp.sum(acc[0:8], axis=0, keepdims=True)
    two = jnp.sum(acc[8:16], axis=0, keepdims=True)
    one = one + swap_halves(one)
    two = two + swap_halves(two)
    return jnp.where(iota((1, LANES), 1) < channels, one, two)


def convolve(devices, parts, pix, far_pix, got, z, edge, norm, pairs, out_cols):
    scenes, size, _ = z.shape
    peers = got.shape[0]
    channels = norm.shape[1]
    cells = 8 + (4 * pairs + 1) * 2 * out_cols + 8
    fixed = lambda i: (0, 0)
    now = lambda i: (jnp.minimum(i, scenes - 1), 0, 0)
    return pl.pallas_call(
        functools.partial(conv_body, devices, parts),
        grid=(scenes + 1,),
        in_specs=[
            pl.BlockSpec(pix.shape, fixed, memory_space=pltpu.SMEM),
            pl.BlockSpec(far_pix.shape, fixed, memory_space=pltpu.SMEM),
            pl.BlockSpec(got.shape, fixed),
            pl.BlockSpec((1, size, LANES), now),
            pl.BlockSpec(edge.shape, fixed),
            pl.BlockSpec(norm.shape, fixed),
        ],
        out_specs=[
            pl.BlockSpec((1, pairs, out_cols, LANES), lambda i: (jnp.maximum(i - 1, 0), 0, 0, 0)),
            pl.BlockSpec((1, size + LANES, LANES), now),
            pl.BlockSpec((peers, LANES), fixed),
            pl.BlockSpec((9 * channels, channels), fixed),
        ],
        out_shape=[
            jax.ShapeDtypeStruct((scenes, pairs, out_cols, LANES), f32),
            jax.ShapeDtypeStruct((scenes, size + LANES, LANES), bf16),
            jax.ShapeDtypeStruct((peers, LANES), f32),
            jax.ShapeDtypeStruct((9 * channels, channels), bf16),
        ],
        scratch_shapes=[
            pltpu.VMEM((8, LANES), f32),
            pltpu.VMEM((size + LANES, LANES), f32),
            pltpu.VMEM((9 * channels, channels), f32),
            pltpu.VMEM((5, LANES, 2 * LANES), bf16),
            pltpu.VMEM((cells, LANES), f32),
            pltpu.VMEM((cells, LANES), f32),
            pltpu.VMEM((pairs * (out_cols + 8), LANES), f32),
            pltpu.VMEM((16, LANES), f32),
        ],
        name="convolve",
    )(pix, far_pix, got, z, edge, norm)


def split_sums(stats, channels):
    tot = jnp.sum(stats[...], axis=0, keepdims=True)
    lower = iota((1, LANES), 1) < channels
    turned = swap_halves(tot)
    return jnp.where(lower, tot, turned), jnp.where(lower, turned, tot)


def conv_params(cells, stats, norm):
    one, two = split_sums(stats, norm.shape[1])
    mean = one / cells
    inv = lax.rsqrt(two / cells - mean * mean + norm_eps)
    nw = norm[...].astype(f32)
    return mean, inv, twice(nw[2:3]), twice(nw[3:4])


def turned_pair(block, j, k):
    _, _, channels, cols = block.shape
    return jnp.transpose(block[2 * j : 2 * j + 2, k].reshape(2 * channels, cols)).astype(f32)


def norm_body(cells, stats, conv, cot, norm, result, sums, acc):
    i = pl.program_id(0)
    channels = norm.shape[1]
    scenes, pairs, out_cols, _ = conv.shape
    mean, inv, gain, bias = conv_params(cells, stats, norm)

    @pl.when(i == 0)
    def _():
        acc[...] = jnp.zeros_like(acc)

    for k in range(scenes):
        for j in range(pairs):
            xhat = (conv[k, j] - mean) * inv
            pre = gain * xhat + bias
            out = jnp.transpose(jnp.maximum(pre, 0.0).astype(bf16))
            result[2 * j : 2 * j + 2, k] = out.reshape(2, channels, out_cols)
            back = jnp.where(pre > 0, turned_pair(cot, j, k), 0.0)
            acc[0:8] += jnp.sum(back.reshape(out_cols // 8, 8, LANES), axis=0)
            acc[8:16] += jnp.sum((back * xhat).reshape(out_cols // 8, 8, LANES), axis=0)

    @pl.when(i == pl.num_programs(0) - 1)
    def _():
        sums[...] = jnp.broadcast_to(both_sums(acc, channels), sums.shape)


def normalize(cells, stats, conv, cot, norm):
    scenes, pairs, out_cols, _ = conv.shape
    rows, _, channels, _ = cot.shape
    peers = stats.shape[0]
    chunk = 2
    fixed = lambda i: (0, 0)
    return pl.pallas_call(
        functools.partial(norm_body, cells),
        grid=(scenes // chunk,),
        in_specs=[
            pl.BlockSpec((peers, LANES), fixed),
            pl.BlockSpec((chunk, pairs, out_cols, LANES), lambda i: (i, 0, 0, 0)),
            pl.BlockSpec((rows, chunk, channels, out_cols), lambda i: (0, i, 0, 0)),
            pl.BlockSpec(norm.shape, fixed),
        ],
        out_specs=[
            pl.BlockSpec((rows, chunk, channels, out_cols), lambda i: (0, i, 0, 0)),
            pl.BlockSpec((peers, LANES), fixed),
        ],
        out_shape=[
            jax.ShapeDtypeStruct(cot.shape, bf16),
            jax.ShapeDtypeStruct((peers, LANES), f32),
        ],
        scratch_shapes=[pltpu.VMEM((16, LANES), f32)],
        name="normalize",
    )(stats, conv, cot, norm)


def grad_body(
    cells, devices, parts, idx, stats, sums, conv, cot, norm, pooled, phase, kernel, slots, far, kgrad, taps, field_a, field_b, taken, acc, rows_k
):
    i = pl.program_id(0)
    scenes = pl.num_programs(0) - 1
    s = jnp.maximum(i - 1, 0)
    channels = norm.shape[1]
    pairs = conv.shape[1]
    out_cols = conv.shape[2]
    size = slots.shape[1]
    strip = out_cols + 8

    @pl.when(i == 0)
    def _():
        for hp in range(2):
            for up in range(2):
                line = []
                for dw in range(2):
                    for dr in range(2):
                        a = ((1, None), (2, 0))[hp][dr]
                        b = ((1, None), (2, 0))[up][dw]
                        if a is None or b is None:
                            line.append(jnp.zeros((channels, channels), f32))
                        else:
                            at = (3 * a + b) * channels
                            line.append(kernel[at : at + channels, :].astype(f32))
                ph = 2 * hp + up
                taps[ph * channels : (ph + 1) * channels, :] = jnp.concatenate(line, axis=1).astype(bf16)
        field_a[...] = jnp.zeros_like(field_a)
        field_b[...] = jnp.zeros_like(field_b)
        taken[...] = jnp.zeros_like(taken)
        acc[...] = jnp.zeros_like(acc)
        far[...] = jnp.zeros_like(far)

    mean, inv, gain, bias = conv_params(cells, stats, norm)
    bias_grad, gain_grad = split_sums(sums, channels)
    scale = gain * inv / cells

    def work(dst, src):
        left = iota((out_cols, LANES), 1) < channels
        before = jnp.zeros((out_cols, LANES), f32)
        for j in range(pairs):
            xhat = (conv[0, j] - mean) * inv
            pre = gain * xhat + bias
            back = jnp.where(pre > 0, turned_pair(cot, j, 0), 0.0)
            grad = scale * (cells * back - bias_grad - xhat * gain_grad)
            grad = grad.astype(bf16).astype(f32)
            turned = swap_halves(grad)
            dst[2 * j * strip : 2 * j * strip + out_cols, :] = jnp.where(left, before, turned)
            dst[(2 * j + 1) * strip : (2 * j + 1) * strip + out_cols, :] = grad
            before = turned
        dst[2 * pairs * strip : 2 * pairs * strip + out_cols, :] = jnp.where(left, before, 0.0)

        for p in range(size + EDGE):
            taken[2 * p : 2 * p + 2, :] = src[pl.ds(idx[s, p], 2), :]

        total = None
        start = 0
        while start < size + LANES:
            tile = min(TILE, size + LANES - start)
            zero_w = taken[pl.ds(2 * start, tile, stride=2), :]
            one_w = taken[pl.ds(2 * start + 1, tile, stride=2), :]
            part = jnp.concatenate([zero_w, one_w], axis=1).astype(bf16)
            out = dot_nt(part, taps[...])
            ph = []
            for c in range(tile // LANES):
                row = phase[0, :, start + c * LANES : start + (c + 1) * LANES]
                ph.append(jnp.transpose(jnp.broadcast_to(row, (LANES, LANES))))
            ph = jnp.concatenate(ph, axis=0)
            half = (iota((tile, LANES), 1) >= channels).astype(f32)
            is_even = ph == half
            is_odd = ph == half + 2.0
            value = jnp.where(is_even, out[:, :LANES], 0.0) + jnp.where(is_odd, out[:, LANES:], 0.0)
            value = value + swap_halves(value)
            pf = pooled[0, start : start + tile, :].astype(f32)
            value = jnp.where(pf > 0, value, 0.0)
            if start < size:
                slots[0, start : start + tile, :] = value
            else:
                spot = pl.ds(pl.multiple_of((s % (scenes // 2)) * EDGE, 8), EDGE)
                lower = iota((EDGE, LANES), 1) < channels
                far[spot, :] = jnp.where(lower == (s < scenes // 2), value[:EDGE], far[spot, :])
            split = jnp.concatenate([jnp.where(is_even, pf, 0.0), jnp.where(is_odd, pf, 0.0)], axis=1)
            prod = dot_tn(split.astype(bf16), part)
            total = prod if total is None else total + prod
            start += tile
        acc[...] += total

    @pl.when(i % 2 == 0)
    def _():
        work(field_a, field_b)

    @pl.when(i % 2 == 1)
    def _():
        work(field_b, field_a)

    @pl.when(i == scenes)
    def _():
        for a in range(3):
            for b in range(3):
                hp, dr = ((1, 1), (0, 0), (1, 0))[a]
                up, dw = ((1, 1), (0, 0), (1, 0))[b]
                row, col = hp * 2 + up, dw * 2 + dr
                at = (3 * a + b) * channels
                rows_k[at : at + channels, :] = acc[
                    row * channels : (row + 1) * channels, col * channels : (col + 1) * channels
                ]
        own = rows_k.shape[0] // devices
        share = own // parts
        for q in range(parts):
            for j in range(share):
                lanes = slice(j * channels, (j + 1) * channels)
                kgrad[q * devices : (q + 1) * devices, lanes] = rows_k[pl.ds(q * share + j, devices, stride=own), :]


def gradients(cells, devices, parts, idx, stats, sums, conv, cot, norm, pooled, phase, kernel):
    scenes, pairs, out_cols, _ = conv.shape
    rows, _, channels, _ = cot.shape
    peers = stats.shape[0]
    size = pooled.shape[1] - LANES
    fixed = lambda i: (0, 0)
    return pl.pallas_call(
        functools.partial(grad_body, cells, devices, parts),
        grid=(scenes + 1,),
        in_specs=[
            pl.BlockSpec(idx.shape, fixed, memory_space=pltpu.SMEM),
            pl.BlockSpec((peers, LANES), fixed),
            pl.BlockSpec((peers, LANES), fixed),
            pl.BlockSpec((1, pairs, out_cols, LANES), lambda i: (jnp.minimum(i, scenes - 1), 0, 0, 0)),
            pl.BlockSpec((rows, 1, channels, out_cols), lambda i: (0, jnp.minimum(i, scenes - 1), 0, 0)),
            pl.BlockSpec(norm.shape, fixed),
            pl.BlockSpec((1, size + LANES, LANES), lambda i: (jnp.maximum(i - 1, 0), 0, 0)),
            pl.BlockSpec((1, 1, size + LANES), lambda i: (jnp.maximum(i - 1, 0), 0, 0)),
            pl.BlockSpec(kernel.shape, fixed),
        ],
        out_specs=[
            pl.BlockSpec((1, size, LANES), lambda i: (jnp.maximum(i - 1, 0), 0, 0)),
            pl.BlockSpec((scenes // 2 * EDGE, LANES), fixed),
            pl.BlockSpec((parts * devices, 9 * channels * channels // devices // parts), fixed),
        ],
        out_shape=[
            jax.ShapeDtypeStruct((scenes, size, LANES), f32),
            jax.ShapeDtypeStruct((scenes // 2 * EDGE, LANES), f32),
            jax.ShapeDtypeStruct((parts * devices, 9 * channels * channels // devices // parts), f32),
        ],
        scratch_shapes=[
            pltpu.VMEM((4 * channels, 4 * channels), bf16),
            pltpu.VMEM(((2 * pairs + 1) * (out_cols + 8), LANES), f32),
            pltpu.VMEM(((2 * pairs + 1) * (out_cols + 8), LANES), f32),
            pltpu.VMEM((2 * (size + LANES), LANES), f32),
            pltpu.VMEM((4 * channels, 4 * channels), f32),
            pltpu.VMEM((9 * channels, channels), f32),
        ],
        name="gradients",
    )(idx, stats, sums, conv, cot, norm, pooled, phase, kernel)


def unlift_body(points, counts, weight, norm, z, slots, far, moments, rest, table, acc, mult):
    s = pl.program_id(0)
    scenes = pl.num_programs(0)
    feats, channels = weight.shape
    depth = points.shape[2]
    size = points.shape[3]
    rows = (feats + 1) * PACK
    tiles = size // TILE

    @pl.when(s == 0)
    def _():
        lift_table(weight, norm, table)
        acc[...] = jnp.zeros_like(acc)

    count = counts[pl.ds(s, 1), :]
    extra = edge_rows_of(far, s, scenes, iota((EDGE, LANES), 1) < channels)
    best, grad = [], []
    for t in range(tiles):
        at = slice(t * TILE, (t + 1) * TILE)
        zs = z[0, at, :]
        best.append(jnp.where(zs > -0.5 * BIG, zs, BIG))
        raw = slots[0, at, :]
        if t == 0:
            raw = jnp.concatenate([raw[:EDGE] + extra, raw[EDGE:]], axis=0)
        grad.append(raw.astype(bf16).astype(f32))

    def visit(fn):
        for half in range(depth // PACK):
            xin = lift_inputs(points.at[0], count, half)
            turned = [jnp.transpose(xin[:, t * TILE : (t + 1) * TILE]) for t in range(tiles)]
            for q in range(PACK // 4):
                rhs = table[:, q * 256 : (q + 1) * 256]
                total = None
                for t in range(tiles):
                    l = dot_nn(turned[t], rhs)
                    total = fn(t, l, xin[:rows, t * TILE : (t + 1) * TILE], total)
                yield q, total

    def fold(q, prod):
        slot = iota((rows, LANES), 0) % PACK - 4 * q
        upper = (iota((rows, LANES), 1) >= channels).astype(jnp.int32)
        return jnp.where(slot == upper, prod[:, :LANES], 0.0) + jnp.where(slot == upper + 2, prod[:, LANES:], 0.0)

    ties = [jnp.zeros((TILE, LANES), f32) for _ in range(tiles)]

    def first(t, l, xin, total):
        one = l[:, :LANES] == best[t]
        two = l[:, LANES:] == best[t]
        ties[t] = ties[t] + (jnp.where(one, 1.0, 0.0) + jnp.where(two, 1.0, 0.0))
        value = jnp.concatenate([jnp.where(one, grad[t], 0.0), jnp.where(two, grad[t], 0.0)], axis=1)
        part = dot_nn(xin, value.astype(bf16))
        return part if total is None else total + part

    for q, total in visit(first):
        acc[...] += fold(q, total)
    most = None
    for t in range(tiles):
        both = ties[t] + swap_halves(ties[t])
        mult[t * TILE : (t + 1) * TILE, :] = both
        most = both if most is None else jnp.maximum(most, both)

    @pl.when(jnp.max(most) > 1.5)
    def _():
        def second(t, l, xin, total):
            many = mult[t * TILE : (t + 1) * TILE, :]
            scaled = jnp.where(many > 1.5, grad[t] / jnp.maximum(many, 1.0) - grad[t], 0.0)
            one = jnp.where(l[:, :LANES] == best[t], scaled, 0.0)
            two = jnp.where(l[:, LANES:] == best[t], scaled, 0.0)
            part = exact_right(xin, jnp.concatenate([one, two], axis=1))
            return part if total is None else total + part

        for q, total in visit(second):
            acc[...] += fold(q, total)

    @pl.when(s == scenes - 1)
    def _():
        out = exact_right(one_hot_cols(16, rows), acc[...])
        out = out + swap_halves(out)
        pieces = [out[i : i + 1, :channels] for i in range(feats + 1)]
        pieces += [moments[i : i + 1, :16] for i in range(feats + 1)]
        width = (feats + 1) * (channels + 16)
        pieces.append(jnp.zeros((1, rest.shape[1] - width), f32))
        rest[...] = jnp.concatenate(pieces, axis=1)


def unlift(points, counts, weight, norm, z, slots, far, moments):
    scenes, feats, depth, size = points.shape
    channels = weight.shape[1]
    full = (feats + 2) * PACK
    rows = (feats + 1) * PACK
    width = -(-(feats + 1) * (channels + 16) // LANES) * LANES
    fixed = lambda s: (0, 0)
    return pl.pallas_call(
        unlift_body,
        grid=(scenes,),
        in_specs=[
            pl.BlockSpec((1, feats, depth, size), lambda s: (s, 0, 0, 0)),
            pl.BlockSpec((scenes, size), fixed),
            pl.BlockSpec(weight.shape, fixed),
            pl.BlockSpec(norm.shape, fixed),
            pl.BlockSpec((1, size, LANES), lambda s: (s, 0, 0)),
            pl.BlockSpec((1, size, LANES), lambda s: (s, 0, 0)),
            pl.BlockSpec(far.shape, fixed),
            pl.BlockSpec(moments.shape, fixed),
        ],
        out_specs=pl.BlockSpec((1, width), fixed),
        out_shape=jax.ShapeDtypeStruct((1, width), f32),
        scratch_shapes=[
            pltpu.VMEM((full, PACK * channels), bf16),
            pltpu.VMEM((rows, LANES), f32),
            pltpu.VMEM((size, LANES), f32),
        ],
        name="unlift",
    )(points, counts, weight, norm, z, slots, far, moments)


def adam(fixes, master, states, grad, rate, fresh, moments, average, copy):
    w = master[...]
    moment = beta_one * states[0] + (1.0 - beta_one) * grad
    second = beta_two * states[1] + (1.0 - beta_two) * grad * grad
    new = w - rate * (moment / fixes[0] / (jnp.sqrt(second / fixes[1]) + adam_eps) + decay_rate * w)
    fresh[...] = new
    moments[0] = moment
    moments[1] = second
    average[...] = average_keep * states[2] + (1.0 - average_keep) * new
    copy[...] = new.astype(bf16)


def step_body(devices, parts, fix, got, sums, weight, norm, *refs):
    pm, ps, nm, ns, km, ks = refs[:6]
    outs = refs[6:18]
    kgrad = refs[18]
    feats, channels = weight.shape
    own = km.shape[0]
    share = own // parts
    peers = got.shape[0]
    scenes = peers // devices
    fixes = (fix[0], fix[1])

    width = share * channels
    tot = None
    for r in range(devices):
        part = got[r * scenes : (r + 1) * scenes, :width]
        tot = part if tot is None else tot + part
    for j in range(share):
        piece = tot[:parts, j * channels : (j + 1) * channels]
        if parts > 1:
            kgrad[pl.ds(j, parts, stride=share), :] = piece
        else:
            kgrad[j : j + 1, :] = piece
    adam(fixes, km, ks, kgrad[...], rate_kernel, *outs[8:12])

    row = jnp.sum(got[:, width:], axis=0, keepdims=True)
    cross = jnp.concatenate([row[:, i * channels : (i + 1) * channels] for i in range(feats + 1)], axis=0)
    base = (feats + 1) * channels
    moments = jnp.concatenate([row[:, base + i * 16 : base + (i + 1) * 16] for i in range(feats + 1)], axis=0)
    w = weight[...].astype(f32)
    nw = norm[...].astype(f32)
    total = moments[feats : feats + 1, feats : feats + 1]
    firsts = moments[:feats, feats : feats + 1]
    mixed = None
    first_sum = None
    for i in range(feats):
        part = moments[:feats, i : i + 1] * w[i : i + 1]
        mixed = part if mixed is None else mixed + part
        part = moments[feats : feats + 1, i : i + 1] * w[i : i + 1]
        first_sum = part if first_sum is None else first_sum + part
    mean = first_sum / total
    inv = lax.rsqrt(jnp.sum(mixed * w, axis=0, keepdims=True) / total - mean * mean + norm_eps)
    bias_p = cross[feats : feats + 1]
    gain_p = inv * (jnp.sum(w * cross[:feats], axis=0, keepdims=True) - mean * bias_p)
    spread = inv * (mixed - firsts * mean)
    point_grad = (nw[0:1] * inv) * (cross[:feats] - (firsts * bias_p + spread * gain_p) / total)
    adam(fixes, pm, ps, point_grad, rate_points, *outs[0:4])
    both = jnp.sum(sums[...], axis=0, keepdims=True)
    norm_grad = jnp.concatenate([gain_p, bias_p, both[:, channels:], both[:, :channels]], axis=0)
    adam(fixes, nm, ns, norm_grad, rate_norms, *outs[4:8])


def update(devices, parts, fix, got, sums, weight, norm, pm, ps, nm, ns, km, ks):
    shapes = []
    for m in (pm, nm, km):
        shapes.append(jax.ShapeDtypeStruct(m.shape, f32))
        shapes.append(jax.ShapeDtypeStruct((2,) + m.shape, f32))
        shapes.append(jax.ShapeDtypeStruct(m.shape, f32))
        shapes.append(jax.ShapeDtypeStruct(m.shape, bf16))
    vmem = pl.BlockSpec(memory_space=pltpu.VMEM)
    return pl.pallas_call(
        functools.partial(step_body, devices, parts),
        in_specs=[pl.BlockSpec(memory_space=pltpu.SMEM)] + [vmem] * 10,
        out_specs=[vmem] * 12,
        out_shape=shapes,
        scratch_shapes=[pltpu.VMEM(km.shape, f32)],
        name="update",
    )(fix, got, sums, weight, norm, pm, ps, nm, ns, km, ks)


def shifted(x, by):
    length = lax.axis_size("rows")
    pairs = [(i, i + by) for i in range(length) if 0 <= i + by < length]
    return lax.ppermute(x, "rows", pairs)


def exchange(x):
    return lax.all_to_all(x, ("rows", "scene"), 0, 0, tiled=True)


def body(
    points,
    pillar_counts,
    pillar_pixels,
    point_weight,
    point_master,
    point_states,
    norm_weight,
    norm_master,
    norm_states,
    kernel_weight,
    kernel_master,
    kernel_states,
    step_count,
    cotangent,
):
    size = points.shape[3]
    out_rows, scenes, channels, out_cols = cotangent.shape
    cols = 2 * out_cols
    devices = lax.axis_size("rows")
    scene_devices = lax.axis_size("scene")
    peers = devices * scene_devices
    cells = float(out_rows * scenes * out_cols * peers)
    own = kernel_weight.shape[0]
    parts = scene_devices if own % scene_devices == 0 else 1
    share = own // parts * channels
    mine = lax.axis_index("scene") if parts > 1 else jnp.int32(0)

    z, edge, stats, moments = lift(
        mine.reshape(1, 1), points, pillar_counts, pillar_pixels, point_weight, norm_weight, kernel_weight, peers, share
    )
    edge = shifted(edge, 1)
    got = exchange(stats)
    held = scenes // 2 * EDGE
    far_pixels = edge[held : held + scenes].astype(jnp.int32)
    conv, pooled, sums, kernel = convolve(
        devices, parts, pillar_pixels, far_pixels, got, z, edge, norm_weight, out_rows // 2, out_cols
    )
    conv_stats = exchange(sums)

    far_pixels = far_pixels[:, :EDGE]
    at = (pillar_pixels % cols) // 2
    own_at = (pillar_pixels // (2 * cols) + 1) * (out_cols + 8) + at
    take_at = jnp.concatenate([own_at, (far_pixels % cols) // 2], axis=1)
    own_phase = (pillar_pixels // cols % 2) * 2 + pillar_pixels % 2
    phase = jnp.concatenate([own_phase, 2 + far_pixels % 2], axis=1)
    phase = jnp.pad(phase, ((0, 0), (0, LANES - EDGE))).astype(f32)[:, None]

    result, sums = normalize(cells, conv_stats, conv, cotangent, norm_weight)
    grad_sums = exchange(sums)
    slots, far, kgrad = gradients(
        cells, devices, parts, take_at, conv_stats, grad_sums, conv, cotangent, norm_weight, pooled, phase, kernel
    )
    far = shifted(far, -1)
    if parts > 1:
        kgrad = lax.all_to_all(kgrad, "scene", 0, 0, tiled=True)
    else:
        kgrad = lax.psum(kgrad, "scene")
    rest = unlift(points, pillar_counts, point_weight, norm_weight, z, slots, far, moments)
    if parts > 1:
        kgrad = jnp.sum(kgrad.reshape(scene_devices, devices, share), axis=0)
    kgrad = jnp.broadcast_to(kgrad[:, None], (devices, scene_devices, share)).reshape(peers, share)
    got = exchange(jnp.concatenate([kgrad, jnp.broadcast_to(rest, (peers, rest.shape[1]))], axis=1))
    steps_done = step_count[0].astype(f32)
    fix = jnp.stack([1.0 - beta_one**steps_done, 1.0 - beta_two**steps_done])
    outs = update(
        devices,
        parts,
        fix,
        got,
        grad_sums,
        point_weight,
        norm_weight,
        point_master,
        point_states,
        norm_master,
        norm_states,
        kernel_master,
        kernel_states,
    )
    return (result, *outs)


def solution(mesh):
    placed = (
        P("scene", None, None, "rows"),
        P("scene", "rows"),
        P("scene", "rows"),
        P(),
        P(),
        P(),
        P(),
        P(),
        P(),
        P("rows", None),
        P("rows", None),
        P(None, "rows", None),
        P(),
        P("rows", "scene", None, None),
    )
    return jax.shard_map(
        body,
        mesh=mesh,
        in_specs=placed,
        out_specs=(
            P("rows", "scene", None, None),
            P(),
            P(),
            P(),
            P(),
            P(),
            P(),
            P(),
            P(),
            P("rows", None),
            P(None, "rows", None),
            P("rows", None),
            P("rows", None),
        ),
        check_vma=False,
    )
```

```python
import functools

import jax
import jax.numpy as jnp
from jax import lax
from jax.experimental import pallas as pl
from jax.experimental.pallas import tpu as pltpu
from jax.sharding import PartitionSpec as P

beta_one = 0.9
beta_two = 0.999
adam_eps = 1e-08
decay_rate = 0.01
average_keep = 0.99
norm_eps = 1e-05
rate_points = 0.3
rate_norms = 0.2
rate_kernel = 0.04

EDGE = 48
BIG = 1e30
PACK = 8
TILE = 256
SCOPE = 40 << 20
LANES = 128
f32 = jnp.float32
bf16 = jnp.bfloat16


def iota(shape, dim):
    return lax.broadcasted_iota(jnp.int32, shape, dim)


def dot_nn(a, b):
    return lax.dot_general(a, b, (((1,), (0,)), ((), ())), preferred_element_type=f32)


def dot_nt(a, b):
    return lax.dot_general(a, b, (((1,), (1,)), ((), ())), preferred_element_type=f32)


def dot_tn(a, b):
    return lax.dot_general(a, b, (((0,), (0,)), ((), ())), preferred_element_type=f32)


def split3(x):
    a = x.astype(bf16)
    r = x - a.astype(f32)
    b = r.astype(bf16)
    c = (r - b.astype(f32)).astype(bf16)
    return a, b, c


def exact_left(x, y):
    a, b, c = split3(x)
    return dot_nn(a, y) + (dot_nn(b, y) + dot_nn(c, y))


def exact_right(x, y):
    a, b, c = split3(y)
    return dot_nn(x, a) + (dot_nn(x, b) + dot_nn(x, c))


def swap_halves(x):
    return pltpu.roll(x, x.shape[1] // 2, axis=1)


def twice(row):
    return jnp.concatenate([row, row], axis=1)


def one_hot_rows(rows, cols):
    return (iota((rows, cols), 0) // PACK == iota((rows, cols), 1)).astype(f32).astype(bf16)


def one_hot_cols(rows, cols):
    return (iota((rows, cols), 1) // PACK == iota((rows, cols), 0)).astype(f32).astype(bf16)


def lift_table(weight, norm, table):
    feats, channels = weight.shape
    rows = table.shape[0]
    gain = norm[0:1, :].astype(f32)
    sign = jnp.where(gain > 0, 1.0, jnp.where(gain < 0, -1.0, 0.0))
    signed = weight[...].astype(f32) * sign
    full = jnp.concatenate([signed, jnp.zeros((1, channels), f32), jnp.ones((1, channels), f32)], axis=0)
    full = jnp.concatenate([full, jnp.zeros((16 - feats - 2, channels), f32)], axis=0)
    base = dot_nn(one_hot_rows(rows, 16), twice(full).astype(bf16))
    slot = iota(base.shape, 0) % PACK
    half = iota(base.shape, 1) // channels
    for m in range(PACK // 2):
        table[:, m * LANES : (m + 1) * LANES] = jnp.where(slot == 2 * m + half, base, 0.0).astype(bf16)


def lift_inputs(pts, count, part):
    feats, _, size = pts.shape
    live = (iota((PACK, size), 0) + part * PACK < count).astype(f32)
    kept = (pts.astype(f32) * live[None]).reshape(feats * PACK, size)
    return jnp.concatenate([kept, live, (live - 1.0) * BIG], axis=0).astype(bf16)


def copy_in(source, target, sems, s):
    return pltpu.make_async_copy(source.at[s], target.at[s], sems.at[s])


def half_store(block, s, scenes, value):
    channels = LANES // 2
    spot = pl.ds(pl.multiple_of((s % (scenes // 2)) * EDGE, 8), EDGE)
    lower = iota((EDGE, LANES), 1) < channels
    block[spot, :] = jnp.where(lower == (s < scenes // 2), value, block[spot, :])


def lift_body(
    mine, points, counts, pixels, weight, norm, kernel, z_out, winner_out, edge, payload, moments,
    table, gram, wide, pts, z, low, high, winner, sems,
):
    feats, channels = weight.shape
    scenes, _, depth, size = points.shape
    rows = (feats + 1) * PACK
    for s in range(scenes):
        copy_in(points, pts, sems.at[0], s).start()
    lift_table(weight, norm, table)
    gram[...] = jnp.zeros_like(gram)
    edge[...] = jnp.zeros_like(edge)
    second_half = (iota((1, LANES), 1) >= channels).astype(f32)

    def scene(s, _):
        copy_in(points, pts, sems.at[0], s).wait()
        count = counts[pl.ds(s, 1), :]
        total = None
        for part in range(depth // PACK):
            xin = lift_inputs(pts[s, :, part * PACK : (part + 1) * PACK, :], count, part)
            prod = dot_nt(xin[:rows], xin[:rows])
            total = prod if total is None else total + prod
            for t in range(size // TILE):
                at = slice(t * TILE, (t + 1) * TILE)
                turned = jnp.transpose(xin[:, at])
                for q in range(PACK // 4):
                    l = dot_nn(turned, table[:, q * 256 : (q + 1) * 256])
                    one, two = l[:, :LANES], l[:, LANES:]
                    n_one = second_half + float(part * PACK + q * 4)
                    n_two = n_one + 2.0
                    m = jnp.maximum(one, two)
                    first = jnp.where(two > one, n_two, n_one)
                    last = jnp.where(two >= one, n_two, n_one)
                    if part > 0 or q > 0:
                        old = z[s, at, :]
                        first = jnp.where(m > old, first, low[at, :])
                        last = jnp.where(m >= old, last, high[at, :])
                        m = jnp.maximum(old, m)
                    if part == depth // PACK - 1 and q == PACK // 4 - 1:
                        other = swap_halves(m)
                        first = jnp.where(other > m, swap_halves(first), first)
                        last = jnp.where(other >= m, swap_halves(last), last)
                        m = jnp.maximum(m, other)
                        only = jnp.where(first == last, first, -1.0)
                        winner[s, at, :] = jnp.where(m > -0.5 * BIG, only, 99.0)
                    else:
                        low[at, :] = first
                        high[at, :] = last
                    z[s, at, :] = m
        gram[...] += total
        copy_in(z, z_out, sems.at[1], s).start()
        copy_in(winner, winner_out, sems.at[2], s).start()
        half_store(edge, s, scenes, z[s, :EDGE, :])
        return 0

    lax.fori_loop(0, scenes, scene, 0)

    count_rows = edge.shape[0] - 2 * scenes
    edge[count_rows : count_rows + scenes, :] = pixels[:, :LANES].astype(f32)
    edge[count_rows + scenes :, :] = jnp.ones((scenes, LANES), f32)
    g = gram[...]
    g = jnp.where(iota(g.shape, 0) % PACK == iota(g.shape, 1) % PACK, g, 0.0)
    y = exact_left(g, one_hot_rows(rows, LANES))
    m = exact_right(one_hot_cols(16, rows), y)
    moments[...] = m
    w = jnp.concatenate([weight[...].astype(f32), jnp.zeros((16 - feats, channels), f32)], axis=0)
    aw = exact_left(m[:, :16], w.astype(bf16))
    two = jnp.sum(aw * w, axis=0, keepdims=True)
    one = aw[feats : feats + 1]
    own = kernel.shape[1]
    flat = jnp.concatenate([kernel[...].astype(f32), jnp.zeros((channels, LANES - own), f32)], axis=1)
    wide[...] = jnp.transpose(jnp.concatenate([flat, jnp.zeros((LANES - channels, LANES), f32)], axis=0))
    pieces = [one, two, m[feats : feats + 1]]
    share = (payload.shape[2] - 256) // channels
    for j in range(share):
        pieces.append(wide[pl.ds(mine[0, 0] * share + j, 1), :channels])
    row = jnp.concatenate(pieces, axis=1)
    payload[...] = jnp.broadcast_to(row[:, None, :], payload.shape)
    for s in range(scenes):
        copy_in(z, z_out, sems.at[1], s).wait()
        copy_in(winner, winner_out, sems.at[2], s).wait()


def vmem(count):
    return [pl.BlockSpec(memory_space=pltpu.VMEM)] * count


def smem(count):
    return [pl.BlockSpec(memory_space=pltpu.SMEM)] * count


def hbm(count):
    return [pl.BlockSpec(memory_space=pltpu.HBM)] * count


def near(x):
    return pltpu.with_memory_space_constraint(x, pltpu.VMEM)


scoped = pltpu.CompilerParams(vmem_limit_bytes=SCOPE)


def lift(mine, points, counts, pixels, weight, norm, kernel, peers, share):
    scenes, feats, depth, size = points.shape
    channels = weight.shape[1]
    full = (feats + 2) * PACK
    rows = (feats + 1) * PACK
    edge_rows = scenes // 2 * EDGE + 2 * scenes
    return pl.pallas_call(
        lift_body,
        in_specs=smem(1) + hbm(1) + vmem(5),
        out_specs=hbm(2) + vmem(3),
        out_shape=[
            jax.ShapeDtypeStruct((scenes, size, LANES), f32),
            jax.ShapeDtypeStruct((scenes, size, LANES), f32),
            jax.ShapeDtypeStruct((edge_rows, LANES), f32),
            jax.ShapeDtypeStruct((peers, 1, 256 + share), f32),
            jax.ShapeDtypeStruct((16, LANES), f32),
        ],
        scratch_shapes=[
            pltpu.VMEM((full, PACK * channels), bf16),
            pltpu.VMEM((rows, rows), f32),
            pltpu.VMEM((LANES, LANES), f32),
            pltpu.VMEM(points.shape, bf16),
            pltpu.VMEM((scenes, size, LANES), f32),
            pltpu.VMEM((size, LANES), f32),
            pltpu.VMEM((size, LANES), f32),
            pltpu.VMEM((scenes, size, LANES), f32),
            pltpu.SemaphoreType.DMA((3, scenes)),
        ],
        compiler_params=scoped,
        name="lift",
    )(mine, points, counts, pixels, weight, norm, kernel)


def gather_kernel(got, kern, devices, parts):
    channels = kern.shape[1]
    share = kern.shape[0] // devices // parts
    peers = got.shape[0]
    for j in range(share):
        rows = got[:, 0, 256 + j * channels : 256 + (j + 1) * channels]
        if parts > 1:
            kern[pl.ds(j, peers, stride=share), :] = rows
        else:
            for r in range(devices):
                at = r * (peers // devices)
                kern[r * share + j : r * share + j + 1, :] = rows[at : at + 1]


def tap(kern, a, b):
    channels = kern.shape[1]
    if a is None or b is None:
        return jnp.zeros((channels, channels), f32)
    return kern[(3 * a + b) * channels : (3 * a + b + 1) * channels, :]


def edge_rows_of(block, s, scenes, lower):
    spot = pl.ds(pl.multiple_of((s % (scenes // 2)) * EDGE, 8), EDGE)
    rows = jnp.where(lower == (s < scenes // 2), block[spot, :], 0.0)
    return rows + swap_halves(rows)


def conv_body(
    devices, parts, pix, far_pix, got, z_in, edge, norm, conv_out, pooled_out, sums, kernel,
    params, source, kern, taps, grid_a, grid_b, side, acc, z, conv, pooled, sems,
):
    scenes, size, _ = z.shape
    for s in range(scenes):
        copy_in(z_in, z, sems.at[0], s).start()
    channels = norm.shape[1]
    _, pairs, out_cols, _ = conv.shape
    cols = 2 * out_cols
    last_row = (4 * pairs - 1) * cols
    tot = jnp.sum(got[:, :, :256], axis=0)
    count = tot[:, 2 * channels + 9 : 2 * channels + 10]
    mean = tot[:, :channels] / count
    inv = lax.rsqrt(tot[:, channels : 2 * channels] / count - mean * mean + norm_eps)
    nw = norm[...].astype(f32)
    gain = nw[0:1]
    sign = jnp.where(gain > 0, 1.0, jnp.where(gain < 0, -1.0, 0.0))
    params[0:1] = twice(mean)
    params[1:2] = twice(inv)
    params[2:3] = twice(gain)
    params[3:4] = twice(nw[1:2])
    params[4:5] = twice(sign)
    gather_kernel(got, kern, devices, parts)
    kernel[...] = kern[...].astype(bf16)
    for w, (low, high) in enumerate(((0, None), (1, None), (2, 0), (None, 1), (None, 2))):
        none = tap(kern, None, None)
        top = jnp.concatenate([tap(kern, low, 1), tap(kern, high, 1), none, none], axis=1)
        end = jnp.concatenate([tap(kern, low, 2), tap(kern, high, 2), tap(kern, low, 0), tap(kern, high, 0)], axis=1)
        taps[w] = jnp.concatenate([top, end], axis=0).astype(bf16)
    grid_a[...] = jnp.zeros_like(grid_a)
    grid_b[...] = jnp.zeros_like(grid_b)
    side[...] = jnp.zeros_like(side)
    acc[...] = jnp.zeros_like(acc)

    def pool(x, ok):
        pre = params[2:3] * ((x * params[4:5] - params[0:1]) * params[1:2]) + params[3:4]
        return jnp.where(ok, jnp.maximum(pre, 0.0), 0.0).astype(bf16)

    own_at = 8 + cols
    far_at = 8 - last_row

    def fill(s):
        zs = z[s]
        own = pool(zs, zs > -0.5 * BIG)
        pooled[s, :size] = own
        source[:size] = own.astype(f32)
        far = edge_rows_of(edge, s, scenes, iota((EDGE, LANES), 1) < channels)
        flag = edge[edge.shape[0] - scenes : edge.shape[0] - scenes + 1, :]
        far = pool(far, (far > -0.5 * BIG) & (flag > 0.5))
        pooled[s, size:] = jnp.concatenate([far, jnp.zeros((LANES - EDGE, LANES), bf16)], axis=0)
        source[size : size + EDGE] = far.astype(f32)

    def place_far(dst, s):
        for p in range(EDGE):
            at = jnp.maximum(far_pix[s, p], last_row) + far_at
            dst[pl.ds(at, 1), :] = source[size + p : size + p + 1, :]

    def place(dst, s, j):
        rows = dst.at[pl.ds(own_at, 4 * pairs * cols), :]
        some = size // pairs
        line = s * pairs + j
        base = pl.multiple_of(j * some, 8)
        for p in range(some):
            rows[pl.ds(pix[line, 0, p], 1), :] = source[pl.ds(base + p, 1), :]

    left = iota((out_cols, LANES), 1) < channels

    def convolve_pair(src, s, j):
        out = None
        for w in range(5):
            base = 8 + (4 * j + w) * cols
            even = src[pl.ds(base, out_cols, stride=2), :]
            odd = src[pl.ds(base + 1, out_cols, stride=2), :]
            part = dot_nn(jnp.where(left, even, odd).astype(bf16), taps[w])
            out = part if out is None else out + part
        side[8:, :] = out[:, LANES:]
        value = out[:, :LANES] + side[7 : 7 + out_cols, :]
        conv[s, j] = value
        acc[0:8] += jnp.sum(value.reshape(out_cols // 8, 8, LANES), axis=0)
        acc[8:16] += jnp.sum((value * value).reshape(out_cols // 8, 8, LANES), axis=0)
        base = pl.multiple_of(8 + 4 * j * cols, 8)
        src[pl.ds(base, 4 * cols), :] = jnp.zeros((4 * cols, LANES), f32)

    def clear_last(src):
        src[8 + 4 * pairs * cols : 8 + (4 * pairs + 1) * cols, :] = jnp.zeros((cols, LANES), f32)

    copy_in(z_in, z, sems.at[0], 0).wait()
    fill(0)
    place_far(grid_a, 0)

    def start(j, _):
        place(grid_a, 0, j)
        return 0

    lax.fori_loop(0, pairs, start, 0)

    def two_scenes(i, _):
        for k, (src, dst) in enumerate(((grid_a, grid_b), (grid_b, grid_a))):
            s = 2 * i + k
            ahead = jnp.minimum(s + 1, scenes - 1)

            @pl.when(s + 1 < scenes)
            def _():
                copy_in(z_in, z, sems.at[0], s + 1).wait()

            fill(ahead)
            place_far(dst, ahead)

            def step(j, _):
                place(dst, ahead, j)
                convolve_pair(src, s, j)
                return 0

            lax.fori_loop(0, pairs, step, 0)
            clear_last(src)
            copy_in(conv, conv_out, sems.at[1], s).start()
            copy_in(pooled, pooled_out, sems.at[2], s).start()
        return 0

    lax.fori_loop(0, scenes // 2, two_scenes, 0)
    for s in range(scenes):
        copy_in(conv, conv_out, sems.at[1], s).wait()
        copy_in(pooled, pooled_out, sems.at[2], s).wait()
    sums[...] = jnp.broadcast_to(both_sums(acc, channels), sums.shape)


def both_sums(acc, channels):
    one = jnp.sum(acc[0:8], axis=0, keepdims=True)
    two = jnp.sum(acc[8:16], axis=0, keepdims=True)
    one = one + swap_halves(one)
    two = two + swap_halves(two)
    return jnp.where(iota((1, LANES), 1) < channels, one, two)


def convolve(devices, parts, pix, far_pix, got, z, edge, norm, pairs, out_cols):
    scenes, size, _ = z.shape
    peers = got.shape[0]
    channels = norm.shape[1]
    cells = 8 + (4 * pairs + 1) * 2 * out_cols + 8
    return pl.pallas_call(
        functools.partial(conv_body, devices, parts),
        in_specs=smem(2) + vmem(1) + hbm(1) + vmem(2),
        out_specs=hbm(2) + vmem(2),
        out_shape=[
            jax.ShapeDtypeStruct((scenes, pairs, out_cols, LANES), f32),
            jax.ShapeDtypeStruct((scenes, size + LANES, LANES), bf16),
            jax.ShapeDtypeStruct((peers, LANES), f32),
            jax.ShapeDtypeStruct((9 * channels, channels), bf16),
        ],
        scratch_shapes=[
            pltpu.VMEM((8, LANES), f32),
            pltpu.VMEM((size + LANES, LANES), f32),
            pltpu.VMEM((9 * channels, channels), f32),
            pltpu.VMEM((5, LANES, 2 * LANES), bf16),
            pltpu.VMEM((cells, LANES), f32),
            pltpu.VMEM((cells, LANES), f32),
            pltpu.VMEM((out_cols + 8, LANES), f32),
            pltpu.VMEM((16, LANES), f32),
            pltpu.VMEM((scenes, size, LANES), f32),
            pltpu.VMEM((scenes, pairs, out_cols, LANES), f32),
            pltpu.VMEM((scenes, size + LANES, LANES), bf16),
            pltpu.SemaphoreType.DMA((3, scenes)),
        ],
        compiler_params=scoped,
        name="convolve",
    )(pix, far_pix, got, z, edge, norm)


def split_sums(stats, channels):
    tot = jnp.sum(stats[...], axis=0)
    lower = iota((1, LANES), 1) < channels
    turned = swap_halves(tot)
    return jnp.where(lower, tot, turned), jnp.where(lower, turned, tot)


def conv_params(cells, stats, norm):
    one, two = split_sums(stats, norm.shape[1])
    mean = one / cells
    inv = lax.rsqrt(two / cells - mean * mean + norm_eps)
    nw = norm[...].astype(f32)
    return mean, inv, twice(nw[2:3]), twice(nw[3:4])


def turned_pair(block, j, k):
    _, _, channels, cols = block.shape
    return jnp.transpose(block[2 * j : 2 * j + 2, k].reshape(2 * channels, cols)).astype(f32)


def scene_copy(source, target, sems, s):
    return pltpu.make_async_copy(source.at[:, s], target.at[:, s], sems.at[s])


def norm_body(cells, stats, conv_in, cot_in, norm, result_out, sums, acc, conv, cot, result, sems):
    channels = norm.shape[1]
    scenes, pairs, out_cols, _ = conv.shape
    for s in range(scenes):
        copy_in(conv_in, conv, sems.at[0], s).start()
        scene_copy(cot_in, cot, sems.at[1], s).start()
    mean, inv, gain, bias = conv_params(cells, stats, norm)
    acc[...] = jnp.zeros_like(acc)

    def scene(k, _):
        copy_in(conv_in, conv, sems.at[0], k).wait()
        scene_copy(cot_in, cot, sems.at[1], k).wait()
        for j in range(pairs):
            xhat = (conv[k, j] - mean) * inv
            pre = gain * xhat + bias
            out = jnp.transpose(jnp.maximum(pre, 0.0).astype(bf16))
            result[2 * j : 2 * j + 2, k] = out.reshape(2, channels, out_cols)
            back = jnp.where(pre > 0, turned_pair(cot, j, k), 0.0)
            acc[0:8] += jnp.sum(back.reshape(out_cols // 8, 8, LANES), axis=0)
            acc[8:16] += jnp.sum((back * xhat).reshape(out_cols // 8, 8, LANES), axis=0)
        scene_copy(result, result_out, sems.at[2], k).start()
        return 0

    lax.fori_loop(0, scenes, scene, 0)
    sums[...] = jnp.broadcast_to(both_sums(acc, channels), sums.shape)
    for s in range(scenes):
        scene_copy(result, result_out, sems.at[2], s).wait()


def normalize(cells, stats, conv, cot, norm):
    peers = stats.shape[0]
    scenes = conv.shape[0]
    return pl.pallas_call(
        functools.partial(norm_body, cells),
        in_specs=vmem(1) + hbm(2) + vmem(1),
        out_specs=hbm(1) + vmem(1),
        out_shape=[
            jax.ShapeDtypeStruct(cot.shape, bf16),
            jax.ShapeDtypeStruct((peers, LANES), f32),
        ],
        scratch_shapes=[
            pltpu.VMEM((16, LANES), f32),
            pltpu.VMEM(conv.shape, f32),
            pltpu.VMEM(cot.shape, bf16),
            pltpu.VMEM(cot.shape, bf16),
            pltpu.SemaphoreType.DMA((3, scenes)),
        ],
        compiler_params=scoped,
        name="normalize",
    )(stats, conv, cot, norm)


def grad_body(
    cells, devices, parts, idx, stats, sums, conv_in, cot_in, norm, pooled_in, phase, kernel, slots_out, edge, far, kgrad,
    taps, field_a, field_b, taken_a, taken_b, turn, column, acc, rows_k, conv, cot, pooled, slots, exact, sems,
):
    scenes, pairs, out_cols, _ = conv.shape
    channels = norm.shape[1]
    size = slots.shape[1]
    strip = out_cols + 8
    some = idx.shape[2]
    for s in range(scenes):
        copy_in(conv_in, conv, sems.at[0], s).start()
        scene_copy(cot_in, cot, sems.at[1], s).start()
    for s in range(scenes):
        copy_in(pooled_in, pooled, sems.at[2], s).start()
    for hp in range(2):
        for up in range(2):
            line = []
            for dw in range(2):
                for dr in range(2):
                    a = ((1, None), (2, 0))[hp][dr]
                    b = ((1, None), (2, 0))[up][dw]
                    if a is None or b is None:
                        line.append(jnp.zeros((channels, channels), f32))
                    else:
                        at = (3 * a + b) * channels
                        line.append(kernel[at : at + channels, :].astype(f32))
            ph = 2 * hp + up
            taps[ph * channels : (ph + 1) * channels, :] = jnp.concatenate(line, axis=1).astype(bf16)
    for block in (field_a, field_b, taken_a, taken_b, acc):
        block[...] = jnp.zeros_like(block)

    def phases(s, _):
        for c in range(column.shape[1] // LANES):
            row = phase[s, :, c * LANES : (c + 1) * LANES]
            column[s, c * LANES : (c + 1) * LANES, :] = jnp.transpose(jnp.broadcast_to(row, (LANES, LANES)))
        return 0

    lax.fori_loop(0, scenes, phases, 0)
    mean, inv, gain, bias = conv_params(cells, stats, norm)
    bias_grad, gain_grad = split_sums(sums, channels)
    scale = gain * inv / cells
    left = iota((out_cols, LANES), 1) < channels
    half = (iota((some, LANES), 1) >= channels).astype(f32)

    def field(dst, s, j):
        xhat = (conv[s, j] - mean) * inv
        pre = gain * xhat + bias
        both = cot[pl.ds(2 * j, 2), s].reshape(2 * channels, out_cols)
        back = jnp.where(pre > 0, jnp.transpose(both).astype(f32), 0.0)
        grad = scale * (cells * back - bias_grad - xhat * gain_grad)
        grad = grad.astype(bf16).astype(f32)
        turned = swap_halves(grad)
        base = pl.multiple_of(2 * j * strip, 8)
        dst[pl.ds(base, out_cols), :] = jnp.where(left, turn[...], turned)
        dst[pl.ds(pl.multiple_of(base + strip, 8), out_cols), :] = grad
        turn[...] = turned

    def take(dst, src, s, j):
        line = s * pairs + j
        for p in range(some):
            dst[2 * p : 2 * p + 2, :] = src[pl.ds(idx[line, 0, p], 2), :]

    def product(src, s, j):
        at = pl.ds(pl.multiple_of(j * some, 16), some)
        part = jnp.concatenate([src[pl.ds(0, some, stride=2), :], src[pl.ds(1, some, stride=2), :]], axis=1).astype(bf16)
        out = dot_nt(part, taps[...])
        ph = column[s, at, :]
        is_even = ph == half
        is_odd = ph == half + 2.0
        value = jnp.where(is_even, out[:, :LANES], 0.0) + jnp.where(is_odd, out[:, LANES:], 0.0)
        value = value + swap_halves(value)
        pf = pooled[s, at, :].astype(f32)
        value = jnp.where(pf > 0, value, 0.0)
        exact[s, at, :] = value
        slots[s, at, :] = value.astype(bf16)
        split = jnp.concatenate([jnp.where(is_even, pf, 0.0), jnp.where(is_odd, pf, 0.0)], axis=1)
        acc[...] += dot_tn(split.astype(bf16), part)

    def walk(dst, src, s):
        before = jnp.clip(s - 1, 0, scenes - 1)
        older = jnp.clip(s - 2, 0, scenes - 1)

        def step(i, _):
            for k, (to, of) in enumerate(((taken_a, taken_b), (taken_b, taken_a))):
                j = 2 * i + k
                if dst is not None:
                    field(dst, s, j)
                take(to, src, before, j)
                last = jnp.where(j > 0, before, older)
                product(of, last, jnp.where(j > 0, j - 1, pairs - 1))
            return 0

        if dst is not None:
            copy_in(conv_in, conv, sems.at[0], s).wait()
            scene_copy(cot_in, cot, sems.at[1], s).wait()
            copy_in(pooled_in, pooled, sems.at[2], s).wait()
            turn[...] = jnp.zeros_like(turn)
        lax.fori_loop(0, pairs // 2, step, 0)
        if dst is not None:
            dst[2 * pairs * strip : 2 * pairs * strip + out_cols, :] = jnp.where(left, turn[...], 0.0)

    def two_scenes(i, _):
        walk(field_a, field_b, 2 * i)
        walk(field_b, field_a, 2 * i + 1)
        return 0

    lax.fori_loop(0, scenes // 2, two_scenes, 0)
    walk(None, field_b, scenes)
    product(taken_b, scenes - 1, pairs - 1)
    for s in range(scenes):
        copy_in(slots, slots_out, sems.at[0], s).start()
    far[...] = jnp.zeros_like(far)
    edge[...] = jnp.zeros_like(edge)

    def pick(s, _):
        half_store(edge, s, scenes, exact[s, :EDGE, :])
        half_store(far, s, scenes, exact[s, size - LANES : size - LANES + EDGE, :])
        return 0

    lax.fori_loop(0, scenes, pick, 0)
    for a in range(3):
        for b in range(3):
            hp, dr = ((1, 1), (0, 0), (1, 0))[a]
            up, dw = ((1, 1), (0, 0), (1, 0))[b]
            row, col = hp * 2 + up, dw * 2 + dr
            at = (3 * a + b) * channels
            rows_k[at : at + channels, :] = acc[
                row * channels : (row + 1) * channels, col * channels : (col + 1) * channels
            ]
    own = rows_k.shape[0] // devices
    share = own // parts
    for q in range(parts):
        for j in range(share):
            lanes = slice(j * channels, (j + 1) * channels)
            kgrad[q * devices : (q + 1) * devices, lanes] = rows_k[pl.ds(q * share + j, devices, stride=own), :]
    for s in range(scenes):
        copy_in(slots, slots_out, sems.at[0], s).wait()


def gradients(cells, devices, parts, idx, stats, sums, conv, cot, norm, pooled, phase, kernel):
    scenes, pairs, out_cols, _ = conv.shape
    channels = norm.shape[1]
    rows = pooled.shape[1]
    return pl.pallas_call(
        functools.partial(grad_body, cells, devices, parts),
        in_specs=smem(1) + vmem(2) + hbm(2) + vmem(1) + hbm(1) + vmem(2),
        out_specs=hbm(1) + vmem(3),
        out_shape=[
            jax.ShapeDtypeStruct((scenes, rows, LANES), bf16),
            jax.ShapeDtypeStruct((scenes // 2 * EDGE, LANES), f32),
            jax.ShapeDtypeStruct((scenes // 2 * EDGE, LANES), f32),
            jax.ShapeDtypeStruct((parts * devices, 9 * channels * channels // devices // parts), f32),
        ],
        scratch_shapes=[
            pltpu.VMEM((4 * channels, 4 * channels), bf16),
            pltpu.VMEM(((2 * pairs + 1) * (out_cols + 8), LANES), f32),
            pltpu.VMEM(((2 * pairs + 1) * (out_cols + 8), LANES), f32),
            pltpu.VMEM((2 * idx.shape[2], LANES), f32),
            pltpu.VMEM((2 * idx.shape[2], LANES), f32),
            pltpu.VMEM((out_cols, LANES), f32),
            pltpu.VMEM((scenes, rows, LANES), f32),
            pltpu.VMEM((4 * channels, 4 * channels), f32),
            pltpu.VMEM((9 * channels, channels), f32),
            pltpu.VMEM(conv.shape, f32),
            pltpu.VMEM(cot.shape, bf16),
            pltpu.VMEM(pooled.shape, bf16),
            pltpu.VMEM((scenes, rows, LANES), bf16),
            pltpu.VMEM((scenes, rows, LANES), f32),
            pltpu.SemaphoreType.DMA((3, scenes)),
        ],
        compiler_params=scoped,
        name="gradients",
    )(idx, stats, sums, conv, cot, norm, pooled, phase, kernel)


def unlift_body(
    points, counts, weight, norm, z, winner_in, slots_in, edge, far, moments, rest,
    table, acc, bias, pts, winner, slots, best, mult, sems,
):
    feats, channels = weight.shape
    scenes, _, depth, size = points.shape
    rows = feats * PACK
    tiles = size // TILE
    for s in range(scenes):
        copy_in(points, pts, sems.at[0], s).start()
        copy_in(winner_in, winner, sems.at[1], s).start()
        copy_in(slots_in, slots, sems.at[2], s).start()
    lift_table(weight, norm, table)
    acc[...] = jnp.zeros_like(acc)
    bias[...] = jnp.zeros_like(bias)
    second_half = (iota((1, LANES), 1) >= channels).astype(f32)
    slot = iota((rows, LANES), 0) % PACK
    upper = (iota((rows, LANES), 1) >= channels).astype(jnp.int32)

    def fold(q, prod):
        near_n = slot - 4 * q
        return jnp.where(near_n == upper, prod[:, :LANES], 0.0) + jnp.where(near_n == upper + 2, prod[:, LANES:], 0.0)

    def tile(u, _):
        s = u // tiles
        t = u % tiles
        at = pl.ds(pl.multiple_of(t * TILE, TILE), TILE)

        @pl.when(t == 0)
        def _():
            copy_in(points, pts, sems.at[0], s).wait()
            copy_in(winner_in, winner, sems.at[1], s).wait()
            copy_in(slots_in, slots, sems.at[2], s).wait()
            lower = iota((EDGE, LANES), 1) < channels
            whole = edge_rows_of(edge, s, scenes, lower) + edge_rows_of(far, s, scenes, lower)
            slots[s, :EDGE, :] = whole.astype(bf16)

        grad = slots[s, at, :].astype(f32)
        who = winner[s, at, :]
        bias[...] += jnp.sum(grad.reshape(TILE // 8, 8, LANES), axis=0)
        total = None
        for part in range(depth // PACK):
            x = pts[s, :, part * PACK : (part + 1) * PACK, at].reshape(rows, TILE)
            for q in range(PACK // 4):
                n_one = second_half + float(part * PACK + q * 4)
                value = jnp.concatenate(
                    [jnp.where(who == n_one, grad, 0.0), jnp.where(who == n_one + 2.0, grad, 0.0)], axis=1
                )
                prod = fold(q, dot_nn(x, value.astype(bf16)))
                total = prod if total is None else total + prod
        acc[...] += total

        @pl.when(jnp.min(who) < 0.0)
        def _():
            fetch = pltpu.make_async_copy(z.at[s, at], best, sems.at[0, 0])
            fetch.start()
            fetch.wait()
            best[...] = jnp.where(winner[s, at, :] < 0.0, best[...], BIG)
            mult[...] = jnp.zeros_like(mult)
            count = counts[pl.ds(s, 1), at]

            def lifted(part, q):
                xin = lift_inputs(pts[s, :, part * PACK : (part + 1) * PACK, at], count, part)
                l = dot_nn(jnp.transpose(xin), table[:, q * 256 : (q + 1) * 256])
                return xin, l[:, :LANES] == best[...], l[:, LANES:] == best[...]

            for part in range(depth // PACK):
                for q in range(PACK // 4):
                    _, one, two = lifted(part, q)
                    mult[...] += jnp.where(one, 1.0, 0.0) + jnp.where(two, 1.0, 0.0)
            many = jnp.maximum(mult[...] + swap_halves(mult[...]), 1.0)
            mult[...] = slots[s, at, :].astype(f32) / many
            for part in range(depth // PACK):
                for q in range(PACK // 4):
                    xin, one, two = lifted(part, q)
                    value = jnp.concatenate([jnp.where(one, mult[...], 0.0), jnp.where(two, mult[...], 0.0)], axis=1)
                    acc[...] += fold(q, exact_right(xin[:rows], value))

        return 0

    lax.fori_loop(0, scenes * tiles, tile, 0)
    out = exact_right(one_hot_cols(16, rows), acc[...])
    out = out + swap_halves(out)
    pieces = [out[i : i + 1, :channels] for i in range(feats)]
    pieces.append(jnp.sum(bias[...], axis=0, keepdims=True)[:, :channels])
    pieces += [moments[i : i + 1, :16] for i in range(feats + 1)]
    width = (feats + 1) * (channels + 16)
    pieces.append(jnp.zeros((1, rest.shape[1] - width), f32))
    rest[...] = jnp.concatenate(pieces, axis=1)


def unlift(points, counts, weight, norm, z, winner, slots, edge, far, moments):
    scenes, feats, depth, size = points.shape
    channels = weight.shape[1]
    full = (feats + 2) * PACK
    width = -(-(feats + 1) * (channels + 16) // LANES) * LANES
    return pl.pallas_call(
        unlift_body,
        in_specs=hbm(1) + vmem(3) + hbm(3) + vmem(3),
        out_specs=pl.BlockSpec(memory_space=pltpu.VMEM),
        out_shape=jax.ShapeDtypeStruct((1, width), f32),
        scratch_shapes=[
            pltpu.VMEM((full, PACK * channels), bf16),
            pltpu.VMEM((feats * PACK, LANES), f32),
            pltpu.VMEM((8, LANES), f32),
            pltpu.VMEM(points.shape, bf16),
            pltpu.VMEM((scenes, size, LANES), f32),
            pltpu.VMEM(slots.shape, bf16),
            pltpu.VMEM((TILE, LANES), f32),
            pltpu.VMEM((TILE, LANES), f32),
            pltpu.SemaphoreType.DMA((3, scenes)),
        ],
        compiler_params=scoped,
        name="unlift",
    )(points, counts, weight, norm, z, winner, slots, edge, far, moments)


def adam(fixes, w, states, grad, rate):
    moment = beta_one * states[0] + (1.0 - beta_one) * grad
    second = beta_two * states[1] + (1.0 - beta_two) * grad * grad
    new = w - rate * (moment / fixes[0] / (jnp.sqrt(second / fixes[1]) + adam_eps) + decay_rate * w)
    return new, moment, second, average_keep * states[2] + (1.0 - average_keep) * new


def step_body(devices, parts, fix, got, sums, weight, norm, pm, ps, nm, ns, km, ks, *refs):
    p_new, p_states, p_avg, p_copy, n_new, n_states, n_avg, n_copy, k_new, k_states, k_avg, k_copy, kgrad = refs
    feats, channels = weight.shape
    own = km.shape[1]
    share = own // parts
    peers = got.shape[0]
    scenes = peers // devices
    fixes = (fix[0], fix[1])

    width = share * channels
    kgrad[...] = jnp.zeros_like(kgrad)
    for q in range(parts):
        tot = got[q, :, :width]
        for r in range(1, devices):
            tot = tot + got[r * scenes + q, :, :width]
        for j in range(share):
            kgrad[q * share + j : q * share + j + 1, :channels] = tot[:, j * channels : (j + 1) * channels]
    grad = jnp.transpose(kgrad[...])[:channels, :own]
    new, moment, second, average = adam(fixes, km[...], (ks[0], ks[1], ks[2]), grad, rate_kernel)
    k_new[...] = new
    k_states[0] = moment
    k_states[1] = second
    k_avg[...] = average
    k_copy[...] = new.astype(bf16)

    row = jnp.sum(got[:, :, width:], axis=0)
    cross = jnp.concatenate([row[:, i * channels : (i + 1) * channels] for i in range(feats + 1)], axis=0)
    base = (feats + 1) * channels
    moments = jnp.concatenate([row[:, base + i * 16 : base + (i + 1) * 16] for i in range(feats + 1)], axis=0)
    w = weight[...].astype(f32)
    nw = norm[...].astype(f32)
    total = moments[feats : feats + 1, feats : feats + 1]
    firsts = moments[:feats, feats : feats + 1]
    mixed = None
    first_sum = None
    for i in range(feats):
        part = moments[:feats, i : i + 1] * w[i : i + 1]
        mixed = part if mixed is None else mixed + part
        part = moments[feats : feats + 1, i : i + 1] * w[i : i + 1]
        first_sum = part if first_sum is None else first_sum + part
    mean = first_sum / total
    inv = lax.rsqrt(jnp.sum(mixed * w, axis=0, keepdims=True) / total - mean * mean + norm_eps)
    bias_p = cross[feats : feats + 1]
    gain_p = inv * (jnp.sum(w * cross[:feats], axis=0, keepdims=True) - mean * bias_p)
    spread = inv * (mixed - firsts * mean)
    point_grad = (nw[0:1] * inv) * (cross[:feats] - (firsts * bias_p + spread * gain_p) / total)
    states = (ps[:, 0, :], ps[:, 1, :], ps[:, 2, :])
    new, moment, second, average = adam(fixes, pm[...], states, point_grad, rate_points)
    p_new[...] = new
    p_states[:, 0, :] = moment
    p_states[:, 1, :] = second
    p_avg[...] = average
    p_copy[...] = new.astype(bf16)

    both = jnp.sum(sums[...], axis=0)
    norm_grad = jnp.concatenate([gain_p, bias_p, both[:, channels:], both[:, :channels]], axis=0)
    new, moment, second, average = adam(fixes, nm[...], (ns[0], ns[1], ns[2]), norm_grad, rate_norms)
    n_new[...] = new
    n_states[0] = moment
    n_states[1] = second
    n_avg[...] = average
    n_copy[...] = new.astype(bf16)


def update(devices, parts, fix, got, sums, weight, norm, pm, ps, nm, ns, km, ks):
    feats, channels = weight.shape
    shapes = []
    for m, states in ((pm, (feats, 2, channels)), (nm, (2,) + nm.shape), (km, (2,) + km.shape)):
        shapes.append(jax.ShapeDtypeStruct(m.shape, f32))
        shapes.append(jax.ShapeDtypeStruct(states, f32))
        shapes.append(jax.ShapeDtypeStruct(m.shape, f32))
        shapes.append(jax.ShapeDtypeStruct(m.shape, bf16))
    return pl.pallas_call(
        functools.partial(step_body, devices, parts),
        in_specs=smem(1) + vmem(10),
        out_specs=vmem(12),
        out_shape=shapes,
        scratch_shapes=[pltpu.VMEM((LANES, LANES), f32)],
        compiler_params=scoped,
        name="update",
    )(fix, got, sums, weight, norm, pm, ps, nm, ns, km, ks)


def shifted(x, by):
    length = lax.axis_size("rows")
    pairs = [(i, i + by) for i in range(length) if 0 <= i + by < length]
    return lax.ppermute(x, "rows", pairs)


def exchange(x):
    return lax.all_to_all(x, ("rows", "scene"), 0, 0, tiled=True)


def body(
    points,
    pillar_counts,
    pillar_pixels,
    point_weight,
    point_master,
    point_states,
    norm_weight,
    norm_master,
    norm_states,
    kernel_weight,
    kernel_master,
    kernel_states,
    step_count,
    cotangent,
):
    size = points.shape[3]
    out_rows, scenes, channels, out_cols = cotangent.shape
    cols = 2 * out_cols
    devices = lax.axis_size("rows")
    scene_devices = lax.axis_size("scene")
    peers = devices * scene_devices
    cells = float(out_rows * scenes * out_cols * peers)
    own = kernel_weight.shape[0]
    parts = scene_devices if own % scene_devices == 0 else 1
    share = own // parts * channels
    mine = lax.axis_index("scene") if parts > 1 else jnp.int32(0)

    z, winner, edge, stats, moments = lift(
        mine.reshape(1, 1), points, pillar_counts, pillar_pixels, point_weight, norm_weight, kernel_weight.T, peers, share
    )
    edge = shifted(edge, 1)
    got = near(exchange(stats))
    held = scenes // 2 * EDGE
    far_pixels = edge[held : held + scenes].astype(jnp.int32)
    pairs = out_rows // 2
    own_pixels = pillar_pixels.reshape(scenes * pairs, 1, size // pairs)
    conv, pooled, sums, kernel = convolve(
        devices, parts, own_pixels, far_pixels, got, z, near(edge), norm_weight, pairs, out_cols
    )
    conv_stats = near(exchange(sums[:, None]))

    far_pixels = far_pixels[:, :EDGE]
    at = (pillar_pixels % cols) // 2
    own_at = (pillar_pixels // (2 * cols) + 1) * (out_cols + 8) + at
    take_at = jnp.concatenate([own_at, (far_pixels % cols) // 2], axis=1)
    take_at = jnp.pad(take_at, ((0, 0), (0, -(size + EDGE) % (16 * pairs))))
    take_at = take_at.reshape(scenes * pairs, 1, take_at.shape[1] // pairs)
    own_phase = (pillar_pixels // cols % 2) * 2 + pillar_pixels % 2
    phase = jnp.concatenate([own_phase, 2 + far_pixels % 2], axis=1)
    phase = jnp.pad(phase, ((0, 0), (0, LANES - EDGE))).astype(f32)[:, None]

    result, sums = normalize(cells, conv_stats, conv, cotangent, norm_weight)
    grad_sums = near(exchange(sums[:, None]))
    slots, own_edge, far, kgrad = gradients(
        cells, devices, parts, take_at, conv_stats, grad_sums, conv, cotangent, norm_weight, pooled, phase, kernel
    )
    far, kgrad = lax.optimization_barrier((shifted(far, -1), kgrad))
    if parts > 1:
        kgrad = lax.all_to_all(kgrad, "scene", 0, 0, tiled=True)
    else:
        kgrad = lax.psum(kgrad, "scene")
    rest = unlift(
        points, pillar_counts, point_weight, norm_weight, z, winner, slots, near(own_edge), near(far), near(moments)
    )
    if parts > 1:
        kgrad = jnp.sum(kgrad.reshape(scene_devices, devices, share), axis=0)
    kgrad = jnp.broadcast_to(kgrad[:, None], (devices, scene_devices, share)).reshape(peers, share)
    got = exchange(jnp.concatenate([kgrad, jnp.broadcast_to(rest, (peers, rest.shape[1]))], axis=1)[:, None])
    got = near(got)
    steps_done = step_count[0].astype(f32)
    fix = jnp.stack([1.0 - beta_one**steps_done, 1.0 - beta_two**steps_done])
    outs = update(
        devices,
        parts,
        fix,
        got,
        grad_sums,
        point_weight,
        norm_weight,
        point_master,
        jnp.transpose(point_states, (1, 0, 2)),
        norm_master,
        norm_states,
        kernel_master.T,
        jnp.transpose(kernel_states, (0, 2, 1)),
    )
    outs = list(outs)
    outs[1] = jnp.transpose(outs[1], (1, 0, 2))
    outs[8], outs[10], outs[11] = outs[8].T, outs[10].T, outs[11].T
    outs[9] = jnp.transpose(outs[9], (0, 2, 1))
    return (result, *outs)


def solution(mesh):
    placed = (
        P("scene", None, None, "rows"),
        P("scene", "rows"),
        P("scene", "rows"),
        P(),
        P(),
        P(),
        P(),
        P(),
        P(),
        P("rows", None),
        P("rows", None),
        P(None, "rows", None),
        P(),
        P("rows", "scene", None, None),
    )
    return jax.shard_map(
        body,
        mesh=mesh,
        in_specs=placed,
        out_specs=(
            P("rows", "scene", None, None),
            P(),
            P(),
            P(),
            P(),
            P(),
            P(),
            P(),
            P(),
            P("rows", None),
            P(None, "rows", None),
            P("rows", None),
            P("rows", None),
        ),
        check_vma=False,
    )
```

```python
import functools

import jax
import jax.numpy as jnp
from jax import lax
from jax.experimental import pallas as pl
from jax.experimental.pallas import tpu as pltpu
from jax.sharding import PartitionSpec as P

beta_one = 0.9
beta_two = 0.999
adam_eps = 1e-08
decay_rate = 0.01
average_keep = 0.99
norm_eps = 1e-05
rate_points = 0.3
rate_norms = 0.2
rate_kernel = 0.04

EDGE = 48
BIG = 1e30
PACK = 8
TILE = 256
LANES = 128
f32 = jnp.float32
bf16 = jnp.bfloat16


def iota(shape, dim):
    return lax.broadcasted_iota(jnp.int32, shape, dim)


def dot_nn(a, b):
    return lax.dot_general(a, b, (((1,), (0,)), ((), ())), preferred_element_type=f32)


def dot_nt(a, b):
    return lax.dot_general(a, b, (((1,), (1,)), ((), ())), preferred_element_type=f32)


def dot_tn(a, b):
    return lax.dot_general(a, b, (((0,), (0,)), ((), ())), preferred_element_type=f32)


def split3(x):
    a = x.astype(bf16)
    r = x - a.astype(f32)
    b = r.astype(bf16)
    c = (r - b.astype(f32)).astype(bf16)
    return a, b, c


def exact_left(x, y):
    a, b, c = split3(x)
    return dot_nn(a, y) + (dot_nn(b, y) + dot_nn(c, y))


def exact_right(x, y):
    a, b, c = split3(y)
    return dot_nn(x, a) + (dot_nn(x, b) + dot_nn(x, c))


def swap_halves(x):
    return pltpu.roll(x, x.shape[1] // 2, axis=1)


def twice(row):
    return jnp.concatenate([row, row], axis=1)


def one_hot_rows(rows, cols):
    return (iota((rows, cols), 0) // PACK == iota((rows, cols), 1)).astype(f32).astype(bf16)


def one_hot_cols(rows, cols):
    return (iota((rows, cols), 1) // PACK == iota((rows, cols), 0)).astype(f32).astype(bf16)


def lift_table(weight, norm, table):
    feats, channels = weight.shape
    rows = table.shape[0]
    gain = norm[0:1, :].astype(f32)
    sign = jnp.where(gain > 0, 1.0, jnp.where(gain < 0, -1.0, 0.0))
    signed = weight[...].astype(f32) * sign
    full = jnp.concatenate([signed, jnp.zeros((1, channels), f32), jnp.ones((1, channels), f32)], axis=0)
    full = jnp.concatenate([full, jnp.zeros((16 - feats - 2, channels), f32)], axis=0)
    base = dot_nn(one_hot_rows(rows, 16), twice(full).astype(bf16))
    slot = iota(base.shape, 0) % PACK
    half = iota(base.shape, 1) // channels
    for m in range(PACK // 2):
        table[:, m * LANES : (m + 1) * LANES] = jnp.where(slot == 2 * m + half, base, 0.0).astype(bf16)


def lift_inputs(pts, count, part):
    feats, _, size = pts.shape
    live = (iota((PACK, size), 0) + part * PACK < count).astype(f32)
    kept = (pts.astype(f32) * live[None]).reshape(feats * PACK, size)
    return jnp.concatenate([kept, live, (live - 1.0) * BIG], axis=0).astype(bf16)


def copy_in(source, target, sems, s):
    return pltpu.make_async_copy(source.at[s], target.at[s], sems.at[s])


def half_store(block, s, scenes, value):
    channels = LANES // 2
    spot = pl.ds(pl.multiple_of((s % (scenes // 2)) * EDGE, 8), EDGE)
    lower = iota((EDGE, LANES), 1) < channels
    block[spot, :] = jnp.where(lower == (s < scenes // 2), value, block[spot, :])


def lift_body(
    mine, points, counts, pixels, weight, norm, kernel, z_out, winner_out, edge, payload, moments,
    table, gram, wide, pts, z, low, high, winner, sems,
):
    feats, channels = weight.shape
    scenes, _, depth, size = points.shape
    rows = (feats + 1) * PACK
    for s in range(scenes):
        copy_in(points, pts, sems.at[0], s).start()
    lift_table(weight, norm, table)
    gram[...] = jnp.zeros_like(gram)
    edge[...] = jnp.zeros_like(edge)
    second_half = (iota((1, LANES), 1) >= channels).astype(f32)

    def scene(s, _):
        copy_in(points, pts, sems.at[0], s).wait()
        count = counts[pl.ds(s, 1), :]
        total = None
        for part in range(depth // PACK):
            xin = lift_inputs(pts[s, :, part * PACK : (part + 1) * PACK, :], count, part)
            prod = dot_nt(xin[:rows], xin[:rows])
            total = prod if total is None else total + prod
            for t in range(size // TILE):
                at = slice(t * TILE, (t + 1) * TILE)
                turned = jnp.transpose(xin[:, at])
                for q in range(PACK // 4):
                    l = dot_nn(turned, table[:, q * 256 : (q + 1) * 256])
                    one, two = l[:, :LANES], l[:, LANES:]
                    n_one = second_half + float(part * PACK + q * 4)
                    n_two = n_one + 2.0
                    m = jnp.maximum(one, two)
                    first = jnp.where(two > one, n_two, n_one)
                    last = jnp.where(two >= one, n_two, n_one)
                    if part > 0 or q > 0:
                        old = z[s, at, :]
                        first = jnp.where(m > old, first, low[at, :])
                        last = jnp.where(m >= old, last, high[at, :])
                        m = jnp.maximum(old, m)
                    if part == depth // PACK - 1 and q == PACK // 4 - 1:
                        other = swap_halves(m)
                        first = jnp.where(other > m, swap_halves(first), first)
                        last = jnp.where(other >= m, swap_halves(last), last)
                        m = jnp.maximum(m, other)
                        only = jnp.where(first == last, first, -1.0)
                        winner[s, at, :] = jnp.where(m > -0.5 * BIG, only, 99.0)
                    else:
                        low[at, :] = first
                        high[at, :] = last
                    z[s, at, :] = m
        gram[...] += total
        copy_in(z, z_out, sems.at[1], s).start()
        copy_in(winner, winner_out, sems.at[2], s).start()
        half_store(edge, s, scenes, z[s, :EDGE, :])
        return 0

    lax.fori_loop(0, scenes, scene, 0)

    count_rows = edge.shape[0] - 2 * scenes
    edge[count_rows : count_rows + scenes, :] = pixels[:, :LANES].astype(f32)
    edge[count_rows + scenes :, :] = jnp.ones((scenes, LANES), f32)
    g = gram[...]
    g = jnp.where(iota(g.shape, 0) % PACK == iota(g.shape, 1) % PACK, g, 0.0)
    y = exact_left(g, one_hot_rows(rows, LANES))
    m = exact_right(one_hot_cols(16, rows), y)
    moments[...] = m
    w = jnp.concatenate([weight[...].astype(f32), jnp.zeros((16 - feats, channels), f32)], axis=0)
    aw = exact_left(m[:, :16], w.astype(bf16))
    two = jnp.sum(aw * w, axis=0, keepdims=True)
    one = aw[feats : feats + 1]
    own = kernel.shape[1]
    flat = jnp.concatenate([kernel[...].astype(f32), jnp.zeros((channels, LANES - own), f32)], axis=1)
    wide[...] = jnp.transpose(jnp.concatenate([flat, jnp.zeros((LANES - channels, LANES), f32)], axis=0))
    pieces = [one, two, m[feats : feats + 1]]
    share = (payload.shape[2] - 256) // channels
    for j in range(share):
        pieces.append(wide[pl.ds(mine[0, 0] * share + j, 1), :channels])
    row = jnp.concatenate(pieces, axis=1)
    payload[...] = jnp.broadcast_to(row[:, None, :], payload.shape)
    for s in range(scenes):
        copy_in(z, z_out, sems.at[1], s).wait()
        copy_in(winner, winner_out, sems.at[2], s).wait()


def vmem(count):
    return [pl.BlockSpec(memory_space=pltpu.VMEM)] * count


def smem(count):
    return [pl.BlockSpec(memory_space=pltpu.SMEM)] * count


def hbm(count):
    return [pl.BlockSpec(memory_space=pltpu.HBM)] * count


def lift(mine, points, counts, pixels, weight, norm, kernel, peers, share):
    scenes, feats, depth, size = points.shape
    channels = weight.shape[1]
    full = (feats + 2) * PACK
    rows = (feats + 1) * PACK
    edge_rows = scenes // 2 * EDGE + 2 * scenes
    return pl.pallas_call(
        lift_body,
        in_specs=smem(1) + hbm(1) + vmem(5),
        out_specs=hbm(2) + vmem(3),
        out_shape=[
            jax.ShapeDtypeStruct((scenes, size, LANES), f32),
            jax.ShapeDtypeStruct((scenes, size, LANES), f32),
            jax.ShapeDtypeStruct((edge_rows, LANES), f32),
            jax.ShapeDtypeStruct((peers, 1, 256 + share), f32),
            jax.ShapeDtypeStruct((16, LANES), f32),
        ],
        scratch_shapes=[
            pltpu.VMEM((full, PACK * channels), bf16),
            pltpu.VMEM((rows, rows), f32),
            pltpu.VMEM((LANES, LANES), f32),
            pltpu.VMEM(points.shape, bf16),
            pltpu.VMEM((scenes, size, LANES), f32),
            pltpu.VMEM((size, LANES), f32),
            pltpu.VMEM((size, LANES), f32),
            pltpu.VMEM((scenes, size, LANES), f32),
            pltpu.SemaphoreType.DMA((3, scenes)),
        ],
        name="lift",
    )(mine, points, counts, pixels, weight, norm, kernel)


def gather_kernel(got, kern, devices, parts):
    channels = kern.shape[1]
    share = kern.shape[0] // devices // parts
    peers = got.shape[0]
    for j in range(share):
        rows = got[:, 0, 256 + j * channels : 256 + (j + 1) * channels]
        if parts > 1:
            kern[pl.ds(j, peers, stride=share), :] = rows
        else:
            for r in range(devices):
                at = r * (peers // devices)
                kern[r * share + j : r * share + j + 1, :] = rows[at : at + 1]


def tap(kern, a, b):
    channels = kern.shape[1]
    if a is None or b is None:
        return jnp.zeros((channels, channels), f32)
    return kern[(3 * a + b) * channels : (3 * a + b + 1) * channels, :]


def edge_rows_of(block, s, scenes, lower):
    spot = pl.ds(pl.multiple_of((s % (scenes // 2)) * EDGE, 8), EDGE)
    rows = jnp.where(lower == (s < scenes // 2), block[spot, :], 0.0)
    return rows + swap_halves(rows)


def conv_body(
    devices, parts, pix, far_pix, got, z_in, edge, norm, conv_out, pooled_out, sums, kernel,
    params, source, kern, taps, grid_a, grid_b, side, acc, z, conv, pooled, sems,
):
    scenes, size, _ = z.shape
    for s in range(scenes):
        copy_in(z_in, z, sems.at[0], s).start()
    channels = norm.shape[1]
    _, pairs, out_cols, _ = conv.shape
    cols = 2 * out_cols
    last_row = (4 * pairs - 1) * cols
    tot = jnp.sum(got[:, :, :256], axis=0)
    count = tot[:, 2 * channels + 9 : 2 * channels + 10]
    mean = tot[:, :channels] / count
    inv = lax.rsqrt(tot[:, channels : 2 * channels] / count - mean * mean + norm_eps)
    nw = norm[...].astype(f32)
    gain = nw[0:1]
    sign = jnp.where(gain > 0, 1.0, jnp.where(gain < 0, -1.0, 0.0))
    params[0:1] = twice(mean)
    params[1:2] = twice(inv)
    params[2:3] = twice(gain)
    params[3:4] = twice(nw[1:2])
    params[4:5] = twice(sign)
    gather_kernel(got, kern, devices, parts)
    kernel[...] = kern[...].astype(bf16)
    for w, (low, high) in enumerate(((0, None), (1, None), (2, 0), (None, 1), (None, 2))):
        none = tap(kern, None, None)
        top = jnp.concatenate([tap(kern, low, 1), tap(kern, high, 1), none, none], axis=1)
        end = jnp.concatenate([tap(kern, low, 2), tap(kern, high, 2), tap(kern, low, 0), tap(kern, high, 0)], axis=1)
        taps[w] = jnp.concatenate([top, end], axis=0).astype(bf16)
    grid_a[...] = jnp.zeros_like(grid_a)
    grid_b[...] = jnp.zeros_like(grid_b)
    side[...] = jnp.zeros_like(side)
    acc[...] = jnp.zeros_like(acc)

    def pool(x, ok):
        pre = params[2:3] * ((x * params[4:5] - params[0:1]) * params[1:2]) + params[3:4]
        return jnp.where(ok, jnp.maximum(pre, 0.0), 0.0).astype(bf16)

    own_at = 8 + cols
    far_at = 8 - last_row

    def fill(s):
        zs = z[s]
        own = pool(zs, zs > -0.5 * BIG)
        pooled[s, :size] = own
        source[:size] = own.astype(f32)
        far = edge_rows_of(edge, s, scenes, iota((EDGE, LANES), 1) < channels)
        flag = edge[edge.shape[0] - scenes : edge.shape[0] - scenes + 1, :]
        far = pool(far, (far > -0.5 * BIG) & (flag > 0.5))
        pooled[s, size:] = jnp.concatenate([far, jnp.zeros((LANES - EDGE, LANES), bf16)], axis=0)
        source[size : size + EDGE] = far.astype(f32)

    def place_far(dst, s):
        for p in range(EDGE):
            at = jnp.maximum(far_pix[s, p], last_row) + far_at
            dst[pl.ds(at, 1), :] = source[size + p : size + p + 1, :]

    def place(dst, s, j):
        rows = dst.at[pl.ds(own_at, 4 * pairs * cols), :]
        some = size // pairs
        line = s * pairs + j
        base = pl.multiple_of(j * some, 8)
        for p in range(some):
            rows[pl.ds(pix[line, 0, p], 1), :] = source[pl.ds(base + p, 1), :]

    left = iota((out_cols, LANES), 1) < channels

    def convolve_pair(src, s, j):
        out = None
        for w in range(5):
            base = 8 + (4 * j + w) * cols
            even = src[pl.ds(base, out_cols, stride=2), :]
            odd = src[pl.ds(base + 1, out_cols, stride=2), :]
            part = dot_nn(jnp.where(left, even, odd).astype(bf16), taps[w])
            out = part if out is None else out + part
        side[8:, :] = out[:, LANES:]
        value = out[:, :LANES] + side[7 : 7 + out_cols, :]
        conv[s, j] = value
        acc[0:8] += jnp.sum(value.reshape(out_cols // 8, 8, LANES), axis=0)
        acc[8:16] += jnp.sum((value * value).reshape(out_cols // 8, 8, LANES), axis=0)
        base = pl.multiple_of(8 + 4 * j * cols, 8)
        src[pl.ds(base, 4 * cols), :] = jnp.zeros((4 * cols, LANES), f32)

    def clear_last(src):
        src[8 + 4 * pairs * cols : 8 + (4 * pairs + 1) * cols, :] = jnp.zeros((cols, LANES), f32)

    copy_in(z_in, z, sems.at[0], 0).wait()
    fill(0)
    place_far(grid_a, 0)

    def start(j, _):
        place(grid_a, 0, j)
        return 0

    lax.fori_loop(0, pairs, start, 0)

    def two_scenes(i, _):
        for k, (src, dst) in enumerate(((grid_a, grid_b), (grid_b, grid_a))):
            s = 2 * i + k
            ahead = jnp.minimum(s + 1, scenes - 1)

            @pl.when(s + 1 < scenes)
            def _():
                copy_in(z_in, z, sems.at[0], s + 1).wait()

            fill(ahead)
            place_far(dst, ahead)

            def step(j, _):
                convolve_pair(src, s, j)
                place(dst, ahead, j)
                return 0

            lax.fori_loop(0, pairs, step, 0)
            clear_last(src)
            copy_in(conv, conv_out, sems.at[1], s).start()
            copy_in(pooled, pooled_out, sems.at[2], s).start()
        return 0

    lax.fori_loop(0, scenes // 2, two_scenes, 0)
    for s in range(scenes):
        copy_in(conv, conv_out, sems.at[1], s).wait()
        copy_in(pooled, pooled_out, sems.at[2], s).wait()
    sums[...] = jnp.broadcast_to(both_sums(acc, channels), sums.shape)


def both_sums(acc, channels):
    one = jnp.sum(acc[0:8], axis=0, keepdims=True)
    two = jnp.sum(acc[8:16], axis=0, keepdims=True)
    one = one + swap_halves(one)
    two = two + swap_halves(two)
    return jnp.where(iota((1, LANES), 1) < channels, one, two)


def convolve(devices, parts, pix, far_pix, got, z, edge, norm, pairs, out_cols):
    scenes, size, _ = z.shape
    peers = got.shape[0]
    channels = norm.shape[1]
    cells = 8 + (4 * pairs + 1) * 2 * out_cols + 8
    return pl.pallas_call(
        functools.partial(conv_body, devices, parts),
        in_specs=smem(2) + vmem(1) + hbm(1) + vmem(2),
        out_specs=hbm(2) + vmem(2),
        out_shape=[
            jax.ShapeDtypeStruct((scenes, pairs, out_cols, LANES), f32),
            jax.ShapeDtypeStruct((scenes, size + LANES, LANES), bf16),
            jax.ShapeDtypeStruct((peers, LANES), f32),
            jax.ShapeDtypeStruct((9 * channels, channels), bf16),
        ],
        scratch_shapes=[
            pltpu.VMEM((8, LANES), f32),
            pltpu.VMEM((size + LANES, LANES), f32),
            pltpu.VMEM((9 * channels, channels), f32),
            pltpu.VMEM((5, LANES, 2 * LANES), bf16),
            pltpu.VMEM((cells, LANES), f32),
            pltpu.VMEM((cells, LANES), f32),
            pltpu.VMEM((out_cols + 8, LANES), f32),
            pltpu.VMEM((16, LANES), f32),
            pltpu.VMEM((scenes, size, LANES), f32),
            pltpu.VMEM((scenes, pairs, out_cols, LANES), f32),
            pltpu.VMEM((scenes, size + LANES, LANES), bf16),
            pltpu.SemaphoreType.DMA((3, scenes)),
        ],
        name="convolve",
    )(pix, far_pix, got, z, edge, norm)


def split_sums(stats, channels):
    tot = jnp.sum(stats[...], axis=0)
    lower = iota((1, LANES), 1) < channels
    turned = swap_halves(tot)
    return jnp.where(lower, tot, turned), jnp.where(lower, turned, tot)


def conv_params(cells, stats, norm):
    one, two = split_sums(stats, norm.shape[1])
    mean = one / cells
    inv = lax.rsqrt(two / cells - mean * mean + norm_eps)
    nw = norm[...].astype(f32)
    return mean, inv, twice(nw[2:3]), twice(nw[3:4])


def turned_pair(block, j, k):
    _, _, channels, cols = block.shape
    return jnp.transpose(block[2 * j : 2 * j + 2, k].reshape(2 * channels, cols)).astype(f32)


def scene_copy(source, target, sems, s):
    return pltpu.make_async_copy(source.at[:, s], target.at[:, s], sems.at[s])


def norm_body(cells, stats, conv_in, cot_in, norm, result_out, sums, acc, conv, cot, result, sems):
    channels = norm.shape[1]
    scenes, pairs, out_cols, _ = conv.shape
    for s in range(scenes):
        copy_in(conv_in, conv, sems.at[0], s).start()
        scene_copy(cot_in, cot, sems.at[1], s).start()
    mean, inv, gain, bias = conv_params(cells, stats, norm)
    acc[...] = jnp.zeros_like(acc)

    def scene(k, _):
        copy_in(conv_in, conv, sems.at[0], k).wait()
        scene_copy(cot_in, cot, sems.at[1], k).wait()
        for j in range(pairs):
            xhat = (conv[k, j] - mean) * inv
            pre = gain * xhat + bias
            out = jnp.transpose(jnp.maximum(pre, 0.0).astype(bf16))
            result[2 * j : 2 * j + 2, k] = out.reshape(2, channels, out_cols)
            back = jnp.where(pre > 0, turned_pair(cot, j, k), 0.0)
            acc[0:8] += jnp.sum(back.reshape(out_cols // 8, 8, LANES), axis=0)
            acc[8:16] += jnp.sum((back * xhat).reshape(out_cols // 8, 8, LANES), axis=0)
        scene_copy(result, result_out, sems.at[2], k).start()
        return 0

    lax.fori_loop(0, scenes, scene, 0)
    sums[...] = jnp.broadcast_to(both_sums(acc, channels), sums.shape)
    for s in range(scenes):
        scene_copy(result, result_out, sems.at[2], s).wait()


def normalize(cells, stats, conv, cot, norm):
    peers = stats.shape[0]
    scenes = conv.shape[0]
    return pl.pallas_call(
        functools.partial(norm_body, cells),
        in_specs=vmem(1) + hbm(2) + vmem(1),
        out_specs=hbm(1) + vmem(1),
        out_shape=[
            jax.ShapeDtypeStruct(cot.shape, bf16),
            jax.ShapeDtypeStruct((peers, LANES), f32),
        ],
        scratch_shapes=[
            pltpu.VMEM((16, LANES), f32),
            pltpu.VMEM(conv.shape, f32),
            pltpu.VMEM(cot.shape, bf16),
            pltpu.VMEM(cot.shape, bf16),
            pltpu.SemaphoreType.DMA((3, scenes)),
        ],
        name="normalize",
    )(stats, conv, cot, norm)


def grad_body(
    cells, devices, parts, idx, stats, sums, conv_in, cot_in, norm, pooled_in, phase, kernel, slots_out, edge, far, kgrad,
    taps, field_a, field_b, taken_a, taken_b, turn, column, acc, rows_k, conv, cot, pooled, slots, exact, sems,
):
    scenes, pairs, out_cols, _ = conv.shape
    channels = norm.shape[1]
    size = slots.shape[1]
    strip = out_cols + 8
    some = idx.shape[2]
    for s in range(scenes):
        copy_in(conv_in, conv, sems.at[0], s).start()
        scene_copy(cot_in, cot, sems.at[1], s).start()
    for s in range(scenes):
        copy_in(pooled_in, pooled, sems.at[2], s).start()
    for hp in range(2):
        for up in range(2):
            line = []
            for dw in range(2):
                for dr in range(2):
                    a = ((1, None), (2, 0))[hp][dr]
                    b = ((1, None), (2, 0))[up][dw]
                    if a is None or b is None:
                        line.append(jnp.zeros((channels, channels), f32))
                    else:
                        at = (3 * a + b) * channels
                        line.append(kernel[at : at + channels, :].astype(f32))
            ph = 2 * hp + up
            taps[ph * channels : (ph + 1) * channels, :] = jnp.concatenate(line, axis=1).astype(bf16)
    for block in (field_a, field_b, taken_a, taken_b, acc):
        block[...] = jnp.zeros_like(block)

    def phases(s, _):
        for c in range(column.shape[1] // LANES):
            row = phase[s, :, c * LANES : (c + 1) * LANES]
            column[s, c * LANES : (c + 1) * LANES, :] = jnp.transpose(jnp.broadcast_to(row, (LANES, LANES)))
        return 0

    lax.fori_loop(0, scenes, phases, 0)
    mean, inv, gain, bias = conv_params(cells, stats, norm)
    bias_grad, gain_grad = split_sums(sums, channels)
    scale = gain * inv / cells
    left = iota((out_cols, LANES), 1) < channels
    half = (iota((some, LANES), 1) >= channels).astype(f32)

    def field(dst, s, j):
        xhat = (conv[s, j] - mean) * inv
        pre = gain * xhat + bias
        both = cot[pl.ds(2 * j, 2), s].reshape(2 * channels, out_cols)
        back = jnp.where(pre > 0, jnp.transpose(both).astype(f32), 0.0)
        grad = scale * (cells * back - bias_grad - xhat * gain_grad)
        grad = grad.astype(bf16).astype(f32)
        turned = swap_halves(grad)
        base = pl.multiple_of(2 * j * strip, 8)
        dst[pl.ds(base, out_cols), :] = jnp.where(left, turn[...], turned)
        dst[pl.ds(pl.multiple_of(base + strip, 8), out_cols), :] = grad
        turn[...] = turned

    def take(dst, src, s, j):
        line = s * pairs + j
        for p in range(some):
            dst[2 * p : 2 * p + 2, :] = src[pl.ds(idx[line, 0, p], 2), :]

    def product(src, s, j):
        at = pl.ds(pl.multiple_of(j * some, 16), some)
        part = jnp.concatenate([src[pl.ds(0, some, stride=2), :], src[pl.ds(1, some, stride=2), :]], axis=1).astype(bf16)
        out = dot_nt(part, taps[...])
        ph = column[s, at, :]
        is_even = ph == half
        is_odd = ph == half + 2.0
        value = jnp.where(is_even, out[:, :LANES], 0.0) + jnp.where(is_odd, out[:, LANES:], 0.0)
        value = value + swap_halves(value)
        pf = pooled[s, at, :].astype(f32)
        value = jnp.where(pf > 0, value, 0.0)
        exact[s, at, :] = value
        slots[s, at, :] = value.astype(bf16)
        split = jnp.concatenate([jnp.where(is_even, pf, 0.0), jnp.where(is_odd, pf, 0.0)], axis=1)
        acc[...] += dot_tn(split.astype(bf16), part)

    def walk(dst, src, s):
        before = jnp.clip(s - 1, 0, scenes - 1)
        older = jnp.clip(s - 2, 0, scenes - 1)

        def step(i, _):
            for k, (to, of) in enumerate(((taken_a, taken_b), (taken_b, taken_a))):
                j = 2 * i + k
                if dst is not None:
                    field(dst, s, j)
                take(to, src, before, j)
                last = jnp.where(j > 0, before, older)
                product(of, last, jnp.where(j > 0, j - 1, pairs - 1))
            return 0

        if dst is not None:
            copy_in(conv_in, conv, sems.at[0], s).wait()
            scene_copy(cot_in, cot, sems.at[1], s).wait()
            copy_in(pooled_in, pooled, sems.at[2], s).wait()
            turn[...] = jnp.zeros_like(turn)
        lax.fori_loop(0, pairs // 2, step, 0)
        if dst is not None:
            dst[2 * pairs * strip : 2 * pairs * strip + out_cols, :] = jnp.where(left, turn[...], 0.0)

    def two_scenes(i, _):
        walk(field_a, field_b, 2 * i)
        walk(field_b, field_a, 2 * i + 1)
        return 0

    lax.fori_loop(0, scenes // 2, two_scenes, 0)
    walk(None, field_b, scenes)
    product(taken_b, scenes - 1, pairs - 1)
    for s in range(scenes):
        copy_in(slots, slots_out, sems.at[0], s).start()
    far[...] = jnp.zeros_like(far)
    edge[...] = jnp.zeros_like(edge)

    def pick(s, _):
        half_store(edge, s, scenes, exact[s, :EDGE, :])
        half_store(far, s, scenes, exact[s, size - LANES : size - LANES + EDGE, :])
        return 0

    lax.fori_loop(0, scenes, pick, 0)
    for a in range(3):
        for b in range(3):
            hp, dr = ((1, 1), (0, 0), (1, 0))[a]
            up, dw = ((1, 1), (0, 0), (1, 0))[b]
            row, col = hp * 2 + up, dw * 2 + dr
            at = (3 * a + b) * channels
            rows_k[at : at + channels, :] = acc[
                row * channels : (row + 1) * channels, col * channels : (col + 1) * channels
            ]
    own = rows_k.shape[0] // devices
    share = own // parts
    for q in range(parts):
        for j in range(share):
            lanes = slice(j * channels, (j + 1) * channels)
            kgrad[q * devices : (q + 1) * devices, lanes] = rows_k[pl.ds(q * share + j, devices, stride=own), :]
    for s in range(scenes):
        copy_in(slots, slots_out, sems.at[0], s).wait()


def gradients(cells, devices, parts, idx, stats, sums, conv, cot, norm, pooled, phase, kernel):
    scenes, pairs, out_cols, _ = conv.shape
    channels = norm.shape[1]
    rows = pooled.shape[1]
    return pl.pallas_call(
        functools.partial(grad_body, cells, devices, parts),
        in_specs=smem(1) + vmem(2) + hbm(2) + vmem(1) + hbm(1) + vmem(2),
        out_specs=hbm(1) + vmem(3),
        out_shape=[
            jax.ShapeDtypeStruct((scenes, rows, LANES), bf16),
            jax.ShapeDtypeStruct((scenes // 2 * EDGE, LANES), f32),
            jax.ShapeDtypeStruct((scenes // 2 * EDGE, LANES), f32),
            jax.ShapeDtypeStruct((parts * devices, 9 * channels * channels // devices // parts), f32),
        ],
        scratch_shapes=[
            pltpu.VMEM((4 * channels, 4 * channels), bf16),
            pltpu.VMEM(((2 * pairs + 1) * (out_cols + 8), LANES), f32),
            pltpu.VMEM(((2 * pairs + 1) * (out_cols + 8), LANES), f32),
            pltpu.VMEM((2 * idx.shape[2], LANES), f32),
            pltpu.VMEM((2 * idx.shape[2], LANES), f32),
            pltpu.VMEM((out_cols, LANES), f32),
            pltpu.VMEM((scenes, rows, LANES), f32),
            pltpu.VMEM((4 * channels, 4 * channels), f32),
            pltpu.VMEM((9 * channels, channels), f32),
            pltpu.VMEM(conv.shape, f32),
            pltpu.VMEM(cot.shape, bf16),
            pltpu.VMEM(pooled.shape, bf16),
            pltpu.VMEM((scenes, rows, LANES), bf16),
            pltpu.VMEM((scenes, rows, LANES), f32),
            pltpu.SemaphoreType.DMA((3, scenes)),
        ],
        name="gradients",
    )(idx, stats, sums, conv, cot, norm, pooled, phase, kernel)


def unlift_body(
    points, counts, weight, norm, z, winner_in, slots_in, edge, far, moments, rest,
    table, acc, bias, pts, winner, slots, best, mult, sems,
):
    feats, channels = weight.shape
    scenes, _, depth, size = points.shape
    rows = feats * PACK
    tiles = size // TILE
    for s in range(scenes):
        copy_in(points, pts, sems.at[0], s).start()
        copy_in(winner_in, winner, sems.at[1], s).start()
        copy_in(slots_in, slots, sems.at[2], s).start()
    lift_table(weight, norm, table)
    acc[...] = jnp.zeros_like(acc)
    bias[...] = jnp.zeros_like(bias)
    second_half = (iota((1, LANES), 1) >= channels).astype(f32)
    slot = iota((rows, LANES), 0) % PACK
    upper = (iota((rows, LANES), 1) >= channels).astype(jnp.int32)

    def fold(q, prod):
        near_n = slot - 4 * q
        return jnp.where(near_n == upper, prod[:, :LANES], 0.0) + jnp.where(near_n == upper + 2, prod[:, LANES:], 0.0)

    def tile(u, _):
        s = u // tiles
        t = u % tiles
        at = pl.ds(pl.multiple_of(t * TILE, TILE), TILE)

        @pl.when(t == 0)
        def _():
            copy_in(points, pts, sems.at[0], s).wait()
            copy_in(winner_in, winner, sems.at[1], s).wait()
            copy_in(slots_in, slots, sems.at[2], s).wait()
            lower = iota((EDGE, LANES), 1) < channels
            whole = edge_rows_of(edge, s, scenes, lower) + edge_rows_of(far, s, scenes, lower)
            slots[s, :EDGE, :] = whole.astype(bf16)

        grad = slots[s, at, :].astype(f32)
        who = winner[s, at, :]
        bias[...] += jnp.sum(grad.reshape(TILE // 8, 8, LANES), axis=0)
        total = None
        for part in range(depth // PACK):
            x = pts[s, :, part * PACK : (part + 1) * PACK, at].reshape(rows, TILE)
            for q in range(PACK // 4):
                n_one = second_half + float(part * PACK + q * 4)
                value = jnp.concatenate(
                    [jnp.where(who == n_one, grad, 0.0), jnp.where(who == n_one + 2.0, grad, 0.0)], axis=1
                )
                prod = fold(q, dot_nn(x, value.astype(bf16)))
                total = prod if total is None else total + prod
        acc[...] += total

        @pl.when(jnp.min(who) < 0.0)
        def _():
            fetch = pltpu.make_async_copy(z.at[s, at], best, sems.at[0, 0])
            fetch.start()
            fetch.wait()
            best[...] = jnp.where(winner[s, at, :] < 0.0, best[...], BIG)
            mult[...] = jnp.zeros_like(mult)
            count = counts[pl.ds(s, 1), at]

            def lifted(part, q):
                xin = lift_inputs(pts[s, :, part * PACK : (part + 1) * PACK, at], count, part)
                l = dot_nn(jnp.transpose(xin), table[:, q * 256 : (q + 1) * 256])
                return xin, l[:, :LANES] == best[...], l[:, LANES:] == best[...]

            for part in range(depth // PACK):
                for q in range(PACK // 4):
                    _, one, two = lifted(part, q)
                    mult[...] += jnp.where(one, 1.0, 0.0) + jnp.where(two, 1.0, 0.0)
            many = jnp.maximum(mult[...] + swap_halves(mult[...]), 1.0)
            mult[...] = slots[s, at, :].astype(f32) / many
            for part in range(depth // PACK):
                for q in range(PACK // 4):
                    xin, one, two = lifted(part, q)
                    value = jnp.concatenate([jnp.where(one, mult[...], 0.0), jnp.where(two, mult[...], 0.0)], axis=1)
                    acc[...] += fold(q, exact_right(xin[:rows], value))

        return 0

    lax.fori_loop(0, scenes * tiles, tile, 0)
    out = exact_right(one_hot_cols(16, rows), acc[...])
    out = out + swap_halves(out)
    pieces = [out[i : i + 1, :channels] for i in range(feats)]
    pieces.append(jnp.sum(bias[...], axis=0, keepdims=True)[:, :channels])
    pieces += [moments[i : i + 1, :16] for i in range(feats + 1)]
    width = (feats + 1) * (channels + 16)
    pieces.append(jnp.zeros((1, rest.shape[1] - width), f32))
    rest[...] = jnp.concatenate(pieces, axis=1)


def unlift(points, counts, weight, norm, z, winner, slots, edge, far, moments):
    scenes, feats, depth, size = points.shape
    channels = weight.shape[1]
    full = (feats + 2) * PACK
    width = -(-(feats + 1) * (channels + 16) // LANES) * LANES
    return pl.pallas_call(
        unlift_body,
        in_specs=hbm(1) + vmem(3) + hbm(3) + vmem(3),
        out_specs=pl.BlockSpec(memory_space=pltpu.VMEM),
        out_shape=jax.ShapeDtypeStruct((1, width), f32),
        scratch_shapes=[
            pltpu.VMEM((full, PACK * channels), bf16),
            pltpu.VMEM((feats * PACK, LANES), f32),
            pltpu.VMEM((8, LANES), f32),
            pltpu.VMEM(points.shape, bf16),
            pltpu.VMEM((scenes, size, LANES), f32),
            pltpu.VMEM(slots.shape, bf16),
            pltpu.VMEM((TILE, LANES), f32),
            pltpu.VMEM((TILE, LANES), f32),
            pltpu.SemaphoreType.DMA((3, scenes)),
        ],
        name="unlift",
    )(points, counts, weight, norm, z, winner, slots, edge, far, moments)


def adam(fixes, w, states, grad, rate):
    moment = beta_one * states[0] + (1.0 - beta_one) * grad
    second = beta_two * states[1] + (1.0 - beta_two) * grad * grad
    new = w - rate * (moment / fixes[0] / (jnp.sqrt(second / fixes[1]) + adam_eps) + decay_rate * w)
    return new, moment, second, average_keep * states[2] + (1.0 - average_keep) * new


def step_body(devices, parts, fix, got, sums, weight, norm, pm, ps, nm, ns, km, ks, *refs):
    p_new, p_states, p_avg, p_copy, n_new, n_states, n_avg, n_copy, k_new, k_states, k_avg, k_copy, kgrad = refs
    feats, channels = weight.shape
    own = km.shape[1]
    share = own // parts
    peers = got.shape[0]
    scenes = peers // devices
    fixes = (fix[0], fix[1])

    width = share * channels
    kgrad[...] = jnp.zeros_like(kgrad)
    for q in range(parts):
        tot = got[q, :, :width]
        for r in range(1, devices):
            tot = tot + got[r * scenes + q, :, :width]
        for j in range(share):
            kgrad[q * share + j : q * share + j + 1, :channels] = tot[:, j * channels : (j + 1) * channels]
    grad = jnp.transpose(kgrad[...])[:channels, :own]
    new, moment, second, average = adam(fixes, km[...], (ks[0], ks[1], ks[2]), grad, rate_kernel)
    k_new[...] = new
    k_states[0] = moment
    k_states[1] = second
    k_avg[...] = average
    k_copy[...] = new.astype(bf16)

    row = jnp.sum(got[:, :, width:], axis=0)
    cross = jnp.concatenate([row[:, i * channels : (i + 1) * channels] for i in range(feats + 1)], axis=0)
    base = (feats + 1) * channels
    moments = jnp.concatenate([row[:, base + i * 16 : base + (i + 1) * 16] for i in range(feats + 1)], axis=0)
    w = weight[...].astype(f32)
    nw = norm[...].astype(f32)
    total = moments[feats : feats + 1, feats : feats + 1]
    firsts = moments[:feats, feats : feats + 1]
    mixed = None
    first_sum = None
    for i in range(feats):
        part = moments[:feats, i : i + 1] * w[i : i + 1]
        mixed = part if mixed is None else mixed + part
        part = moments[feats : feats + 1, i : i + 1] * w[i : i + 1]
        first_sum = part if first_sum is None else first_sum + part
    mean = first_sum / total
    inv = lax.rsqrt(jnp.sum(mixed * w, axis=0, keepdims=True) / total - mean * mean + norm_eps)
    bias_p = cross[feats : feats + 1]
    gain_p = inv * (jnp.sum(w * cross[:feats], axis=0, keepdims=True) - mean * bias_p)
    spread = inv * (mixed - firsts * mean)
    point_grad = (nw[0:1] * inv) * (cross[:feats] - (firsts * bias_p + spread * gain_p) / total)
    states = (ps[:, 0, :], ps[:, 1, :], ps[:, 2, :])
    new, moment, second, average = adam(fixes, pm[...], states, point_grad, rate_points)
    p_new[...] = new
    p_states[:, 0, :] = moment
    p_states[:, 1, :] = second
    p_avg[...] = average
    p_copy[...] = new.astype(bf16)

    both = jnp.sum(sums[...], axis=0)
    norm_grad = jnp.concatenate([gain_p, bias_p, both[:, channels:], both[:, :channels]], axis=0)
    new, moment, second, average = adam(fixes, nm[...], (ns[0], ns[1], ns[2]), norm_grad, rate_norms)
    n_new[...] = new
    n_states[0] = moment
    n_states[1] = second
    n_avg[...] = average
    n_copy[...] = new.astype(bf16)


def update(devices, parts, fix, got, sums, weight, norm, pm, ps, nm, ns, km, ks):
    feats, channels = weight.shape
    shapes = []
    for m, states in ((pm, (feats, 2, channels)), (nm, (2,) + nm.shape), (km, (2,) + km.shape)):
        shapes.append(jax.ShapeDtypeStruct(m.shape, f32))
        shapes.append(jax.ShapeDtypeStruct(states, f32))
        shapes.append(jax.ShapeDtypeStruct(m.shape, f32))
        shapes.append(jax.ShapeDtypeStruct(m.shape, bf16))
    return pl.pallas_call(
        functools.partial(step_body, devices, parts),
        in_specs=smem(1) + vmem(10),
        out_specs=vmem(12),
        out_shape=shapes,
        scratch_shapes=[pltpu.VMEM((LANES, LANES), f32)],
        name="update",
    )(fix, got, sums, weight, norm, pm, ps, nm, ns, km, ks)


def shifted(x, by):
    length = lax.axis_size("rows")
    pairs = [(i, i + by) for i in range(length) if 0 <= i + by < length]
    return lax.ppermute(x, "rows", pairs)


def exchange(x):
    return lax.all_to_all(x, ("rows", "scene"), 0, 0, tiled=True)


def body(
    points,
    pillar_counts,
    pillar_pixels,
    point_weight,
    point_master,
    point_states,
    norm_weight,
    norm_master,
    norm_states,
    kernel_weight,
    kernel_master,
    kernel_states,
    step_count,
    cotangent,
):
    size = points.shape[3]
    out_rows, scenes, channels, out_cols = cotangent.shape
    cols = 2 * out_cols
    devices = lax.axis_size("rows")
    scene_devices = lax.axis_size("scene")
    peers = devices * scene_devices
    cells = float(out_rows * scenes * out_cols * peers)
    own = kernel_weight.shape[0]
    parts = scene_devices if own % scene_devices == 0 else 1
    share = own // parts * channels
    mine = lax.axis_index("scene") if parts > 1 else jnp.int32(0)

    z, winner, edge, stats, moments = lift(
        mine.reshape(1, 1), points, pillar_counts, pillar_pixels, point_weight, norm_weight, kernel_weight.T, peers, share
    )
    edge = shifted(edge, 1)
    got = exchange(stats)
    held = scenes // 2 * EDGE
    far_pixels = edge[held : held + scenes].astype(jnp.int32)
    pairs = out_rows // 2
    own_pixels = pillar_pixels.reshape(scenes * pairs, 1, size // pairs)
    conv, pooled, sums, kernel = convolve(
        devices, parts, own_pixels, far_pixels, got, z, edge, norm_weight, pairs, out_cols
    )
    conv_stats = exchange(sums[:, None])

    far_pixels = far_pixels[:, :EDGE]
    at = (pillar_pixels % cols) // 2
    own_at = (pillar_pixels // (2 * cols) + 1) * (out_cols + 8) + at
    take_at = jnp.concatenate([own_at, (far_pixels % cols) // 2], axis=1)
    take_at = jnp.pad(take_at, ((0, 0), (0, -(size + EDGE) % (16 * pairs))))
    take_at = take_at.reshape(scenes * pairs, 1, take_at.shape[1] // pairs)
    own_phase = (pillar_pixels // cols % 2) * 2 + pillar_pixels % 2
    phase = jnp.concatenate([own_phase, 2 + far_pixels % 2], axis=1)
    phase = jnp.pad(phase, ((0, 0), (0, LANES - EDGE))).astype(f32)[:, None]

    result, sums = normalize(cells, conv_stats, conv, cotangent, norm_weight)
    grad_sums = exchange(sums[:, None])
    slots, own_edge, far, kgrad = gradients(
        cells, devices, parts, take_at, conv_stats, grad_sums, conv, cotangent, norm_weight, pooled, phase, kernel
    )
    far, kgrad = lax.optimization_barrier((shifted(far, -1), kgrad))
    if parts > 1:
        kgrad = lax.all_to_all(kgrad, "scene", 0, 0, tiled=True)
    else:
        kgrad = lax.psum(kgrad, "scene")
    rest = unlift(
        points, pillar_counts, point_weight, norm_weight, z, winner, slots, own_edge, far, moments
    )
    if parts > 1:
        kgrad = jnp.sum(kgrad.reshape(scene_devices, devices, share), axis=0)
    kgrad = jnp.broadcast_to(kgrad[:, None], (devices, scene_devices, share)).reshape(peers, share)
    got = exchange(jnp.concatenate([kgrad, jnp.broadcast_to(rest, (peers, rest.shape[1]))], axis=1)[:, None])
    got = got
    steps_done = step_count[0].astype(f32)
    fix = jnp.stack([1.0 - beta_one**steps_done, 1.0 - beta_two**steps_done])
    outs = update(
        devices,
        parts,
        fix,
        got,
        grad_sums,
        point_weight,
        norm_weight,
        point_master,
        jnp.transpose(point_states, (1, 0, 2)),
        norm_master,
        norm_states,
        kernel_master.T,
        jnp.transpose(kernel_states, (0, 2, 1)),
    )
    outs = list(outs)
    outs[1] = jnp.transpose(outs[1], (1, 0, 2))
    outs[8], outs[10], outs[11] = outs[8].T, outs[10].T, outs[11].T
    outs[9] = jnp.transpose(outs[9], (0, 2, 1))
    return (result, *outs)


def solution(mesh):
    placed = (
        P("scene", None, None, "rows"),
        P("scene", "rows"),
        P("scene", "rows"),
        P(),
        P(),
        P(),
        P(),
        P(),
        P(),
        P("rows", None),
        P("rows", None),
        P(None, "rows", None),
        P(),
        P("rows", "scene", None, None),
    )
    return jax.shard_map(
        body,
        mesh=mesh,
        in_specs=placed,
        out_specs=(
            P("rows", "scene", None, None),
            P(),
            P(),
            P(),
            P(),
            P(),
            P(),
            P(),
            P(),
            P("rows", None),
            P(None, "rows", None),
            P("rows", None),
            P("rows", None),
        ),
        check_vma=False,
    )
```

```python
import functools

import jax
import jax.numpy as jnp
from jax import lax
from jax.experimental import pallas as pl
from jax.experimental.pallas import tpu as pltpu
from jax.sharding import PartitionSpec as P

beta_one = 0.9
beta_two = 0.999
adam_eps = 1e-08
decay_rate = 0.01
average_keep = 0.99
norm_eps = 1e-05
rate_points = 0.3
rate_norms = 0.2
rate_kernel = 0.04

EDGE = 48
BIG = 1e30
PACK = 8
TILE = 256
LANES = 128
f32 = jnp.float32
bf16 = jnp.bfloat16


def iota(shape, dim):
    return lax.broadcasted_iota(jnp.int32, shape, dim)


def dot_nn(a, b):
    return lax.dot_general(a, b, (((1,), (0,)), ((), ())), preferred_element_type=f32)


def dot_nt(a, b):
    return lax.dot_general(a, b, (((1,), (1,)), ((), ())), preferred_element_type=f32)


def dot_tn(a, b):
    return lax.dot_general(a, b, (((0,), (0,)), ((), ())), preferred_element_type=f32)


def split3(x):
    a = x.astype(bf16)
    r = x - a.astype(f32)
    b = r.astype(bf16)
    c = (r - b.astype(f32)).astype(bf16)
    return a, b, c


def exact_left(x, y):
    a, b, c = split3(x)
    return dot_nn(a, y) + (dot_nn(b, y) + dot_nn(c, y))


def exact_right(x, y):
    a, b, c = split3(y)
    return dot_nn(x, a) + (dot_nn(x, b) + dot_nn(x, c))


def swap_halves(x):
    return pltpu.roll(x, x.shape[1] // 2, axis=1)


def twice(row):
    return jnp.concatenate([row, row], axis=1)


def one_hot_rows(rows, cols):
    return (iota((rows, cols), 0) // PACK == iota((rows, cols), 1)).astype(f32).astype(bf16)


def one_hot_cols(rows, cols):
    return (iota((rows, cols), 1) // PACK == iota((rows, cols), 0)).astype(f32).astype(bf16)


def lift_table(weight, norm, table):
    feats, channels = weight.shape
    rows = table.shape[0]
    gain = norm[0:1, :].astype(f32)
    sign = jnp.where(gain > 0, 1.0, jnp.where(gain < 0, -1.0, 0.0))
    signed = weight[...].astype(f32) * sign
    full = jnp.concatenate([signed, jnp.zeros((1, channels), f32), jnp.ones((1, channels), f32)], axis=0)
    full = jnp.concatenate([full, jnp.zeros((16 - feats - 2, channels), f32)], axis=0)
    base = dot_nn(one_hot_rows(rows, 16), twice(full).astype(bf16))
    slot = iota(base.shape, 0) % PACK
    half = iota(base.shape, 1) // channels
    for m in range(PACK // 2):
        table[:, m * LANES : (m + 1) * LANES] = jnp.where(slot == 2 * m + half, base, 0.0).astype(bf16)


def lift_inputs(pts, count, part):
    feats, _, size = pts.shape
    live = (iota((PACK, size), 0) + part * PACK < count).astype(f32)
    kept = (pts.astype(f32) * live[None]).reshape(feats * PACK, size)
    return jnp.concatenate([kept, live, (live - 1.0) * BIG], axis=0).astype(bf16)


def copy_in(source, target, sems, s):
    return pltpu.make_async_copy(source.at[s], target.at[s], sems.at[s])


def half_store(block, s, scenes, value):
    channels = LANES // 2
    spot = pl.ds(pl.multiple_of((s % (scenes // 2)) * EDGE, 8), EDGE)
    lower = iota((EDGE, LANES), 1) < channels
    block[spot, :] = jnp.where(lower == (s < scenes // 2), value, block[spot, :])


def lift_body(
    mine, points, counts, pixels, weight, norm, kernel, z_out, winner_out, edge, payload, moments,
    table, gram, wide, pts, z, low, high, winner, sems,
):
    feats, channels = weight.shape
    scenes, _, depth, size = points.shape
    rows = (feats + 1) * PACK
    for s in range(scenes):
        copy_in(points, pts, sems.at[0], s).start()
    lift_table(weight, norm, table)
    gram[...] = jnp.zeros_like(gram)
    edge[...] = jnp.zeros_like(edge)

    def scene(s, _):
        copy_in(points, pts, sems.at[0], s).wait()
        count = counts[pl.ds(s, 1), :]
        total = None
        for part in range(depth // PACK):
            xin = lift_inputs(pts[s, :, part * PACK : (part + 1) * PACK, :], count, part)
            prod = dot_nt(xin[:rows], xin[:rows])
            total = prod if total is None else total + prod
            for t in range(size // TILE):
                at = slice(t * TILE, (t + 1) * TILE)
                turned = jnp.transpose(xin[:, at])
                for q in range(PACK // 4):
                    l = dot_nn(turned, table[:, q * 256 : (q + 1) * 256])
                    one, two = l[:, :LANES], l[:, LANES:]
                    n_one, n_two = float(part * PACK + q * 4), float(part * PACK + q * 4 + 2)
                    m = jnp.maximum(one, two)
                    first = jnp.where(two > one, n_two, n_one)
                    last = jnp.where(two >= one, n_two, n_one)
                    if part > 0 or q > 0:
                        old = z[s, at, :]
                        first = jnp.where(m > old, first, low[at, :])
                        last = jnp.where(m >= old, last, high[at, :])
                        m = jnp.maximum(old, m)
                    if part == depth // PACK - 1 and q == PACK // 4 - 1:
                        upper = (iota((TILE, LANES), 1) >= channels).astype(f32)
                        first, last = first + upper, last + upper
                        other = swap_halves(m)
                        first = jnp.where(other > m, swap_halves(first), first)
                        last = jnp.where(other >= m, swap_halves(last), last)
                        m = jnp.maximum(m, other)
                        only = jnp.where(first == last, first, -1.0)
                        winner[s, at, :] = jnp.where(m > -0.5 * BIG, only, 99.0)
                    else:
                        low[at, :] = first
                        high[at, :] = last
                    z[s, at, :] = m
        gram[...] += total
        copy_in(z, z_out, sems.at[1], s).start()
        copy_in(winner, winner_out, sems.at[2], s).start()
        half_store(edge, s, scenes, z[s, :EDGE, :])
        return 0

    lax.fori_loop(0, scenes, scene, 0)

    count_rows = edge.shape[0] - 2 * scenes
    edge[count_rows : count_rows + scenes, :] = pixels[:, :LANES].astype(f32)
    edge[count_rows + scenes :, :] = jnp.ones((scenes, LANES), f32)
    g = gram[...]
    g = jnp.where(iota(g.shape, 0) % PACK == iota(g.shape, 1) % PACK, g, 0.0)
    y = exact_left(g, one_hot_rows(rows, LANES))
    m = exact_right(one_hot_cols(16, rows), y)
    moments[...] = m
    w = jnp.concatenate([weight[...].astype(f32), jnp.zeros((16 - feats, channels), f32)], axis=0)
    aw = exact_left(m[:, :16], w.astype(bf16))
    two = jnp.sum(aw * w, axis=0, keepdims=True)
    one = aw[feats : feats + 1]
    own = kernel.shape[1]
    flat = jnp.concatenate([kernel[...].astype(f32), jnp.zeros((channels, LANES - own), f32)], axis=1)
    wide[...] = jnp.transpose(jnp.concatenate([flat, jnp.zeros((LANES - channels, LANES), f32)], axis=0))
    pieces = [one, two, m[feats : feats + 1]]
    share = (payload.shape[2] - 256) // channels
    for j in range(share):
        pieces.append(wide[pl.ds(mine[0, 0] * share + j, 1), :channels])
    row = jnp.concatenate(pieces, axis=1)
    payload[...] = jnp.broadcast_to(row[:, None, :], payload.shape)
    for s in range(scenes):
        copy_in(z, z_out, sems.at[1], s).wait()
        copy_in(winner, winner_out, sems.at[2], s).wait()


def vmem(count):
    return [pl.BlockSpec(memory_space=pltpu.VMEM)] * count


def smem(count):
    return [pl.BlockSpec(memory_space=pltpu.SMEM)] * count


def hbm(count):
    return [pl.BlockSpec(memory_space=pltpu.HBM)] * count


def lift(mine, points, counts, pixels, weight, norm, kernel, peers, share):
    scenes, feats, depth, size = points.shape
    channels = weight.shape[1]
    full = (feats + 2) * PACK
    rows = (feats + 1) * PACK
    edge_rows = scenes // 2 * EDGE + 2 * scenes
    return pl.pallas_call(
        lift_body,
        in_specs=smem(1) + hbm(1) + vmem(5),
        out_specs=hbm(2) + vmem(3),
        out_shape=[
            jax.ShapeDtypeStruct((scenes, size, LANES), f32),
            jax.ShapeDtypeStruct((scenes, size, LANES), f32),
            jax.ShapeDtypeStruct((edge_rows, LANES), f32),
            jax.ShapeDtypeStruct((peers, 1, 256 + share), f32),
            jax.ShapeDtypeStruct((16, LANES), f32),
        ],
        scratch_shapes=[
            pltpu.VMEM((full, PACK * channels), bf16),
            pltpu.VMEM((rows, rows), f32),
            pltpu.VMEM((LANES, LANES), f32),
            pltpu.VMEM(points.shape, bf16),
            pltpu.VMEM((scenes, size, LANES), f32),
            pltpu.VMEM((size, LANES), f32),
            pltpu.VMEM((size, LANES), f32),
            pltpu.VMEM((scenes, size, LANES), f32),
            pltpu.SemaphoreType.DMA((3, scenes)),
        ],
        name="lift",
    )(mine, points, counts, pixels, weight, norm, kernel)


def gather_kernel(got, kern, devices, parts):
    channels = kern.shape[1]
    share = kern.shape[0] // devices // parts
    peers = got.shape[0]
    for j in range(share):
        rows = got[:, 0, 256 + j * channels : 256 + (j + 1) * channels]
        if parts > 1:
            kern[pl.ds(j, peers, stride=share), :] = rows
        else:
            for r in range(devices):
                at = r * (peers // devices)
                kern[r * share + j : r * share + j + 1, :] = rows[at : at + 1]


def tap(kern, a, b):
    channels = kern.shape[1]
    if a is None or b is None:
        return jnp.zeros((channels, channels), f32)
    return kern[(3 * a + b) * channels : (3 * a + b + 1) * channels, :]


def edge_rows_of(block, s, scenes, lower):
    spot = pl.ds(pl.multiple_of((s % (scenes // 2)) * EDGE, 8), EDGE)
    rows = jnp.where(lower == (s < scenes // 2), block[spot, :], 0.0)
    return rows + swap_halves(rows)


def conv_body(
    devices, parts, pix, far_pix, got, z_in, edge, norm, conv_out, pooled_out, sums, kernel,
    params, source, kern, taps, grid_a, grid_b, side, acc, z, conv, pooled, sems,
):
    scenes, size, _ = z.shape
    for s in range(scenes):
        copy_in(z_in, z, sems.at[0], s).start()
    channels = norm.shape[1]
    _, pairs, out_cols, _ = conv.shape
    cols = 2 * out_cols
    last_row = (4 * pairs - 1) * cols
    tot = jnp.sum(got[:, :, :256], axis=0)
    count = tot[:, 2 * channels + 9 : 2 * channels + 10]
    mean = tot[:, :channels] / count
    inv = lax.rsqrt(tot[:, channels : 2 * channels] / count - mean * mean + norm_eps)
    nw = norm[...].astype(f32)
    gain = nw[0:1]
    sign = jnp.where(gain > 0, 1.0, jnp.where(gain < 0, -1.0, 0.0))
    params[0:1] = twice(mean)
    params[1:2] = twice(inv)
    params[2:3] = twice(gain)
    params[3:4] = twice(nw[1:2])
    params[4:5] = twice(sign)
    gather_kernel(got, kern, devices, parts)
    kernel[...] = kern[...].astype(bf16)
    for w, (low, high) in enumerate(((0, None), (1, None), (2, 0), (None, 1), (None, 2))):
        none = tap(kern, None, None)
        top = jnp.concatenate([tap(kern, low, 1), tap(kern, high, 1), none, none], axis=1)
        end = jnp.concatenate([tap(kern, low, 2), tap(kern, high, 2), tap(kern, low, 0), tap(kern, high, 0)], axis=1)
        taps[w] = jnp.concatenate([top, end], axis=0).astype(bf16)
    grid_a[...] = jnp.zeros_like(grid_a)
    side[...] = jnp.zeros_like(side)
    acc[...] = jnp.zeros_like(acc)

    def pool(x, ok):
        pre = params[2:3] * ((x * params[4:5] - params[0:1]) * params[1:2]) + params[3:4]
        return jnp.where(ok, jnp.maximum(pre, 0.0), 0.0).astype(bf16)

    own_at = 8 + cols
    far_at = 8 - last_row
    some = size // pairs

    def part_of(j):
        return pl.ds(j * some if isinstance(j, int) else pl.multiple_of(j * some, 16), some)

    def fill(s, j):
        zs = z[s, part_of(j), :]
        own = pool(zs, zs > -0.5 * BIG)
        pooled[s, part_of(j), :] = own
        source[part_of(j), :] = own.astype(f32)

    def fill_far(dst, s):
        far = edge_rows_of(edge, s, scenes, iota((EDGE, LANES), 1) < channels)
        flag = edge[edge.shape[0] - scenes : edge.shape[0] - scenes + 1, :]
        far = pool(far, (far > -0.5 * BIG) & (flag > 0.5))
        pooled[s, size:] = jnp.concatenate([far, jnp.zeros((LANES - EDGE, LANES), bf16)], axis=0)
        source[size : size + EDGE] = far.astype(f32)
        for p in range(EDGE):
            at = jnp.maximum(far_pix[s, p], last_row) + far_at
            dst[pl.ds(at, 1), :] = source[size + p : size + p + 1, :]

    def place(dst, s, j):
        rows = dst.at[pl.ds(own_at, 4 * pairs * cols), :]
        line = pix.at[s * pairs + j]
        values = source.at[part_of(j), :]
        for p in range(some):
            rows[pl.ds(line[0, p], 1), :] = values[p : p + 1, :]

    left = iota((out_cols, LANES), 1) < channels

    def convolve_pair(src, s, j):
        out = None
        for w in range(5):
            base = 8 + (4 * j + w) * cols
            even = src[pl.ds(base, out_cols, stride=2), :]
            odd = src[pl.ds(base + 1, out_cols, stride=2), :]
            part = dot_nn(jnp.where(left, even, odd).astype(bf16), taps[w])
            out = part if out is None else out + part
        side[8:, :] = out[:, LANES:]
        value = out[:, :LANES] + side[7 : 7 + out_cols, :]
        conv[s, j] = value
        acc[0:8] += jnp.sum(value.reshape(out_cols // 8, 8, LANES), axis=0)
        acc[8:16] += jnp.sum((value * value).reshape(out_cols // 8, 8, LANES), axis=0)
        used = (5 if j == pairs - 1 else 4) * cols
        base = 8 + 4 * j * cols
        src[base : base + used, :] = jnp.zeros((used, LANES), f32)

    copy_in(z_in, z, sems.at[0], 0).wait()
    fill_far(grid_a, 0)
    grid_b[:8, :] = jnp.zeros((8, LANES), f32)
    grid_b[8 + 4 * pairs * cols :, :] = jnp.zeros((grid_b.shape[0] - 8 - 4 * pairs * cols, LANES), f32)

    def start(j, _):
        grid_b[pl.ds(pl.multiple_of(8 + 4 * j * cols, 8), 4 * cols), :] = jnp.zeros((4 * cols, LANES), f32)
        fill(0, j)
        place(grid_a, 0, j)
        return 0

    lax.fori_loop(0, pairs, start, 0)

    def two_scenes(i, _):
        for k, (src, dst) in enumerate(((grid_a, grid_b), (grid_b, grid_a))):
            s = 2 * i + k
            ahead = jnp.minimum(s + 1, scenes - 1)

            @pl.when(s + 1 < scenes)
            def _():
                copy_in(z_in, z, sems.at[0], s + 1).wait()

            fill_far(dst, ahead)
            for j in range(pairs):
                fill(ahead, j)
                place(dst, ahead, j)
                convolve_pair(src, s, j)

            copy_in(conv, conv_out, sems.at[1], s).start()
            copy_in(pooled, pooled_out, sems.at[2], s).start()
        return 0

    lax.fori_loop(0, scenes // 2, two_scenes, 0)
    for s in range(scenes):
        copy_in(conv, conv_out, sems.at[1], s).wait()
        copy_in(pooled, pooled_out, sems.at[2], s).wait()
    sums[...] = jnp.broadcast_to(both_sums(acc, channels), sums.shape)


def both_sums(acc, channels):
    one = jnp.sum(acc[0:8], axis=0, keepdims=True)
    two = jnp.sum(acc[8:16], axis=0, keepdims=True)
    one = one + swap_halves(one)
    two = two + swap_halves(two)
    return jnp.where(iota((1, LANES), 1) < channels, one, two)


def convolve(devices, parts, pix, far_pix, got, z, edge, norm, pairs, out_cols):
    scenes, size, _ = z.shape
    peers = got.shape[0]
    channels = norm.shape[1]
    cells = 8 + (4 * pairs + 1) * 2 * out_cols + 8
    return pl.pallas_call(
        functools.partial(conv_body, devices, parts),
        in_specs=smem(2) + vmem(1) + hbm(1) + vmem(2),
        out_specs=hbm(2) + vmem(2),
        out_shape=[
            jax.ShapeDtypeStruct((scenes, pairs, out_cols, LANES), f32),
            jax.ShapeDtypeStruct((scenes, size + LANES, LANES), bf16),
            jax.ShapeDtypeStruct((peers, LANES), f32),
            jax.ShapeDtypeStruct((9 * channels, channels), bf16),
        ],
        scratch_shapes=[
            pltpu.VMEM((8, LANES), f32),
            pltpu.VMEM((size + LANES, LANES), f32),
            pltpu.VMEM((9 * channels, channels), f32),
            pltpu.VMEM((5, LANES, 2 * LANES), bf16),
            pltpu.VMEM((cells, LANES), f32),
            pltpu.VMEM((cells, LANES), f32),
            pltpu.VMEM((out_cols + 8, LANES), f32),
            pltpu.VMEM((16, LANES), f32),
            pltpu.VMEM((scenes, size, LANES), f32),
            pltpu.VMEM((scenes, pairs, out_cols, LANES), f32),
            pltpu.VMEM((scenes, size + LANES, LANES), bf16),
            pltpu.SemaphoreType.DMA((3, scenes)),
        ],
        name="convolve",
    )(pix, far_pix, got, z, edge, norm)


def split_sums(stats, channels):
    tot = jnp.sum(stats[...], axis=0)
    lower = iota((1, LANES), 1) < channels
    turned = swap_halves(tot)
    return jnp.where(lower, tot, turned), jnp.where(lower, turned, tot)


def conv_params(cells, stats, norm):
    one, two = split_sums(stats, norm.shape[1])
    mean = one / cells
    inv = lax.rsqrt(two / cells - mean * mean + norm_eps)
    nw = norm[...].astype(f32)
    return mean, inv, twice(nw[2:3]), twice(nw[3:4])


def turned_pair(block, j, k):
    _, _, channels, cols = block.shape
    return jnp.transpose(block[2 * j : 2 * j + 2, k].reshape(2 * channels, cols)).astype(f32)


def scene_copy(source, target, sems, s):
    return pltpu.make_async_copy(source.at[:, s], target.at[:, s], sems.at[s])


def norm_body(cells, stats, conv_in, cot_in, norm, result_out, sums, acc, conv, cot, result, sems):
    channels = norm.shape[1]
    scenes, pairs, out_cols, _ = conv.shape
    for s in range(scenes):
        copy_in(conv_in, conv, sems.at[0], s).start()
        scene_copy(cot_in, cot, sems.at[1], s).start()
    mean, inv, gain, bias = conv_params(cells, stats, norm)
    acc[...] = jnp.zeros_like(acc)

    def scene(k, _):
        copy_in(conv_in, conv, sems.at[0], k).wait()
        scene_copy(cot_in, cot, sems.at[1], k).wait()
        for j in range(pairs):
            xhat = (conv[k, j] - mean) * inv
            pre = gain * xhat + bias
            out = jnp.transpose(jnp.maximum(pre, 0.0).astype(bf16))
            result[2 * j : 2 * j + 2, k] = out.reshape(2, channels, out_cols)
            back = jnp.where(pre > 0, turned_pair(cot, j, k), 0.0)
            acc[0:8] += jnp.sum(back.reshape(out_cols // 8, 8, LANES), axis=0)
            acc[8:16] += jnp.sum((back * xhat).reshape(out_cols // 8, 8, LANES), axis=0)
        scene_copy(result, result_out, sems.at[2], k).start()
        return 0

    lax.fori_loop(0, scenes, scene, 0)
    sums[...] = jnp.broadcast_to(both_sums(acc, channels), sums.shape)
    for s in range(scenes):
        scene_copy(result, result_out, sems.at[2], s).wait()


def normalize(cells, stats, conv, cot, norm):
    peers = stats.shape[0]
    scenes = conv.shape[0]
    return pl.pallas_call(
        functools.partial(norm_body, cells),
        in_specs=vmem(1) + hbm(2) + vmem(1),
        out_specs=hbm(1) + vmem(1),
        out_shape=[
            jax.ShapeDtypeStruct(cot.shape, bf16),
            jax.ShapeDtypeStruct((peers, LANES), f32),
        ],
        scratch_shapes=[
            pltpu.VMEM((16, LANES), f32),
            pltpu.VMEM(conv.shape, f32),
            pltpu.VMEM(cot.shape, bf16),
            pltpu.VMEM(cot.shape, bf16),
            pltpu.SemaphoreType.DMA((3, scenes)),
        ],
        name="normalize",
    )(stats, conv, cot, norm)


def grad_body(
    cells, devices, parts, idx, stats, sums, conv_in, cot_in, norm, pooled_in, phase, kernel, slots_out, edge, far, kgrad,
    taps, field_a, field_b, taken_a, taken_b, turn, column_a, column_b, acc, rows_k, conv, cot, pooled, slots_a, slots_b, exact_a, exact_b, sems,
):
    scenes, pairs, out_cols, _ = conv.shape
    channels = norm.shape[1]
    size = slots_a.shape[0]
    strip = out_cols + 8
    some = idx.shape[2]
    columns, slots, exact = (column_a, column_b), (slots_a, slots_b), (exact_a, exact_b)
    for s in range(scenes):
        copy_in(conv_in, conv, sems.at[0], s).start()
        scene_copy(cot_in, cot, sems.at[1], s).start()
        copy_in(pooled_in, pooled, sems.at[2], s).start()
    for hp in range(2):
        for up in range(2):
            line = []
            for dw in range(2):
                for dr in range(2):
                    a = ((1, None), (2, 0))[hp][dr]
                    b = ((1, None), (2, 0))[up][dw]
                    if a is None or b is None:
                        line.append(jnp.zeros((channels, channels), f32))
                    else:
                        at = (3 * a + b) * channels
                        line.append(kernel[at : at + channels, :].astype(f32))
            ph = 2 * hp + up
            taps[ph * channels : (ph + 1) * channels, :] = jnp.concatenate(line, axis=1).astype(bf16)
    for block in (field_a, field_b, taken_a, taken_b, acc):
        block[...] = jnp.zeros_like(block)

    def phases(column, s, j):
        chunks = column.shape[0] // LANES
        for c in range(j * chunks // pairs, (j + 1) * chunks // pairs):
            row = phase[s, :, c * LANES : (c + 1) * LANES]
            column[c * LANES : (c + 1) * LANES, :] = jnp.transpose(jnp.broadcast_to(row, (LANES, LANES)))

    mean, inv, gain, bias = conv_params(cells, stats, norm)
    bias_grad, gain_grad = split_sums(sums, channels)
    scale = gain * inv / cells
    left = iota((out_cols, LANES), 1) < channels
    half = (iota((some, LANES), 1) >= channels).astype(f32)

    def field(dst, s, j):
        xhat = (conv[s, j] - mean) * inv
        pre = gain * xhat + bias
        both = cot[2 * j : 2 * j + 2, s].reshape(2 * channels, out_cols)
        back = jnp.where(pre > 0, jnp.transpose(both).astype(f32), 0.0)
        grad = scale * (cells * back - bias_grad - xhat * gain_grad)
        grad = grad.astype(bf16).astype(f32)
        turned = swap_halves(grad)
        base = 2 * j * strip
        dst[base : base + out_cols, :] = jnp.where(left, turn[...], turned)
        dst[base + strip : base + strip + out_cols, :] = grad
        turn[...] = turned

    def take(dst, src, s, j):
        line = idx.at[s * pairs + j]
        for p in range(some):
            dst[2 * p : 2 * p + 2, :] = src[pl.ds(line[0, p], 2), :]

    def product(src, k, s, j):
        at = slice(j * some, (j + 1) * some)
        part = jnp.concatenate([src[pl.ds(0, some, stride=2), :], src[pl.ds(1, some, stride=2), :]], axis=1).astype(bf16)
        out = dot_nt(part, taps[...])
        ph = columns[k][at, :]
        is_even = ph == half
        is_odd = ph == half + 2.0
        value = jnp.where(is_even, out[:, :LANES], 0.0) + jnp.where(is_odd, out[:, LANES:], 0.0)
        value = value + swap_halves(value)
        pf = pooled[s, at, :].astype(f32)
        value = jnp.where(pf > 0, value, 0.0)
        exact[k][at, :] = value
        slots[k][at, :] = value.astype(bf16)
        split = jnp.concatenate([jnp.where(is_even, pf, 0.0), jnp.where(is_odd, pf, 0.0)], axis=1)
        acc[...] += dot_tn(split.astype(bf16), part)

    def copy_out(k, s):
        return pltpu.make_async_copy(slots[k], slots_out.at[s], sems.at[3, k])

    def done(k, s):
        half_store(edge, s, scenes, exact[k][:EDGE, :])
        half_store(far, s, scenes, exact[k][size - LANES : size - LANES + EDGE, :])
        slots[k][:EDGE, :] = jnp.zeros((EDGE, LANES), bf16)
        copy_out(k, s).start()

    def walk(dst, src, k, s):
        before = jnp.clip(s - 1, 0, scenes - 1)
        held = jnp.where(s > 0, s - 1, scenes)
        older = jnp.where(s > 1, s - 2, scenes)
        if dst is not None:
            copy_in(conv_in, conv, sems.at[0], s).wait()
            scene_copy(cot_in, cot, sems.at[1], s).wait()
            turn[...] = jnp.zeros_like(turn)

        @pl.when(s > 0)
        def _():
            copy_in(pooled_in, pooled, sems.at[2], before).wait()


        @pl.when(s >= 3)
        def _():
            copy_out(1 - k, s - 3).wait()

        for j in range(pairs):
            to, of = ((taken_a, taken_b), (taken_b, taken_a))[j % 2]
            if dst is not None:
                phases(columns[k], s, j)
                field(dst, s, j)
            take(to, src, before, j)
            product(of, k if j == 0 else 1 - k, held if j > 0 else older, (j - 1) % pairs)

        @pl.when(s >= 2)
        def _():
            done(k, s - 2)

        if dst is not None:
            dst[2 * pairs * strip : 2 * pairs * strip + out_cols, :] = jnp.where(left, turn[...], 0.0)

    def two_scenes(i, _):
        walk(field_a, field_b, 0, 2 * i)
        walk(field_b, field_a, 1, 2 * i + 1)
        return 0

    far[...] = jnp.zeros_like(far)
    edge[...] = jnp.zeros_like(edge)
    for block in (column_a, column_b):
        block[...] = jnp.zeros_like(block)
    pooled[scenes] = jnp.zeros_like(pooled[scenes])
    lax.fori_loop(0, scenes // 2, two_scenes, 0)
    walk(None, field_b, 0, scenes)
    product(taken_b, 1, scenes - 1, pairs - 1)
    done(1, scenes - 1)
    for a in range(3):
        for b in range(3):
            hp, dr = ((1, 1), (0, 0), (1, 0))[a]
            up, dw = ((1, 1), (0, 0), (1, 0))[b]
            row, col = hp * 2 + up, dw * 2 + dr
            at = (3 * a + b) * channels
            rows_k[at : at + channels, :] = acc[
                row * channels : (row + 1) * channels, col * channels : (col + 1) * channels
            ]
    own = rows_k.shape[0] // devices
    share = own // parts
    for q in range(parts):
        for j in range(share):
            lanes = slice(j * channels, (j + 1) * channels)
            kgrad[q * devices : (q + 1) * devices, lanes] = rows_k[pl.ds(q * share + j, devices, stride=own), :]
    copy_out(0, scenes - 2).wait()
    copy_out(1, scenes - 1).wait()


def gradients(cells, devices, parts, idx, stats, sums, conv, cot, norm, pooled, phase, kernel):
    scenes, pairs, out_cols, _ = conv.shape
    channels = norm.shape[1]
    rows = pooled.shape[1]
    return pl.pallas_call(
        functools.partial(grad_body, cells, devices, parts),
        in_specs=smem(1) + vmem(2) + hbm(2) + vmem(1) + hbm(1) + vmem(2),
        out_specs=hbm(1) + vmem(3),
        out_shape=[
            jax.ShapeDtypeStruct((scenes, rows, LANES), bf16),
            jax.ShapeDtypeStruct((scenes // 2 * EDGE, LANES), f32),
            jax.ShapeDtypeStruct((scenes // 2 * EDGE, LANES), f32),
            jax.ShapeDtypeStruct((parts * devices, 9 * channels * channels // devices // parts), f32),
        ],
        scratch_shapes=[
            pltpu.VMEM((4 * channels, 4 * channels), bf16),
            pltpu.VMEM(((2 * pairs + 1) * (out_cols + 8), LANES), f32),
            pltpu.VMEM(((2 * pairs + 1) * (out_cols + 8), LANES), f32),
            pltpu.VMEM((2 * idx.shape[2], LANES), f32),
            pltpu.VMEM((2 * idx.shape[2], LANES), f32),
            pltpu.VMEM((out_cols, LANES), f32),
            pltpu.VMEM((rows, LANES), f32),
            pltpu.VMEM((rows, LANES), f32),
            pltpu.VMEM((4 * channels, 4 * channels), f32),
            pltpu.VMEM((9 * channels, channels), f32),
            pltpu.VMEM(conv.shape, f32),
            pltpu.VMEM(cot.shape, bf16),
            pltpu.VMEM((scenes + 1, rows, LANES), bf16),
            pltpu.VMEM((rows, LANES), bf16),
            pltpu.VMEM((rows, LANES), bf16),
            pltpu.VMEM((rows, LANES), f32),
            pltpu.VMEM((rows, LANES), f32),
            pltpu.SemaphoreType.DMA((4, scenes)),
        ],
        name="gradients",
    )(idx, stats, sums, conv, cot, norm, pooled, phase, kernel)


def fold(q, prod, channels):
    shape = (prod.shape[0], LANES)
    slot = iota(shape, 0) % PACK - 4 * q
    upper = (iota(shape, 1) >= channels).astype(jnp.int32)
    return jnp.where(slot == upper, prod[:, :LANES], 0.0) + jnp.where(slot == upper + 2, prod[:, LANES:], 0.0)


def single_winners(pts, who, grad, channels):
    size = who.shape[0]
    who = who - (iota((size, LANES), 1) >= channels).astype(f32)
    total = None
    for part, x in enumerate(pts):
        for q in range(PACK // 4):
            n = part * PACK + q * 4
            one = jnp.where(who == float(n), grad, 0.0)
            two = jnp.where(who == float(n + 2), grad, 0.0)
            prod = fold(q, dot_nn(x, jnp.concatenate([one, two], axis=1).astype(bf16)), channels)
            total = prod if total is None else total + prod
    return total


def shared_winners(pts, count, table, best, grad, mult, acc, depth, channels):
    feats = pts.shape[0]

    def lifted(part, q):
        xin = lift_inputs(pts[:, part * PACK : (part + 1) * PACK, :], count, part)
        l = dot_nn(jnp.transpose(xin), table[:, q * 256 : (q + 1) * 256])
        return xin, l[:, :LANES] == best[...], l[:, LANES:] == best[...]

    mult[...] = jnp.zeros_like(mult)
    for part in range(depth // PACK):
        for q in range(PACK // 4):
            _, one, two = lifted(part, q)
            mult[...] += jnp.where(one, 1.0, 0.0) + jnp.where(two, 1.0, 0.0)
    many = jnp.maximum(mult[...] + swap_halves(mult[...]), 1.0)
    mult[...] = grad / many
    for part in range(depth // PACK):
        for q in range(PACK // 4):
            xin, one, two = lifted(part, q)
            value = jnp.concatenate([jnp.where(one, mult[...], 0.0), jnp.where(two, mult[...], 0.0)], axis=1)
            acc[...] += fold(q, exact_right(xin[: feats * PACK], value), channels)


def unlift_body(
    points, counts, weight, norm, z, winner_in, slots_in, acc, bias, table, pts, winner, slots, best, mult, sems
):
    feats, channels = weight.shape
    scenes, _, depth, size = points.shape
    rows = feats * PACK
    tiles = size // TILE
    for s in range(scenes):
        copy_in(points, pts, sems.at[0], s).start()
        copy_in(winner_in, winner, sems.at[1], s).start()
        copy_in(slots_in, slots, sems.at[2], s).start()
    lift_table(weight, norm, table)
    acc[...] = jnp.zeros_like(acc)
    bias[...] = jnp.zeros_like(bias)

    def scene(s, _):
        copy_in(points, pts, sems.at[0], s).wait()
        copy_in(winner_in, winner, sems.at[1], s).wait()
        copy_in(slots_in, slots, sems.at[2], s).wait()
        total = None
        sums = None
        for t in range(tiles):
            at = slice(t * TILE, (t + 1) * TILE)
            grad = slots[s, at, :].astype(f32)
            one = jnp.sum(grad.reshape(TILE // 8, 8, LANES), axis=0)
            sums = one if sums is None else sums + one
            x = [pts[s, :, part * PACK : (part + 1) * PACK, at].reshape(rows, TILE) for part in range(depth // PACK)]
            one = single_winners(x, winner[s, at, :], grad, channels)
            total = one if total is None else total + one
        acc[...] += total
        bias[...] += sums

        @pl.when(jnp.min(winner[s]) < 0.0)
        def _():
            def tile(t, _):
                at = pl.ds(pl.multiple_of(t * TILE, TILE), TILE)

                @pl.when(jnp.min(winner[s, at, :]) < 0.0)
                def _():
                    fetch = pltpu.make_async_copy(z.at[s, at], best, sems.at[0, 0])
                    fetch.start()
                    fetch.wait()
                    best[...] = jnp.where(winner[s, at, :] < 0.0, best[...], BIG)
                    grad = slots[s, at, :].astype(f32)
                    count = counts[pl.ds(s, 1), at]
                    shared_winners(pts.at[s, :, :, at], count, table, best, grad, mult, acc, depth, channels)

                return 0

            lax.fori_loop(0, tiles, tile, 0)

        return 0

    lax.fori_loop(0, scenes, scene, 0)


def unlift(points, counts, weight, norm, z, winner, slots):
    scenes, feats, depth, size = points.shape
    channels = weight.shape[1]
    full = (feats + 2) * PACK
    return pl.pallas_call(
        unlift_body,
        in_specs=hbm(1) + vmem(3) + hbm(3),
        out_specs=vmem(2),
        out_shape=[
            jax.ShapeDtypeStruct((feats * PACK, LANES), f32),
            jax.ShapeDtypeStruct((8, LANES), f32),
        ],
        scratch_shapes=[
            pltpu.VMEM((full, PACK * channels), bf16),
            pltpu.VMEM(points.shape, bf16),
            pltpu.VMEM((scenes, size, LANES), f32),
            pltpu.VMEM(slots.shape, bf16),
            pltpu.VMEM((TILE, LANES), f32),
            pltpu.VMEM((TILE, LANES), f32),
            pltpu.SemaphoreType.DMA((3, scenes)),
        ],
        cost_estimate=pl.CostEstimate(flops=40_000_000_000, bytes_accessed=16_000_000, transcendentals=0),
        name="unlift",
    )(points, counts, weight, norm, z, winner, slots)


def edges_body(
    devices, parts, pts, counts, weight, norm, z, winner, edge, far, moments, inner, inner_bias, kgrad, payload,
    table, acc, bias, best, mult, sem,
):
    feats, channels = weight.shape
    scenes, _, depth, _ = pts.shape
    rows = feats * PACK
    size = pts.shape[3]
    lift_table(weight, norm, table)
    acc[...] = inner[...]
    bias[...] = inner_bias[...]
    peers = payload.shape[0]
    share = kgrad.shape[1]
    for r in range(devices):
        row = kgrad[r : r + 1, :]
        for q in range(1, parts):
            row = row + kgrad[q * devices + r : q * devices + r + 1, :]
        each = peers // devices
        payload[r * each : (r + 1) * each, :, :share] = jnp.broadcast_to(row[:, None, :], (each, 1, share))

    def scene(s, _):
        lower = iota((EDGE, LANES), 1) < channels
        whole = edge_rows_of(edge, s, scenes, lower) + edge_rows_of(far, s, scenes, lower)
        whole = whole.astype(bf16).astype(f32)
        grad = jnp.concatenate([whole, jnp.zeros((size - EDGE, LANES), f32)], axis=0)
        bias[...] += jnp.sum(whole.reshape(EDGE // 8, 8, LANES), axis=0)
        x = [pts[s, :, part * PACK : (part + 1) * PACK, :].reshape(rows, size) for part in range(depth // PACK)]
        acc[...] += single_winners(x, winner[s], grad, channels)

        @pl.when(jnp.min(winner[s, :EDGE, :]) < 0.0)
        def _():
            fetch = pltpu.make_async_copy(z.at[s, :size], best, sem)
            fetch.start()
            fetch.wait()
            best[...] = jnp.where(winner[s] < 0.0, best[...], BIG)
            count = counts[pl.ds(s, 1), :][:, :size]
            shared_winners(pts.at[s], count, table, best, grad, mult, acc, depth, channels)

        return 0

    lax.fori_loop(0, scenes, scene, 0)
    out = exact_right(one_hot_cols(16, rows), acc[...])
    out = out + swap_halves(out)
    pieces = [out[i : i + 1, :channels] for i in range(feats)]
    pieces.append(jnp.sum(bias[...], axis=0, keepdims=True)[:, :channels])
    pieces += [moments[i : i + 1, :16] for i in range(feats + 1)]
    width = (feats + 1) * (channels + 16)
    pieces.append(jnp.zeros((1, payload.shape[2] - share - width), f32))
    row = jnp.concatenate(pieces, axis=1)
    payload[:, :, share:] = jnp.broadcast_to(row[:, None, :], (peers, 1, row.shape[1]))


def unlift_edges(devices, parts, peers, points, counts, weight, norm, z, winner, edge, far, moments, inner, bias, kgrad):
    scenes, feats, depth, _ = points.shape
    channels = weight.shape[1]
    full = (feats + 2) * PACK
    width = -(-(feats + 1) * (channels + 16) // LANES) * LANES
    return pl.pallas_call(
        functools.partial(edges_body, devices, parts),
        grid=(1,),
        in_specs=[
            pl.BlockSpec((scenes, feats, depth, LANES), lambda i: (0, 0, 0, 0)),
            pl.BlockSpec(counts.shape, lambda i: (0, 0)),
            pl.BlockSpec(weight.shape, lambda i: (0, 0)),
            pl.BlockSpec(norm.shape, lambda i: (0, 0)),
            pl.BlockSpec(memory_space=pltpu.HBM),
            pl.BlockSpec((scenes, LANES, LANES), lambda i: (0, 0, 0)),
        ]
        + [pl.BlockSpec(x.shape, lambda i: (0, 0)) for x in (edge, far, moments, inner, bias, kgrad)],
        out_specs=pl.BlockSpec((peers, 1, kgrad.shape[1] + width), lambda i: (0, 0, 0)),
        out_shape=jax.ShapeDtypeStruct((peers, 1, kgrad.shape[1] + width), f32),
        scratch_shapes=[
            pltpu.VMEM((full, PACK * channels), bf16),
            pltpu.VMEM((feats * PACK, LANES), f32),
            pltpu.VMEM((8, LANES), f32),
            pltpu.VMEM((LANES, LANES), f32),
            pltpu.VMEM((LANES, LANES), f32),
            pltpu.SemaphoreType.DMA,
        ],
        name="edges",
    )(points, counts, weight, norm, z, winner, edge, far, moments, inner, bias, kgrad)


def adam(fixes, w, states, grad, rate):
    moment = beta_one * states[0] + (1.0 - beta_one) * grad
    second = beta_two * states[1] + (1.0 - beta_two) * grad * grad
    new = w - rate * (moment / fixes[0] / (jnp.sqrt(second / fixes[1]) + adam_eps) + decay_rate * w)
    return new, moment, second, average_keep * states[2] + (1.0 - average_keep) * new


def step_body(devices, parts, fix, got, sums, weight, norm, pm, ps, nm, ns, km, ks, *refs):
    p_new, p_states, p_avg, p_copy, n_new, n_states, n_avg, n_copy, k_new, k_states, k_avg, k_copy, kgrad = refs
    feats, channels = weight.shape
    own = km.shape[1]
    share = own // parts
    peers = got.shape[0]
    scenes = peers // devices
    fixes = (fix[0], fix[1])

    width = share * channels
    kgrad[...] = jnp.zeros_like(kgrad)
    for q in range(parts):
        tot = got[q, :, :width]
        for r in range(1, devices):
            tot = tot + got[r * scenes + q, :, :width]
        for j in range(share):
            kgrad[q * share + j : q * share + j + 1, :channels] = tot[:, j * channels : (j + 1) * channels]
    grad = jnp.transpose(kgrad[...])[:channels, :own]
    new, moment, second, average = adam(fixes, km[...], (ks[0], ks[1], ks[2]), grad, rate_kernel)
    k_new[...] = new
    k_states[0] = moment
    k_states[1] = second
    k_avg[...] = average
    k_copy[...] = new.astype(bf16)

    row = jnp.sum(got[:, :, width:], axis=0)
    cross = jnp.concatenate([row[:, i * channels : (i + 1) * channels] for i in range(feats + 1)], axis=0)
    base = (feats + 1) * channels
    moments = jnp.concatenate([row[:, base + i * 16 : base + (i + 1) * 16] for i in range(feats + 1)], axis=0)
    w = weight[...].astype(f32)
    nw = norm[...].astype(f32)
    total = moments[feats : feats + 1, feats : feats + 1]
    firsts = moments[:feats, feats : feats + 1]
    mixed = None
    first_sum = None
    for i in range(feats):
        part = moments[:feats, i : i + 1] * w[i : i + 1]
        mixed = part if mixed is None else mixed + part
        part = moments[feats : feats + 1, i : i + 1] * w[i : i + 1]
        first_sum = part if first_sum is None else first_sum + part
    mean = first_sum / total
    inv = lax.rsqrt(jnp.sum(mixed * w, axis=0, keepdims=True) / total - mean * mean + norm_eps)
    bias_p = cross[feats : feats + 1]
    gain_p = inv * (jnp.sum(w * cross[:feats], axis=0, keepdims=True) - mean * bias_p)
    spread = inv * (mixed - firsts * mean)
    point_grad = (nw[0:1] * inv) * (cross[:feats] - (firsts * bias_p + spread * gain_p) / total)
    states = (ps[:, 0, :], ps[:, 1, :], ps[:, 2, :])
    new, moment, second, average = adam(fixes, pm[...], states, point_grad, rate_points)
    p_new[...] = new
    p_states[:, 0, :] = moment
    p_states[:, 1, :] = second
    p_avg[...] = average
    p_copy[...] = new.astype(bf16)

    both = jnp.sum(sums[...], axis=0)
    norm_grad = jnp.concatenate([gain_p, bias_p, both[:, channels:], both[:, :channels]], axis=0)
    new, moment, second, average = adam(fixes, nm[...], (ns[0], ns[1], ns[2]), norm_grad, rate_norms)
    n_new[...] = new
    n_states[0] = moment
    n_states[1] = second
    n_avg[...] = average
    n_copy[...] = new.astype(bf16)


def update(devices, parts, fix, got, sums, weight, norm, pm, ps, nm, ns, km, ks):
    feats, channels = weight.shape
    shapes = []
    for m, states in ((pm, (feats, 2, channels)), (nm, (2,) + nm.shape), (km, (2,) + km.shape)):
        shapes.append(jax.ShapeDtypeStruct(m.shape, f32))
        shapes.append(jax.ShapeDtypeStruct(states, f32))
        shapes.append(jax.ShapeDtypeStruct(m.shape, f32))
        shapes.append(jax.ShapeDtypeStruct(m.shape, bf16))
    return pl.pallas_call(
        functools.partial(step_body, devices, parts),
        in_specs=smem(1) + vmem(10),
        out_specs=vmem(12),
        out_shape=shapes,
        scratch_shapes=[pltpu.VMEM((LANES, LANES), f32)],
        name="update",
    )(fix, got, sums, weight, norm, pm, ps, nm, ns, km, ks)


def shifted(x, by):
    length = lax.axis_size("rows")
    pairs = [(i, i + by) for i in range(length) if 0 <= i + by < length]
    return lax.ppermute(x, "rows", pairs)


def exchange(x):
    return lax.all_to_all(x, ("rows", "scene"), 0, 0, tiled=True)


def body(
    points,
    pillar_counts,
    pillar_pixels,
    point_weight,
    point_master,
    point_states,
    norm_weight,
    norm_master,
    norm_states,
    kernel_weight,
    kernel_master,
    kernel_states,
    step_count,
    cotangent,
):
    size = points.shape[3]
    out_rows, scenes, channels, out_cols = cotangent.shape
    cols = 2 * out_cols
    devices = lax.axis_size("rows")
    scene_devices = lax.axis_size("scene")
    peers = devices * scene_devices
    cells = float(out_rows * scenes * out_cols * peers)
    own = kernel_weight.shape[0]
    parts = scene_devices if own % scene_devices == 0 else 1
    share = own // parts * channels
    mine = lax.axis_index("scene") if parts > 1 else jnp.int32(0)

    z, winner, edge, stats, moments = lift(
        mine.reshape(1, 1), points, pillar_counts, pillar_pixels, point_weight, norm_weight, kernel_weight.T, peers, share
    )
    edge = shifted(edge, 1)
    got = exchange(stats)
    held = scenes // 2 * EDGE
    far_pixels = edge[held : held + scenes].astype(jnp.int32)
    pairs = out_rows // 2
    own_pixels = pillar_pixels.reshape(scenes * pairs, 1, size // pairs)
    conv, pooled, sums, kernel = convolve(
        devices, parts, own_pixels, far_pixels, got, z, edge, norm_weight, pairs, out_cols
    )
    conv_stats = exchange(sums[:, None])

    far_pixels = far_pixels[:, :EDGE]
    at = (pillar_pixels % cols) // 2
    own_at = (pillar_pixels // (2 * cols) + 1) * (out_cols + 8) + at
    take_at = jnp.concatenate([own_at, (far_pixels % cols) // 2], axis=1)
    take_at = jnp.pad(take_at, ((0, 0), (0, -(size + EDGE) % (16 * pairs))))
    take_at = take_at.reshape(scenes * pairs, 1, take_at.shape[1] // pairs)
    own_phase = (pillar_pixels // cols % 2) * 2 + pillar_pixels % 2
    phase = jnp.concatenate([own_phase, 2 + far_pixels % 2], axis=1)
    phase = jnp.pad(phase, ((0, 0), (0, LANES - EDGE))).astype(f32)[:, None]

    result, sums = normalize(cells, conv_stats, conv, cotangent, norm_weight)
    grad_sums = exchange(sums[:, None])
    slots, own_edge, far, kgrad = gradients(
        cells, devices, parts, take_at, conv_stats, grad_sums, conv, cotangent, norm_weight, pooled, phase, kernel
    )
    far = shifted(far, -1)
    if parts > 1:
        kgrad = lax.all_to_all(kgrad, "scene", 0, 0, tiled=True)
    else:
        kgrad = lax.psum(kgrad, "scene")
    inner, bias = unlift(points, pillar_counts, point_weight, norm_weight, z, winner, slots)
    far, kgrad, inner, bias = lax.optimization_barrier((far, kgrad, inner, bias))
    payload = unlift_edges(
        devices, parts, peers, points, pillar_counts, point_weight, norm_weight, z, winner, own_edge, far, moments, inner, bias, kgrad
    )
    got = exchange(payload)
    steps_done = step_count[0].astype(f32)
    fix = jnp.stack([1.0 - beta_one**steps_done, 1.0 - beta_two**steps_done])
    outs = update(
        devices,
        parts,
        fix,
        got,
        grad_sums,
        point_weight,
        norm_weight,
        point_master,
        jnp.transpose(point_states, (1, 0, 2)),
        norm_master,
        norm_states,
        kernel_master.T,
        jnp.transpose(kernel_states, (0, 2, 1)),
    )
    outs = list(outs)
    outs[1] = jnp.transpose(outs[1], (1, 0, 2))
    outs[8], outs[10], outs[11] = outs[8].T, outs[10].T, outs[11].T
    outs[9] = jnp.transpose(outs[9], (0, 2, 1))
    return (result, *outs)


def solution(mesh):
    placed = (
        P("scene", None, None, "rows"),
        P("scene", "rows"),
        P("scene", "rows"),
        P(),
        P(),
        P(),
        P(),
        P(),
        P(),
        P("rows", None),
        P("rows", None),
        P(None, "rows", None),
        P(),
        P("rows", "scene", None, None),
    )
    return jax.shard_map(
        body,
        mesh=mesh,
        in_specs=placed,
        out_specs=(
            P("rows", "scene", None, None),
            P(),
            P(),
            P(),
            P(),
            P(),
            P(),
            P(),
            P(),
            P("rows", None),
            P(None, "rows", None),
            P("rows", None),
            P("rows", None),
        ),
        check_vma=False,
    )
```

```python
import functools

import jax
import jax.numpy as jnp
from jax import lax
from jax.experimental import pallas as pl
from jax.experimental.pallas import tpu as pltpu
from jax.sharding import PartitionSpec as P

beta_one = 0.9
beta_two = 0.999
adam_eps = 1e-08
decay_rate = 0.01
average_keep = 0.99
norm_eps = 1e-05
rate_points = 0.3
rate_norms = 0.2
rate_kernel = 0.04

EDGE = 48
BIG = 1e30
PACK = 8
ROWS = 128
TILE = 256
LANES = 128
f32 = jnp.float32
bf16 = jnp.bfloat16


def iota(shape, dim):
    return lax.broadcasted_iota(jnp.int32, shape, dim)


def dot_nn(a, b):
    return lax.dot_general(a, b, (((1,), (0,)), ((), ())), preferred_element_type=f32)


def dot_nt(a, b):
    return lax.dot_general(a, b, (((1,), (1,)), ((), ())), preferred_element_type=f32)


def dot_tn(a, b):
    return lax.dot_general(a, b, (((0,), (0,)), ((), ())), preferred_element_type=f32)


def split3(x):
    a = x.astype(bf16)
    r = x - a.astype(f32)
    b = r.astype(bf16)
    c = (r - b.astype(f32)).astype(bf16)
    return a, b, c


def exact_left(x, y):
    a, b, c = split3(x)
    return dot_nn(a, y) + (dot_nn(b, y) + dot_nn(c, y))


def exact_right(x, y):
    a, b, c = split3(y)
    return dot_nn(x, a) + (dot_nn(x, b) + dot_nn(x, c))


def swap_halves(x):
    return pltpu.roll(x, x.shape[1] // 2, axis=1)


def twice(row):
    return jnp.concatenate([row, row], axis=1)


def one_hot_rows(rows, cols):
    return (iota((rows, cols), 0) // PACK == iota((rows, cols), 1)).astype(f32).astype(bf16)


def one_hot_cols(rows, cols):
    return (iota((rows, cols), 1) // PACK == iota((rows, cols), 0)).astype(f32).astype(bf16)


def lift_table(weight, norm, table):
    feats, channels = weight.shape
    rows = table.shape[0]
    gain = norm[0:1, :].astype(f32)
    sign = jnp.where(gain > 0, 1.0, jnp.where(gain < 0, -1.0, 0.0))
    signed = weight[...].astype(f32) * sign
    full = jnp.concatenate([signed, jnp.zeros((1, channels), f32), jnp.ones((1, channels), f32)], axis=0)
    full = jnp.concatenate([full, jnp.zeros((16 - feats - 2, channels), f32)], axis=0)
    base = dot_nn(one_hot_rows(rows, 16), twice(full).astype(bf16))
    slot = iota(base.shape, 0) % PACK
    half = iota(base.shape, 1) // channels
    for m in range(PACK // 2):
        table[:, m * LANES : (m + 1) * LANES] = jnp.where(slot == 2 * m + half, base, 0.0).astype(bf16)


def lift_inputs(pts, count, part):
    feats, _, size = pts.shape
    live = (iota((PACK, size), 0) + part * PACK < count).astype(f32)
    low = live.astype(bf16)
    dead = ((live - 1.0) * BIG).astype(bf16)
    full = jnp.concatenate([pts.reshape(feats * PACK, size), low, dead], axis=0)
    kept = jnp.concatenate([(pts * low[None]).reshape(feats * PACK, size), low], axis=0)
    return full, kept


def copy_in(source, target, sems, s):
    return pltpu.make_async_copy(source.at[s], target.at[s], sems.at[s])


def half_store(block, s, scenes, value):
    channels = LANES // 2
    spot = pl.ds(pl.multiple_of((s % (scenes // 2)) * EDGE, 8), EDGE)
    lower = iota((EDGE, LANES), 1) < channels
    block[spot, :] = jnp.where(lower == (s < scenes // 2), value, block[spot, :])


def lift_body(
    mine, points, counts, pixels, weight, norm, kernel, z_out, winner_out, edge, payload, moments,
    table, gram, wide, pts, z, winner, sems,
):
    feats, channels = weight.shape
    scenes, _, depth, size = points.shape
    rows = (feats + 1) * PACK
    for s in range(scenes):
        copy_in(points, pts, sems.at[0], s).start()
    lift_table(weight, norm, table)
    gram[...] = jnp.zeros_like(gram)
    edge[...] = jnp.zeros_like(edge)

    def scene(s, _):
        copy_in(points, pts, sems.at[0], s).wait()
        count = counts[pl.ds(s, 1), :]
        total = None
        inputs = []
        for part in range(depth // PACK):
            xin, kept = lift_inputs(pts[s, :, part * PACK : (part + 1) * PACK, :], count, part)
            prod = dot_nt(kept, xin[:rows])
            total = prod if total is None else total + prod
            inputs.append(xin)
        for t in range(size // LANES):
            turned = [jnp.transpose(x[:, t * LANES : (t + 1) * LANES]) for x in inputs]
            for h in range(LANES // ROWS):
                best = None
                for part in range(depth // PACK):
                    lhs = turned[part][h * ROWS : (h + 1) * ROWS]
                    for q in range(PACK // 4):
                        l = dot_nn(lhs, table[:, q * 256 : (q + 1) * 256])
                        one, two = l[:, :LANES], l[:, LANES:]
                        n_one, n_two = float(part * PACK + q * 4), float(part * PACK + q * 4 + 2)
                        m = jnp.maximum(one, two)
                        low = jnp.where(two > one, n_two, n_one)
                        high = jnp.where(two >= one, n_two, n_one)
                        if best is None:
                            best, first, last = m, low, high
                        else:
                            first = jnp.where(m > best, low, first)
                            last = jnp.where(m >= best, high, last)
                            best = jnp.maximum(best, m)
                at = slice(t * LANES + h * ROWS, t * LANES + (h + 1) * ROWS)
                upper = (iota((ROWS, LANES), 1) >= channels).astype(f32)
                first, last = first + upper, last + upper
                other = swap_halves(best)
                first = jnp.where(other > best, swap_halves(first), first)
                last = jnp.where(other >= best, swap_halves(last), last)
                best = jnp.maximum(best, other)
                only = jnp.where(first == last, first, -1.0)
                winner[s, at, :] = jnp.where(best > -0.5 * BIG, only, 99.0).astype(bf16)
                z[s, at, :] = best
        gram[...] += total
        copy_in(z, z_out, sems.at[1], s).start()
        copy_in(winner, winner_out, sems.at[2], s).start()
        half_store(edge, s, scenes, z[s, :EDGE, :])
        return 0

    lax.fori_loop(0, scenes, scene, 0)

    count_rows = edge.shape[0] - 2 * scenes
    edge[count_rows : count_rows + scenes, :] = pixels[:, :LANES].astype(f32)
    edge[count_rows + scenes :, :] = jnp.ones((scenes, LANES), f32)
    g = gram[...]
    g = jnp.where(iota(g.shape, 0) % PACK == iota(g.shape, 1) % PACK, g, 0.0)
    y = exact_left(g, one_hot_rows(rows, LANES))
    m = exact_right(one_hot_cols(16, rows), y)
    moments[...] = m
    w = jnp.concatenate([weight[...].astype(f32), jnp.zeros((16 - feats, channels), f32)], axis=0)
    aw = exact_left(m[:, :16], w.astype(bf16))
    two = jnp.sum(aw * w, axis=0, keepdims=True)
    one = aw[feats : feats + 1]
    own = kernel.shape[1]
    flat = jnp.concatenate([kernel[...].astype(f32), jnp.zeros((channels, LANES - own), f32)], axis=1)
    wide[...] = jnp.transpose(jnp.concatenate([flat, jnp.zeros((LANES - channels, LANES), f32)], axis=0))
    pieces = [one, two, m[feats : feats + 1]]
    share = (payload.shape[2] - 256) // channels
    for j in range(share):
        pieces.append(wide[pl.ds(mine[0, 0] * share + j, 1), :channels])
    row = jnp.concatenate(pieces, axis=1)
    payload[...] = jnp.broadcast_to(row[:, None, :], payload.shape)
    for s in range(scenes):
        copy_in(z, z_out, sems.at[1], s).wait()
        copy_in(winner, winner_out, sems.at[2], s).wait()


def vmem(count):
    return [pl.BlockSpec(memory_space=pltpu.VMEM)] * count


def smem(count):
    return [pl.BlockSpec(memory_space=pltpu.SMEM)] * count


def hbm(count):
    return [pl.BlockSpec(memory_space=pltpu.HBM)] * count


def lift(mine, points, counts, pixels, weight, norm, kernel, peers, share):
    scenes, feats, depth, size = points.shape
    channels = weight.shape[1]
    full = (feats + 2) * PACK
    rows = (feats + 1) * PACK
    edge_rows = scenes // 2 * EDGE + 2 * scenes
    return pl.pallas_call(
        lift_body,
        in_specs=smem(1) + hbm(1) + vmem(5),
        out_specs=hbm(2) + vmem(3),
        out_shape=[
            jax.ShapeDtypeStruct((scenes, size, LANES), f32),
            jax.ShapeDtypeStruct((scenes, size, LANES), bf16),
            jax.ShapeDtypeStruct((edge_rows, LANES), f32),
            jax.ShapeDtypeStruct((peers, 1, 256 + share), f32),
            jax.ShapeDtypeStruct((16, LANES), f32),
        ],
        scratch_shapes=[
            pltpu.VMEM((full, PACK * channels), bf16),
            pltpu.VMEM((rows, rows), f32),
            pltpu.VMEM((LANES, LANES), f32),
            pltpu.VMEM(points.shape, bf16),
            pltpu.VMEM((scenes, size, LANES), f32),
            pltpu.VMEM((scenes, size, LANES), bf16),
            pltpu.SemaphoreType.DMA((3, scenes)),
        ],
        name="lift",
    )(mine, points, counts, pixels, weight, norm, kernel)


def gather_kernel(got, kern, devices, parts):
    channels = kern.shape[1]
    share = kern.shape[0] // devices // parts
    peers = got.shape[0]
    for j in range(share):
        rows = got[:, 0, 256 + j * channels : 256 + (j + 1) * channels]
        if parts > 1:
            kern[pl.ds(j, peers, stride=share), :] = rows
        else:
            for r in range(devices):
                at = r * (peers // devices)
                kern[r * share + j : r * share + j + 1, :] = rows[at : at + 1]


def tap(kern, a, b):
    channels = kern.shape[1]
    if a is None or b is None:
        return jnp.zeros((channels, channels), f32)
    return kern[(3 * a + b) * channels : (3 * a + b + 1) * channels, :]


def edge_rows_of(block, s, scenes, lower):
    base = (s % (scenes // 2)) * EDGE
    spot = pl.ds(base if isinstance(base, int) else pl.multiple_of(base, 8), EDGE)
    rows = jnp.where(lower == (s < scenes // 2), block[spot, :], 0.0)
    return rows + swap_halves(rows)


def conv_body(
    devices, parts, pix, far_pix, got, z_in, edge, norm, conv_out, pooled_out, sums, kernel,
    params, source, kern, taps, grid_a, grid_b, side, acc, z, conv, pooled, sems,
):
    scenes, size, _ = z.shape
    for s in range(scenes):
        copy_in(z_in, z, sems.at[0], s).start()
    channels = norm.shape[1]
    _, pairs, out_cols, _ = conv.shape
    cols = 2 * out_cols
    last_row = (4 * pairs - 1) * cols
    tot = jnp.sum(got[:, :, :256], axis=0)
    count = tot[:, 2 * channels + 9 : 2 * channels + 10]
    mean = tot[:, :channels] / count
    inv = lax.rsqrt(tot[:, channels : 2 * channels] / count - mean * mean + norm_eps)
    nw = norm[...].astype(f32)
    gain = nw[0:1]
    sign = jnp.where(gain > 0, 1.0, jnp.where(gain < 0, -1.0, 0.0))
    params[0:1] = twice(mean)
    params[1:2] = twice(inv)
    params[2:3] = twice(gain)
    params[3:4] = twice(nw[1:2])
    params[4:5] = twice(sign)
    gather_kernel(got, kern, devices, parts)
    kernel[...] = kern[...].astype(bf16)
    for w, (low, high) in enumerate(((0, None), (1, None), (2, 0), (None, 1), (None, 2))):
        none = tap(kern, None, None)
        top = jnp.concatenate([tap(kern, low, 1), tap(kern, high, 1), none, none], axis=1)
        end = jnp.concatenate([tap(kern, low, 2), tap(kern, high, 2), tap(kern, low, 0), tap(kern, high, 0)], axis=1)
        taps[w] = jnp.concatenate([top, end], axis=0).astype(bf16)
    grid_a[...] = jnp.zeros_like(grid_a)
    side[...] = jnp.zeros_like(side)
    acc[...] = jnp.zeros_like(acc)

    def pool(x, ok):
        pre = params[2:3] * ((x * params[4:5] - params[0:1]) * params[1:2]) + params[3:4]
        return jnp.where(ok, jnp.maximum(pre, 0.0), 0.0).astype(bf16)

    own_at = 8 + cols
    far_at = 8 - last_row
    some = size // pairs

    def part_of(j):
        return pl.ds(j * some if isinstance(j, int) else pl.multiple_of(j * some, 16), some)

    def fill(s, j):
        zs = z[s, part_of(j), :]
        own = pool(zs, zs > -0.5 * BIG)
        pooled[s, part_of(j), :] = own
        source[part_of(j), :] = own.astype(f32)

    def fill_far(dst, s):
        far = edge_rows_of(edge, s, scenes, iota((EDGE, LANES), 1) < channels)
        flag = edge[edge.shape[0] - scenes : edge.shape[0] - scenes + 1, :]
        far = pool(far, (far > -0.5 * BIG) & (flag > 0.5))
        pooled[s, size:] = jnp.concatenate([far, jnp.zeros((LANES - EDGE, LANES), bf16)], axis=0)
        source[size : size + EDGE] = far.astype(f32)
        for p in range(EDGE):
            at = jnp.maximum(far_pix[s, p], last_row) + far_at
            dst[pl.ds(at, 1), :] = source[size + p : size + p + 1, :]

    def place(dst, s, j):
        rows = dst.at[pl.ds(own_at, 4 * pairs * cols), :]
        line = pix.at[s * pairs + j]
        values = source.at[part_of(j), :]
        for p in range(some):
            rows[pl.ds(line[0, p], 1), :] = values[p : p + 1, :]

    left = iota((out_cols, LANES), 1) < channels

    def convolve_pair(src, s, j):
        out = None
        for w in range(5):
            base = 8 + (4 * j + w) * cols
            even = src[pl.ds(base, out_cols, stride=2), :]
            odd = src[pl.ds(base + 1, out_cols, stride=2), :]
            part = dot_nn(jnp.where(left, even, odd).astype(bf16), taps[w])
            out = part if out is None else out + part
        side[8:, :] = out[:, LANES:]
        value = out[:, :LANES] + side[7 : 7 + out_cols, :]
        conv[s, j] = value
        acc[0:8] += jnp.sum(value.reshape(out_cols // 8, 8, LANES), axis=0)
        acc[8:16] += jnp.sum((value * value).reshape(out_cols // 8, 8, LANES), axis=0)
        used = (5 if j == pairs - 1 else 4) * cols
        base = 8 + 4 * j * cols
        src[base : base + used, :] = jnp.zeros((used, LANES), f32)

    copy_in(z_in, z, sems.at[0], 0).wait()
    fill_far(grid_a, 0)
    grid_b[:8, :] = jnp.zeros((8, LANES), f32)
    grid_b[8 + 4 * pairs * cols :, :] = jnp.zeros((grid_b.shape[0] - 8 - 4 * pairs * cols, LANES), f32)

    def start(j, _):
        grid_b[pl.ds(pl.multiple_of(8 + 4 * j * cols, 8), 4 * cols), :] = jnp.zeros((4 * cols, LANES), f32)
        fill(0, j)
        place(grid_a, 0, j)
        return 0

    lax.fori_loop(0, pairs, start, 0)

    def two_scenes(i, _):
        for k, (src, dst) in enumerate(((grid_a, grid_b), (grid_b, grid_a))):
            s = 2 * i + k
            ahead = jnp.minimum(s + 1, scenes - 1)

            @pl.when(s + 1 < scenes)
            def _():
                copy_in(z_in, z, sems.at[0], s + 1).wait()

            fill_far(dst, ahead)
            for j in range(pairs):
                fill(ahead, j)
                place(dst, ahead, j)
                convolve_pair(src, s, j)

            copy_in(conv, conv_out, sems.at[1], s).start()
            copy_in(pooled, pooled_out, sems.at[2], s).start()
        return 0

    lax.fori_loop(0, scenes // 2, two_scenes, 0)
    for s in range(scenes):
        copy_in(conv, conv_out, sems.at[1], s).wait()
        copy_in(pooled, pooled_out, sems.at[2], s).wait()
    sums[...] = jnp.broadcast_to(both_sums(acc, channels), sums.shape)


def both_sums(acc, channels):
    one = jnp.sum(acc[0:8], axis=0, keepdims=True)
    two = jnp.sum(acc[8:16], axis=0, keepdims=True)
    one = one + swap_halves(one)
    two = two + swap_halves(two)
    return jnp.where(iota((1, LANES), 1) < channels, one, two)


def convolve(devices, parts, pix, far_pix, got, z, edge, norm, pairs, out_cols):
    scenes, size, _ = z.shape
    peers = got.shape[0]
    channels = norm.shape[1]
    cells = 8 + (4 * pairs + 1) * 2 * out_cols + 8
    return pl.pallas_call(
        functools.partial(conv_body, devices, parts),
        in_specs=smem(2) + vmem(1) + hbm(1) + vmem(2),
        out_specs=hbm(2) + vmem(2),
        out_shape=[
            jax.ShapeDtypeStruct((scenes, pairs, out_cols, LANES), f32),
            jax.ShapeDtypeStruct((scenes, size + LANES, LANES), bf16),
            jax.ShapeDtypeStruct((peers, LANES), f32),
            jax.ShapeDtypeStruct((9 * channels, channels), bf16),
        ],
        scratch_shapes=[
            pltpu.VMEM((8, LANES), f32),
            pltpu.VMEM((size + LANES, LANES), f32),
            pltpu.VMEM((9 * channels, channels), f32),
            pltpu.VMEM((5, LANES, 2 * LANES), bf16),
            pltpu.VMEM((cells, LANES), f32),
            pltpu.VMEM((cells, LANES), f32),
            pltpu.VMEM((out_cols + 8, LANES), f32),
            pltpu.VMEM((16, LANES), f32),
            pltpu.VMEM((scenes, size, LANES), f32),
            pltpu.VMEM((scenes, pairs, out_cols, LANES), f32),
            pltpu.VMEM((scenes, size + LANES, LANES), bf16),
            pltpu.SemaphoreType.DMA((3, scenes)),
        ],
        name="convolve",
    )(pix, far_pix, got, z, edge, norm)


def split_sums(stats, channels):
    tot = jnp.sum(stats[...], axis=0)
    lower = iota((1, LANES), 1) < channels
    turned = swap_halves(tot)
    return jnp.where(lower, tot, turned), jnp.where(lower, turned, tot)


def conv_params(cells, stats, norm):
    one, two = split_sums(stats, norm.shape[1])
    mean = one / cells
    inv = lax.rsqrt(two / cells - mean * mean + norm_eps)
    nw = norm[...].astype(f32)
    return mean, inv, twice(nw[2:3]), twice(nw[3:4])


def turned_pair(block, j, k):
    _, _, channels, cols = block.shape
    return jnp.transpose(block[2 * j : 2 * j + 2, k].reshape(2 * channels, cols)).astype(f32)


def scene_copy(source, target, sems, s):
    return pltpu.make_async_copy(source.at[:, s], target.at[:, s], sems.at[s])


def norm_body(cells, stats, conv_in, cot_in, norm, result_out, sums, acc, conv, cot, result, sems):
    channels = norm.shape[1]
    scenes, pairs, out_cols, _ = conv.shape
    for s in range(scenes):
        copy_in(conv_in, conv, sems.at[0], s).start()
        scene_copy(cot_in, cot, sems.at[1], s).start()
    mean, inv, gain, bias = conv_params(cells, stats, norm)
    acc[...] = jnp.zeros_like(acc)

    def scene(k, _):
        copy_in(conv_in, conv, sems.at[0], k).wait()
        scene_copy(cot_in, cot, sems.at[1], k).wait()
        for j in range(pairs):
            xhat = (conv[k, j] - mean) * inv
            pre = gain * xhat + bias
            out = jnp.transpose(jnp.maximum(pre, 0.0).astype(bf16))
            result[2 * j : 2 * j + 2, k] = out.reshape(2, channels, out_cols)
            back = jnp.where(pre > 0, turned_pair(cot, j, k), 0.0)
            acc[0:8] += jnp.sum(back.reshape(out_cols // 8, 8, LANES), axis=0)
            acc[8:16] += jnp.sum((back * xhat).reshape(out_cols // 8, 8, LANES), axis=0)
        scene_copy(result, result_out, sems.at[2], k).start()
        return 0

    lax.fori_loop(0, scenes, scene, 0)
    sums[...] = jnp.broadcast_to(both_sums(acc, channels), sums.shape)
    for s in range(scenes):
        scene_copy(result, result_out, sems.at[2], s).wait()


def normalize(cells, stats, conv, cot, norm):
    peers = stats.shape[0]
    scenes = conv.shape[0]
    return pl.pallas_call(
        functools.partial(norm_body, cells),
        in_specs=vmem(1) + hbm(2) + vmem(1),
        out_specs=hbm(1) + vmem(1),
        out_shape=[
            jax.ShapeDtypeStruct(cot.shape, bf16),
            jax.ShapeDtypeStruct((peers, LANES), f32),
        ],
        scratch_shapes=[
            pltpu.VMEM((16, LANES), f32),
            pltpu.VMEM(conv.shape, f32),
            pltpu.VMEM(cot.shape, bf16),
            pltpu.VMEM(cot.shape, bf16),
            pltpu.SemaphoreType.DMA((3, scenes)),
        ],
        name="normalize",
    )(stats, conv, cot, norm)


def grad_body(
    cells, devices, parts, idx, stats, sums, conv_in, cot_in, norm, pooled_in, phase, kernel, slots_out, edge, far, kgrad,
    taps, field_a, field_b, taken_a, taken_b, turn, column_a, column_b, acc, rows_k, conv, cot, pooled, slots_a, slots_b, exact_a, exact_b, staged, sems,
):
    scenes, pairs, out_cols, _ = conv.shape
    channels = norm.shape[1]
    size = slots_a.shape[0]
    strip = out_cols + 8
    some = idx.shape[2]
    columns, slots, exact = (column_a, column_b), (slots_a, slots_b), (exact_a, exact_b)
    for s in range(scenes):
        copy_in(conv_in, conv, sems.at[0], s).start()
        scene_copy(cot_in, cot, sems.at[1], s).start()
        copy_in(pooled_in, pooled, sems.at[2], s).start()
    for hp in range(2):
        for up in range(2):
            line = []
            for dw in range(2):
                for dr in range(2):
                    a = ((1, None), (2, 0))[hp][dr]
                    b = ((1, None), (2, 0))[up][dw]
                    if a is None or b is None:
                        line.append(jnp.zeros((channels, channels), f32))
                    else:
                        at = (3 * a + b) * channels
                        line.append(kernel[at : at + channels, :].astype(f32))
            ph = 2 * hp + up
            taps[ph * channels : (ph + 1) * channels, :] = jnp.concatenate(line, axis=1).astype(bf16)
    for block in (field_a, field_b, taken_a, taken_b, acc):
        block[...] = jnp.zeros_like(block)

    def phases(column, s, j):
        chunks = column.shape[0] // LANES
        for c in range(j * chunks // pairs, (j + 1) * chunks // pairs):
            row = phase[s, :, c * LANES : (c + 1) * LANES]
            column[c * LANES : (c + 1) * LANES, :] = jnp.transpose(jnp.broadcast_to(row, (LANES, LANES)))

    mean, inv, gain, bias = conv_params(cells, stats, norm)
    bias_grad, gain_grad = split_sums(sums, channels)
    scale = gain * inv / cells
    left = iota((out_cols, LANES), 1) < channels
    half = (iota((some, LANES), 1) >= channels).astype(f32)

    def field(dst, s, j):
        xhat = (conv[s, j] - mean) * inv
        pre = gain * xhat + bias
        both = cot[2 * j : 2 * j + 2, s].reshape(2 * channels, out_cols)
        back = jnp.where(pre > 0, jnp.transpose(both).astype(f32), 0.0)
        grad = scale * (cells * back - bias_grad - xhat * gain_grad)
        grad = grad.astype(bf16).astype(f32)
        turned = swap_halves(grad)
        base = 2 * j * strip
        dst[base : base + out_cols, :] = jnp.where(left, turn[...], turned)
        dst[base + strip : base + strip + out_cols, :] = grad
        turn[...] = turned

    def take(dst, src, s, j):
        line = idx.at[s * pairs + j]
        for p in range(some):
            dst[2 * p : 2 * p + 2, :] = src[pl.ds(line[0, p], 2), :]

    def product(src, k, s, j):
        at = slice(j * some, (j + 1) * some)
        part = jnp.concatenate([src[pl.ds(0, some, stride=2), :], src[pl.ds(1, some, stride=2), :]], axis=1).astype(bf16)
        out = dot_nt(part, taps[...])
        ph = columns[k][at, :]
        is_even = ph == half
        is_odd = ph == half + 2.0
        value = jnp.where(is_even, out[:, :LANES], 0.0) + jnp.where(is_odd, out[:, LANES:], 0.0)
        value = value + swap_halves(value)
        pf = pooled[s, at, :].astype(f32)
        value = jnp.where(pf > 0, value, 0.0)
        exact[k][at, :] = value
        slots[k][at, :] = value.astype(bf16)
        split = jnp.concatenate([jnp.where(is_even, pf, 0.0), jnp.where(is_odd, pf, 0.0)], axis=1)
        acc[...] += dot_tn(split.astype(bf16), part)

    def copy_out(s):
        return copy_in(staged, slots_out, sems.at[3], s)

    def done(k, s):
        half_store(edge, s, scenes, exact[k][:EDGE, :])
        half_store(far, s, scenes, exact[k][size - LANES : size - LANES + EDGE, :])
        staged[s, :EDGE, :] = jnp.zeros((EDGE, LANES), bf16)
        staged[s, EDGE:, :] = slots[k][EDGE:, :]
        copy_out(s).start()

    def walk(dst, src, k, s):
        before = jnp.clip(s - 1, 0, scenes - 1)
        held = jnp.where(s > 0, s - 1, scenes)
        older = jnp.where(s > 1, s - 2, scenes)
        if dst is not None:
            copy_in(conv_in, conv, sems.at[0], s).wait()
            scene_copy(cot_in, cot, sems.at[1], s).wait()
            turn[...] = jnp.zeros_like(turn)

        @pl.when(s > 0)
        def _():
            copy_in(pooled_in, pooled, sems.at[2], before).wait()


        for j in range(pairs):
            to, of = ((taken_a, taken_b), (taken_b, taken_a))[j % 2]
            if dst is not None:
                phases(columns[k], s, j)
                field(dst, s, j)
            take(to, src, before, j)
            product(of, k if j == 0 else 1 - k, held if j > 0 else older, (j - 1) % pairs)

        @pl.when(s >= 2)
        def _():
            done(k, s - 2)

        if dst is not None:
            dst[2 * pairs * strip : 2 * pairs * strip + out_cols, :] = jnp.where(left, turn[...], 0.0)

    def two_scenes(i, _):
        walk(field_a, field_b, 0, 2 * i)
        walk(field_b, field_a, 1, 2 * i + 1)
        return 0

    far[...] = jnp.zeros_like(far)
    edge[...] = jnp.zeros_like(edge)
    for block in (column_a, column_b):
        block[...] = jnp.zeros_like(block)
    pooled[scenes] = jnp.zeros_like(pooled[scenes])
    lax.fori_loop(0, scenes // 2, two_scenes, 0)
    walk(None, field_b, 0, scenes)
    product(taken_b, 1, scenes - 1, pairs - 1)
    done(1, scenes - 1)
    for a in range(3):
        for b in range(3):
            hp, dr = ((1, 1), (0, 0), (1, 0))[a]
            up, dw = ((1, 1), (0, 0), (1, 0))[b]
            row, col = hp * 2 + up, dw * 2 + dr
            at = (3 * a + b) * channels
            rows_k[at : at + channels, :] = acc[
                row * channels : (row + 1) * channels, col * channels : (col + 1) * channels
            ]
    own = rows_k.shape[0] // devices
    share = own // parts
    for q in range(parts):
        for j in range(share):
            lanes = slice(j * channels, (j + 1) * channels)
            kgrad[q * devices : (q + 1) * devices, lanes] = rows_k[pl.ds(q * share + j, devices, stride=own), :]
    for s in range(scenes):
        copy_out(s).wait()


def gradients(cells, devices, parts, idx, stats, sums, conv, cot, norm, pooled, phase, kernel):
    scenes, pairs, out_cols, _ = conv.shape
    channels = norm.shape[1]
    rows = pooled.shape[1]
    return pl.pallas_call(
        functools.partial(grad_body, cells, devices, parts),
        in_specs=smem(1) + vmem(2) + hbm(2) + vmem(1) + hbm(1) + vmem(2),
        out_specs=hbm(1) + vmem(3),
        out_shape=[
            jax.ShapeDtypeStruct((scenes, rows, LANES), bf16),
            jax.ShapeDtypeStruct((scenes // 2 * EDGE, LANES), f32),
            jax.ShapeDtypeStruct((scenes // 2 * EDGE, LANES), f32),
            jax.ShapeDtypeStruct((parts * devices, 9 * channels * channels // devices // parts), f32),
        ],
        scratch_shapes=[
            pltpu.VMEM((4 * channels, 4 * channels), bf16),
            pltpu.VMEM(((2 * pairs + 1) * (out_cols + 8), LANES), f32),
            pltpu.VMEM(((2 * pairs + 1) * (out_cols + 8), LANES), f32),
            pltpu.VMEM((2 * idx.shape[2], LANES), f32),
            pltpu.VMEM((2 * idx.shape[2], LANES), f32),
            pltpu.VMEM((out_cols, LANES), f32),
            pltpu.VMEM((rows, LANES), f32),
            pltpu.VMEM((rows, LANES), f32),
            pltpu.VMEM((4 * channels, 4 * channels), f32),
            pltpu.VMEM((9 * channels, channels), f32),
            pltpu.VMEM(conv.shape, f32),
            pltpu.VMEM(cot.shape, bf16),
            pltpu.VMEM((scenes + 1, rows, LANES), bf16),
            pltpu.VMEM((rows, LANES), bf16),
            pltpu.VMEM((rows, LANES), bf16),
            pltpu.VMEM((rows, LANES), f32),
            pltpu.VMEM((rows, LANES), f32),
            pltpu.VMEM((scenes, rows, LANES), bf16),
            pltpu.SemaphoreType.DMA((4, scenes)),
        ],
        name="gradients",
    )(idx, stats, sums, conv, cot, norm, pooled, phase, kernel)


def fold(q, prod, channels):
    shape = (prod.shape[0], LANES)
    slot = iota(shape, 0) % PACK - 4 * q
    upper = (iota(shape, 1) >= channels).astype(jnp.int32)
    return jnp.where(slot == upper, prod[:, :LANES], 0.0) + jnp.where(slot == upper + 2, prod[:, LANES:], 0.0)


def single_winners(pts, who, grad, channels):
    size = who.shape[0]
    who = who.astype(f32) - (iota((size, LANES), 1) >= channels).astype(f32)
    total = None
    for part, x in enumerate(pts):
        for q in range(PACK // 4):
            n = part * PACK + q * 4
            one = jnp.where(who == float(n), grad, 0.0)
            two = jnp.where(who == float(n + 2), grad, 0.0)
            prod = fold(q, dot_nn(x, jnp.concatenate([one, two], axis=1).astype(bf16)), channels)
            total = prod if total is None else total + prod
    return total


def shared_winners(pts, count, table, best, grad, mult, acc, depth, channels):
    feats = pts.shape[0]

    def lifted(part, q):
        xin, _ = lift_inputs(pts[:, part * PACK : (part + 1) * PACK, :], count, part)
        l = dot_nn(jnp.transpose(xin), table[:, q * 256 : (q + 1) * 256])
        return xin, l[:, :LANES] == best[...], l[:, LANES:] == best[...]

    mult[...] = jnp.zeros_like(mult)
    for part in range(depth // PACK):
        for q in range(PACK // 4):
            _, one, two = lifted(part, q)
            mult[...] += jnp.where(one, 1.0, 0.0) + jnp.where(two, 1.0, 0.0)
    many = jnp.maximum(mult[...] + swap_halves(mult[...]), 1.0)
    mult[...] = grad / many
    for part in range(depth // PACK):
        for q in range(PACK // 4):
            xin, one, two = lifted(part, q)
            value = jnp.concatenate([jnp.where(one, mult[...], 0.0), jnp.where(two, mult[...], 0.0)], axis=1)
            acc[...] += fold(q, exact_right(xin[: feats * PACK], value), channels)


def unlift_body(
    points, counts_in, weight_in, norm_in, z, winner_in, slots_in, acc, bias,
    table, pts, winner, slots, best, mult, counts, weight, norm, sems,
):
    feats, channels = weight.shape
    scenes, _, depth, size = points.shape
    rows = feats * PACK
    tiles = size // TILE
    for s in range(scenes):
        copy_in(points, pts, sems.at[0], s).start()
        copy_in(winner_in, winner, sems.at[1], s).start()
        copy_in(slots_in, slots, sems.at[2], s).start()
    acc[...] = jnp.zeros_like(acc)
    bias[...] = jnp.zeros_like(bias)

    def scene(s, _):
        copy_in(points, pts, sems.at[0], s).wait()
        copy_in(winner_in, winner, sems.at[1], s).wait()
        copy_in(slots_in, slots, sems.at[2], s).wait()
        total = None
        sums = None
        for t in range(tiles):
            at = slice(t * TILE, (t + 1) * TILE)
            grad = slots[s, at, :].astype(f32)
            one = jnp.sum(grad.reshape(TILE // 8, 8, LANES), axis=0)
            sums = one if sums is None else sums + one
            x = [pts[s, :, part * PACK : (part + 1) * PACK, at].reshape(rows, TILE) for part in range(depth // PACK)]
            one = single_winners(x, winner[s, at, :], grad, channels)
            total = one if total is None else total + one
        acc[...] += total
        bias[...] += sums

        @pl.when(jnp.min(winner[s].astype(f32)) < 0.0)
        def _():
            for i, (of, to) in enumerate(((counts_in, counts), (weight_in, weight), (norm_in, norm))):
                fetch = pltpu.make_async_copy(of, to, sems.at[3, i])
                fetch.start()
                fetch.wait()
            lift_table(weight, norm, table)

            def tile(t, _):
                at = pl.ds(pl.multiple_of(t * LANES, LANES), LANES)

                @pl.when(jnp.min(winner[s, at, :].astype(f32)) < 0.0)
                def _():
                    fetch = pltpu.make_async_copy(z.at[s, at], best, sems.at[0, 0])
                    fetch.start()
                    fetch.wait()
                    best[...] = jnp.where(winner[s, at, :].astype(f32) < 0.0, best[...], BIG)
                    grad = slots[s, at, :].astype(f32)
                    count = counts[:, at]
                    count = jnp.sum(jnp.where(iota(count.shape, 0) == s, count, 0), axis=0, keepdims=True)
                    shared_winners(pts.at[s, :, :, at], count, table, best, grad, mult, acc, depth, channels)

                return 0

            lax.fori_loop(0, size // LANES, tile, 0)

        return 0

    lax.fori_loop(0, scenes, scene, 0)


def unlift(points, counts, weight, norm, z, winner, slots):
    scenes, feats, depth, size = points.shape
    channels = weight.shape[1]
    full = (feats + 2) * PACK
    return pl.pallas_call(
        unlift_body,
        in_specs=hbm(7),
        out_specs=vmem(2),
        out_shape=[
            jax.ShapeDtypeStruct((feats * PACK, LANES), f32),
            jax.ShapeDtypeStruct((8, LANES), f32),
        ],
        scratch_shapes=[
            pltpu.VMEM((full, PACK * channels), bf16),
            pltpu.VMEM(points.shape, bf16),
            pltpu.VMEM((scenes, size, LANES), bf16),
            pltpu.VMEM(slots.shape, bf16),
            pltpu.VMEM((LANES, LANES), f32),
            pltpu.VMEM((LANES, LANES), f32),
            pltpu.VMEM(counts.shape, jnp.int32),
            pltpu.VMEM(weight.shape, bf16),
            pltpu.VMEM(norm.shape, bf16),
            pltpu.SemaphoreType.DMA((4, scenes)),
        ],
        cost_estimate=pl.CostEstimate(flops=40_000_000_000, bytes_accessed=16_000_000, transcendentals=0),
        name="unlift",
    )(points, counts, weight, norm, z, winner, slots)


def edges_body(
    devices, parts, pts, counts, weight, norm, z, winner, edge, far, moments, inner, inner_bias, kgrad, payload,
    table, acc, bias, best, mult, sem,
):
    feats, channels = weight.shape
    scenes, _, depth, _ = pts.shape
    rows = feats * PACK
    size = pts.shape[3]
    peers = payload.shape[0]
    share = kgrad.shape[1]
    for r in range(devices):
        row = kgrad[r : r + 1, :]
        for q in range(1, parts):
            row = row + kgrad[q * devices + r : q * devices + r + 1, :]
        each = peers // devices
        payload[r * each : (r + 1) * each, :, :share] = jnp.broadcast_to(row[:, None, :], (each, 1, share))

    lower = iota((EDGE, LANES), 1) < channels

    def whole(s):
        rows_of = edge_rows_of(edge, s, scenes, lower) + edge_rows_of(far, s, scenes, lower)
        return rows_of.astype(bf16).astype(f32)

    def padded(grad):
        return jnp.concatenate([grad, jnp.zeros((size - EDGE, LANES), f32)], axis=0)

    total, sums = inner[...], inner_bias[...]
    for s in range(scenes):
        grad = whole(s)
        sums = sums + jnp.sum(grad.reshape(EDGE // 8, 8, LANES), axis=0)
        x = [pts[s, :, part * PACK : (part + 1) * PACK, :].reshape(rows, size) for part in range(depth // PACK)]
        total = total + single_winners(x, winner[s], padded(grad), channels)
    acc[...] = total
    bias[...] = sums

    @pl.when(jnp.min(winner[:, :EDGE, :].astype(f32)) < 0.0)
    def _():
        lift_table(weight, norm, table)

        def scene(s, _):
            @pl.when(jnp.min(winner[s, :EDGE, :].astype(f32)) < 0.0)
            def _():
                fetch = pltpu.make_async_copy(z.at[s, :size], best, sem)
                fetch.start()
                fetch.wait()
                best[...] = jnp.where(winner[s].astype(f32) < 0.0, best[...], BIG)
                count = counts[pl.ds(s, 1), :][:, :size]
                shared_winners(pts.at[s], count, table, best, padded(whole(s)), mult, acc, depth, channels)

            return 0

        lax.fori_loop(0, scenes, scene, 0)

    out = exact_right(one_hot_cols(16, rows), acc[...])
    out = out + swap_halves(out)
    pieces = [out[i : i + 1, :channels] for i in range(feats)]
    pieces.append(jnp.sum(bias[...], axis=0, keepdims=True)[:, :channels])
    pieces += [moments[i : i + 1, :16] for i in range(feats + 1)]
    width = (feats + 1) * (channels + 16)
    pieces.append(jnp.zeros((1, payload.shape[2] - share - width), f32))
    row = jnp.concatenate(pieces, axis=1)
    payload[:, :, share:] = jnp.broadcast_to(row[:, None, :], (peers, 1, row.shape[1]))


def unlift_edges(devices, parts, peers, points, counts, weight, norm, z, winner, edge, far, moments, inner, bias, kgrad):
    scenes, feats, depth, _ = points.shape
    channels = weight.shape[1]
    full = (feats + 2) * PACK
    width = -(-(feats + 1) * (channels + 16) // LANES) * LANES
    return pl.pallas_call(
        functools.partial(edges_body, devices, parts),
        grid=(1,),
        in_specs=[
            pl.BlockSpec((scenes, feats, depth, LANES), lambda i: (0, 0, 0, 0)),
            pl.BlockSpec(counts.shape, lambda i: (0, 0)),
            pl.BlockSpec(weight.shape, lambda i: (0, 0)),
            pl.BlockSpec(norm.shape, lambda i: (0, 0)),
            pl.BlockSpec(memory_space=pltpu.HBM),
            pl.BlockSpec((scenes, LANES, LANES), lambda i: (0, 0, 0)),
        ]
        + [pl.BlockSpec(x.shape, lambda i: (0, 0)) for x in (edge, far, moments, inner, bias, kgrad)],
        out_specs=pl.BlockSpec((peers, 1, kgrad.shape[1] + width), lambda i: (0, 0, 0)),
        out_shape=jax.ShapeDtypeStruct((peers, 1, kgrad.shape[1] + width), f32),
        scratch_shapes=[
            pltpu.VMEM((full, PACK * channels), bf16),
            pltpu.VMEM((feats * PACK, LANES), f32),
            pltpu.VMEM((8, LANES), f32),
            pltpu.VMEM((LANES, LANES), f32),
            pltpu.VMEM((LANES, LANES), f32),
            pltpu.SemaphoreType.DMA,
        ],
        name="edges",
    )(points, counts, weight, norm, z, winner, edge, far, moments, inner, bias, kgrad)


def adam(fixes, w, states, grad, rate):
    moment = beta_one * states[0] + (1.0 - beta_one) * grad
    second = beta_two * states[1] + (1.0 - beta_two) * grad * grad
    new = w - rate * (moment / fixes[0] / (jnp.sqrt(second / fixes[1]) + adam_eps) + decay_rate * w)
    return new, moment, second, average_keep * states[2] + (1.0 - average_keep) * new


def step_body(devices, parts, fix, got, sums, weight, norm, pm, ps, nm, ns, km, ks, *refs):
    p_new, p_states, p_avg, p_copy, n_new, n_states, n_avg, n_copy, k_new, k_states, k_avg, k_copy, kgrad = refs
    feats, channels = weight.shape
    own = km.shape[1]
    share = own // parts
    peers = got.shape[0]
    scenes = peers // devices
    fixes = (fix[0], fix[1])

    width = share * channels
    kgrad[...] = jnp.zeros_like(kgrad)
    for q in range(parts):
        tot = got[q, :, :width]
        for r in range(1, devices):
            tot = tot + got[r * scenes + q, :, :width]
        for j in range(share):
            kgrad[q * share + j : q * share + j + 1, :channels] = tot[:, j * channels : (j + 1) * channels]
    grad = jnp.transpose(kgrad[...])[:channels, :own]
    new, moment, second, average = adam(fixes, km[...], (ks[0], ks[1], ks[2]), grad, rate_kernel)
    k_new[...] = new
    k_states[0] = moment
    k_states[1] = second
    k_avg[...] = average
    k_copy[...] = new.astype(bf16)

    row = jnp.sum(got[:, :, width:], axis=0)
    cross = jnp.concatenate([row[:, i * channels : (i + 1) * channels] for i in range(feats + 1)], axis=0)
    base = (feats + 1) * channels
    moments = jnp.concatenate([row[:, base + i * 16 : base + (i + 1) * 16] for i in range(feats + 1)], axis=0)
    w = weight[...].astype(f32)
    nw = norm[...].astype(f32)
    total = moments[feats : feats + 1, feats : feats + 1]
    firsts = moments[:feats, feats : feats + 1]
    mixed = None
    first_sum = None
    for i in range(feats):
        part = moments[:feats, i : i + 1] * w[i : i + 1]
        mixed = part if mixed is None else mixed + part
        part = moments[feats : feats + 1, i : i + 1] * w[i : i + 1]
        first_sum = part if first_sum is None else first_sum + part
    mean = first_sum / total
    inv = lax.rsqrt(jnp.sum(mixed * w, axis=0, keepdims=True) / total - mean * mean + norm_eps)
    bias_p = cross[feats : feats + 1]
    gain_p = inv * (jnp.sum(w * cross[:feats], axis=0, keepdims=True) - mean * bias_p)
    spread = inv * (mixed - firsts * mean)
    point_grad = (nw[0:1] * inv) * (cross[:feats] - (firsts * bias_p + spread * gain_p) / total)
    states = (ps[:, 0, :], ps[:, 1, :], ps[:, 2, :])
    new, moment, second, average = adam(fixes, pm[...], states, point_grad, rate_points)
    p_new[...] = new
    p_states[:, 0, :] = moment
    p_states[:, 1, :] = second
    p_avg[...] = average
    p_copy[...] = new.astype(bf16)

    both = jnp.sum(sums[...], axis=0)
    norm_grad = jnp.concatenate([gain_p, bias_p, both[:, channels:], both[:, :channels]], axis=0)
    new, moment, second, average = adam(fixes, nm[...], (ns[0], ns[1], ns[2]), norm_grad, rate_norms)
    n_new[...] = new
    n_states[0] = moment
    n_states[1] = second
    n_avg[...] = average
    n_copy[...] = new.astype(bf16)


def update(devices, parts, fix, got, sums, weight, norm, pm, ps, nm, ns, km, ks):
    feats, channels = weight.shape
    shapes = []
    for m, states in ((pm, (feats, 2, channels)), (nm, (2,) + nm.shape), (km, (2,) + km.shape)):
        shapes.append(jax.ShapeDtypeStruct(m.shape, f32))
        shapes.append(jax.ShapeDtypeStruct(states, f32))
        shapes.append(jax.ShapeDtypeStruct(m.shape, f32))
        shapes.append(jax.ShapeDtypeStruct(m.shape, bf16))
    return pl.pallas_call(
        functools.partial(step_body, devices, parts),
        in_specs=smem(1) + vmem(10),
        out_specs=vmem(12),
        out_shape=shapes,
        scratch_shapes=[pltpu.VMEM((LANES, LANES), f32)],
        name="update",
    )(fix, got, sums, weight, norm, pm, ps, nm, ns, km, ks)


def shifted(x, by):
    length = lax.axis_size("rows")
    pairs = [(i, i + by) for i in range(length) if 0 <= i + by < length]
    return lax.ppermute(x, "rows", pairs)


def exchange(x):
    return lax.all_to_all(x, ("rows", "scene"), 0, 0, tiled=True)


def body(
    points,
    pillar_counts,
    pillar_pixels,
    point_weight,
    point_master,
    point_states,
    norm_weight,
    norm_master,
    norm_states,
    kernel_weight,
    kernel_master,
    kernel_states,
    step_count,
    cotangent,
):
    size = points.shape[3]
    out_rows, scenes, channels, out_cols = cotangent.shape
    cols = 2 * out_cols
    devices = lax.axis_size("rows")
    scene_devices = lax.axis_size("scene")
    peers = devices * scene_devices
    cells = float(out_rows * scenes * out_cols * peers)
    own = kernel_weight.shape[0]
    parts = scene_devices if own % scene_devices == 0 else 1
    share = own // parts * channels
    mine = lax.axis_index("scene") if parts > 1 else jnp.int32(0)

    z, winner, edge, stats, moments = lift(
        mine.reshape(1, 1), points, pillar_counts, pillar_pixels, point_weight, norm_weight, kernel_weight.T, peers, share
    )
    edge = shifted(edge, 1)
    got = exchange(stats)
    held = scenes // 2 * EDGE
    far_pixels = edge[held : held + scenes].astype(jnp.int32)
    pairs = out_rows // 2
    own_pixels = pillar_pixels.reshape(scenes * pairs, 1, size // pairs)
    conv, pooled, sums, kernel = convolve(
        devices, parts, own_pixels, far_pixels, got, z, edge, norm_weight, pairs, out_cols
    )
    conv_stats = exchange(sums[:, None])

    far_pixels = far_pixels[:, :EDGE]
    at = (pillar_pixels % cols) // 2
    own_at = (pillar_pixels // (2 * cols) + 1) * (out_cols + 8) + at
    take_at = jnp.concatenate([own_at, (far_pixels % cols) // 2], axis=1)
    take_at = jnp.pad(take_at, ((0, 0), (0, -(size + EDGE) % (16 * pairs))))
    take_at = take_at.reshape(scenes * pairs, 1, take_at.shape[1] // pairs)
    own_phase = (pillar_pixels // cols % 2) * 2 + pillar_pixels % 2
    phase = jnp.concatenate([own_phase, 2 + far_pixels % 2], axis=1)
    phase = jnp.pad(phase, ((0, 0), (0, LANES - EDGE))).astype(f32)[:, None]

    result, sums = normalize(cells, conv_stats, conv, cotangent, norm_weight)
    grad_sums = exchange(sums[:, None])
    slots, own_edge, far, kgrad = gradients(
        cells, devices, parts, take_at, conv_stats, grad_sums, conv, cotangent, norm_weight, pooled, phase, kernel
    )
    far = shifted(far, -1)
    if parts > 1:
        kgrad = lax.all_to_all(kgrad, "scene", 0, 0, tiled=True)
    else:
        kgrad = lax.psum(kgrad, "scene")
    inner, bias = unlift(points, pillar_counts, point_weight, norm_weight, z, winner, slots)
    far, kgrad, inner, bias = lax.optimization_barrier((far, kgrad, inner, bias))
    payload = unlift_edges(
        devices, parts, peers, points, pillar_counts, point_weight, norm_weight, z, winner, own_edge, far, moments, inner, bias, kgrad
    )
    got = exchange(payload)
    steps_done = step_count[0].astype(f32)
    fix = jnp.stack([1.0 - beta_one**steps_done, 1.0 - beta_two**steps_done])
    outs = update(
        devices,
        parts,
        fix,
        got,
        grad_sums,
        point_weight,
        norm_weight,
        point_master,
        jnp.transpose(point_states, (1, 0, 2)),
        norm_master,
        norm_states,
        kernel_master.T,
        jnp.transpose(kernel_states, (0, 2, 1)),
    )
    outs = list(outs)
    outs[1] = jnp.transpose(outs[1], (1, 0, 2))
    outs[8], outs[10], outs[11] = outs[8].T, outs[10].T, outs[11].T
    outs[9] = jnp.transpose(outs[9], (0, 2, 1))
    return (result, *outs)


def solution(mesh):
    placed = (
        P("scene", None, None, "rows"),
        P("scene", "rows"),
        P("scene", "rows"),
        P(),
        P(),
        P(),
        P(),
        P(),
        P(),
        P("rows", None),
        P("rows", None),
        P(None, "rows", None),
        P(),
        P("rows", "scene", None, None),
    )
    return jax.shard_map(
        body,
        mesh=mesh,
        in_specs=placed,
        out_specs=(
            P("rows", "scene", None, None),
            P(),
            P(),
            P(),
            P(),
            P(),
            P(),
            P(),
            P(),
            P("rows", None),
            P(None, "rows", None),
            P("rows", None),
            P("rows", None),
        ),
        check_vma=False,
    )
```

```python
import functools

import jax
import jax.numpy as jnp
from jax import lax
from jax.experimental import pallas as pl
from jax.experimental.pallas import tpu as pltpu
from jax.sharding import PartitionSpec as P

beta_one = 0.9
beta_two = 0.999
adam_eps = 1e-08
decay_rate = 0.01
average_keep = 0.99
norm_eps = 1e-05
rate_points = 0.3
rate_norms = 0.2
rate_kernel = 0.04

EDGE = 48
BIG = 1e30
PACK = 8
ROWS = 128
TILE = 256
LANES = 128
f32 = jnp.float32
bf16 = jnp.bfloat16


def iota(shape, dim):
    return lax.broadcasted_iota(jnp.int32, shape, dim)


def dot_nn(a, b):
    return lax.dot_general(a, b, (((1,), (0,)), ((), ())), preferred_element_type=f32)


def dot_nt(a, b):
    return lax.dot_general(a, b, (((1,), (1,)), ((), ())), preferred_element_type=f32)


def dot_tn(a, b):
    return lax.dot_general(a, b, (((0,), (0,)), ((), ())), preferred_element_type=f32)


def split3(x):
    a = x.astype(bf16)
    r = x - a.astype(f32)
    b = r.astype(bf16)
    c = (r - b.astype(f32)).astype(bf16)
    return a, b, c


def exact_left(x, y):
    a, b, c = split3(x)
    return dot_nn(a, y) + (dot_nn(b, y) + dot_nn(c, y))


def exact_right(x, y):
    a, b, c = split3(y)
    return dot_nn(x, a) + (dot_nn(x, b) + dot_nn(x, c))


def swap_halves(x):
    return pltpu.roll(x, x.shape[1] // 2, axis=1)


def twice(row):
    return jnp.concatenate([row, row], axis=1)


def one_hot_rows(rows, cols):
    return (iota((rows, cols), 0) // PACK == iota((rows, cols), 1)).astype(f32).astype(bf16)


def one_hot_cols(rows, cols):
    return (iota((rows, cols), 1) // PACK == iota((rows, cols), 0)).astype(f32).astype(bf16)


def lift_table(weight, norm, table):
    feats, channels = weight.shape
    rows = table.shape[0]
    gain = norm[0:1, :].astype(f32)
    sign = jnp.where(gain > 0, 1.0, jnp.where(gain < 0, -1.0, 0.0))
    signed = weight[...].astype(f32) * sign
    full = jnp.concatenate([signed, jnp.zeros((1, channels), f32), jnp.ones((1, channels), f32)], axis=0)
    full = jnp.concatenate([full, jnp.zeros((16 - feats - 2, channels), f32)], axis=0)
    base = dot_nn(one_hot_rows(rows, 16), twice(full).astype(bf16))
    slot = iota(base.shape, 0) % PACK
    half = iota(base.shape, 1) // channels
    for m in range(PACK // 2):
        table[:, m * LANES : (m + 1) * LANES] = jnp.where(slot == 2 * m + half, base, 0.0).astype(bf16)


def lift_inputs(pts, count, part):
    feats, _, size = pts.shape
    live = (iota((PACK, size), 0) + part * PACK < count).astype(f32)
    low = live.astype(bf16)
    dead = ((live - 1.0) * BIG).astype(bf16)
    full = jnp.concatenate([pts.reshape(feats * PACK, size), low, dead], axis=0)
    kept = jnp.concatenate([(pts * low[None]).reshape(feats * PACK, size), low], axis=0)
    return full, kept


def copy_in(source, target, sems, s):
    return pltpu.make_async_copy(source.at[s], target.at[s], sems.at[s])


def half_store(block, s, scenes, value):
    channels = LANES // 2
    spot = pl.ds(pl.multiple_of((s % (scenes // 2)) * EDGE, 8), EDGE)
    lower = iota((EDGE, LANES), 1) < channels
    block[spot, :] = jnp.where(lower == (s < scenes // 2), value, block[spot, :])


def lift_body(
    mine, points, counts, pixels, weight, norm, kernel, z_out, winner_out, edge, payload, moments,
    table, gram, wide, pts, z, winner, sems,
):
    feats, channels = weight.shape
    scenes, _, depth, size = points.shape
    rows = (feats + 1) * PACK
    for s in range(scenes):
        copy_in(points, pts, sems.at[0], s).start()
    lift_table(weight, norm, table)
    gram[...] = jnp.zeros_like(gram)
    edge[...] = jnp.zeros_like(edge)

    def scene(s, _):
        copy_in(points, pts, sems.at[0], s).wait()
        count = counts[pl.ds(s, 1), :]
        total = None
        inputs = []
        for part in range(depth // PACK):
            xin, kept = lift_inputs(pts[s, :, part * PACK : (part + 1) * PACK, :], count, part)
            prod = dot_nt(kept, xin[:rows])
            total = prod if total is None else total + prod
            inputs.append(xin)
        for t in range(size // LANES):
            turned = [jnp.transpose(x[:, t * LANES : (t + 1) * LANES]) for x in inputs]
            for h in range(LANES // ROWS):
                best = None
                for part in range(depth // PACK):
                    lhs = turned[part][h * ROWS : (h + 1) * ROWS]
                    for q in range(PACK // 4):
                        l = dot_nn(lhs, table[:, q * 256 : (q + 1) * 256])
                        one, two = l[:, :LANES], l[:, LANES:]
                        n_one, n_two = float(part * PACK + q * 4), float(part * PACK + q * 4 + 2)
                        m = jnp.maximum(one, two)
                        low = jnp.where(two > one, n_two, n_one)
                        high = jnp.where(two >= one, n_two, n_one)
                        if best is None:
                            best, first, last = m, low, high
                        else:
                            first = jnp.where(m > best, low, first)
                            last = jnp.where(m >= best, high, last)
                            best = jnp.maximum(best, m)
                at = slice(t * LANES + h * ROWS, t * LANES + (h + 1) * ROWS)
                upper = (iota((ROWS, LANES), 1) >= channels).astype(f32)
                first, last = first + upper, last + upper
                other = swap_halves(best)
                first = jnp.where(other > best, swap_halves(first), first)
                last = jnp.where(other >= best, swap_halves(last), last)
                best = jnp.maximum(best, other)
                only = jnp.where(first == last, first, -1.0)
                winner[s, at, :] = jnp.where(best > -0.5 * BIG, only, 99.0).astype(bf16)
                z[s, at, :] = best
        gram[...] += total
        copy_in(z, z_out, sems.at[1], s).start()
        copy_in(winner, winner_out, sems.at[2], s).start()
        half_store(edge, s, scenes, z[s, :EDGE, :])
        return 0

    lax.fori_loop(0, scenes, scene, 0)

    count_rows = edge.shape[0] - 2 * scenes
    edge[count_rows : count_rows + scenes, :] = pixels[:, :LANES].astype(f32)
    edge[count_rows + scenes :, :] = jnp.ones((scenes, LANES), f32)
    g = gram[...]
    g = jnp.where(iota(g.shape, 0) % PACK == iota(g.shape, 1) % PACK, g, 0.0)
    y = exact_left(g, one_hot_rows(rows, LANES))
    m = exact_right(one_hot_cols(16, rows), y)
    moments[...] = m
    w = jnp.concatenate([weight[...].astype(f32), jnp.zeros((16 - feats, channels), f32)], axis=0)
    aw = exact_left(m[:, :16], w.astype(bf16))
    two = jnp.sum(aw * w, axis=0, keepdims=True)
    one = aw[feats : feats + 1]
    own = kernel.shape[1]
    flat = jnp.concatenate([kernel[...].astype(f32), jnp.zeros((channels, LANES - own), f32)], axis=1)
    wide[...] = jnp.transpose(jnp.concatenate([flat, jnp.zeros((LANES - channels, LANES), f32)], axis=0))
    pieces = [one, two, m[feats : feats + 1]]
    share = (payload.shape[2] - 256) // channels
    for j in range(share):
        pieces.append(wide[pl.ds(mine[0, 0] * share + j, 1), :channels])
    row = jnp.concatenate(pieces, axis=1)
    payload[...] = jnp.broadcast_to(row[:, None, :], payload.shape)
    for s in range(scenes):
        copy_in(z, z_out, sems.at[1], s).wait()
        copy_in(winner, winner_out, sems.at[2], s).wait()


def vmem(count):
    return [pl.BlockSpec(memory_space=pltpu.VMEM)] * count


def smem(count):
    return [pl.BlockSpec(memory_space=pltpu.SMEM)] * count


def own_copies(body, small, *refs):
    refs = list(refs)
    count = len(small)
    places, sems = refs[-count - 1 : -1], refs[-1]
    refs = refs[: -count - 1]
    copies = []
    for i, (at, place) in enumerate(zip(small, places)):
        copies.append(pltpu.make_async_copy(refs[at], place, sems.at[i]))
        refs[at] = place
    for copy in copies:
        copy.start()

    def ready():
        for copy in copies:
            copy.wait()

    body(ready, *refs)


def places_of(inputs, small):
    return [pltpu.VMEM(inputs[at].shape, inputs[at].dtype) for at in small] + [pltpu.SemaphoreType.DMA((len(small),))]


def hbm(count):
    return [pl.BlockSpec(memory_space=pltpu.HBM)] * count


def lift(mine, points, counts, pixels, weight, norm, kernel, peers, share):
    scenes, feats, depth, size = points.shape
    channels = weight.shape[1]
    full = (feats + 2) * PACK
    rows = (feats + 1) * PACK
    edge_rows = scenes // 2 * EDGE + 2 * scenes
    return pl.pallas_call(
        lift_body,
        in_specs=smem(1) + hbm(1) + vmem(5),
        out_specs=hbm(2) + vmem(3),
        out_shape=[
            jax.ShapeDtypeStruct((scenes, size, LANES), f32),
            jax.ShapeDtypeStruct((scenes, size, LANES), bf16),
            jax.ShapeDtypeStruct((edge_rows, LANES), f32),
            jax.ShapeDtypeStruct((peers, 1, 256 + share), f32),
            jax.ShapeDtypeStruct((16, LANES), f32),
        ],
        scratch_shapes=[
            pltpu.VMEM((full, PACK * channels), bf16),
            pltpu.VMEM((rows, rows), f32),
            pltpu.VMEM((LANES, LANES), f32),
            pltpu.VMEM(points.shape, bf16),
            pltpu.VMEM((scenes, size, LANES), f32),
            pltpu.VMEM((scenes, size, LANES), bf16),
            pltpu.SemaphoreType.DMA((3, scenes)),
        ],
        name="lift",
    )(mine, points, counts, pixels, weight, norm, kernel)


def gather_kernel(got, kern, devices, parts):
    channels = kern.shape[1]
    share = kern.shape[0] // devices // parts
    peers = got.shape[0]
    for j in range(share):
        rows = got[:, 0, 256 + j * channels : 256 + (j + 1) * channels]
        if parts > 1:
            kern[pl.ds(j, peers, stride=share), :] = rows
        else:
            for r in range(devices):
                at = r * (peers // devices)
                kern[r * share + j : r * share + j + 1, :] = rows[at : at + 1]


def tap(kern, a, b):
    channels = kern.shape[1]
    if a is None or b is None:
        return jnp.zeros((channels, channels), f32)
    return kern[(3 * a + b) * channels : (3 * a + b + 1) * channels, :]


def edge_rows_of(block, s, scenes, lower):
    base = (s % (scenes // 2)) * EDGE
    spot = pl.ds(base if isinstance(base, int) else pl.multiple_of(base, 8), EDGE)
    rows = jnp.where(lower == (s < scenes // 2), block[spot, :], 0.0)
    return rows + swap_halves(rows)


def conv_body(
    devices, parts, pix, far_pix, got, z_in, edge, norm, conv_out, pooled_out, sums, kernel,
    params, source, kern, taps, grid_a, grid_b, side, acc, z, conv, pooled, sems,
):
    scenes, size, _ = z.shape
    for s in range(scenes):
        copy_in(z_in, z, sems.at[0], s).start()
    channels = norm.shape[1]
    _, pairs, out_cols, _ = conv.shape
    cols = 2 * out_cols
    last_row = (4 * pairs - 1) * cols
    tot = jnp.sum(got[:, :, :256], axis=0)
    count = tot[:, 2 * channels + 9 : 2 * channels + 10]
    mean = tot[:, :channels] / count
    inv = lax.rsqrt(tot[:, channels : 2 * channels] / count - mean * mean + norm_eps)
    nw = norm[...].astype(f32)
    gain = nw[0:1]
    sign = jnp.where(gain > 0, 1.0, jnp.where(gain < 0, -1.0, 0.0))
    params[0:1] = twice(mean)
    params[1:2] = twice(inv)
    params[2:3] = twice(gain)
    params[3:4] = twice(nw[1:2])
    params[4:5] = twice(sign)
    gather_kernel(got, kern, devices, parts)
    kernel[...] = kern[...].astype(bf16)
    for w, (low, high) in enumerate(((0, None), (1, None), (2, 0), (None, 1), (None, 2))):
        none = tap(kern, None, None)
        top = jnp.concatenate([tap(kern, low, 1), tap(kern, high, 1), none, none], axis=1)
        end = jnp.concatenate([tap(kern, low, 2), tap(kern, high, 2), tap(kern, low, 0), tap(kern, high, 0)], axis=1)
        taps[w] = jnp.concatenate([top, end], axis=0).astype(bf16)
    grid_a[...] = jnp.zeros_like(grid_a)
    side[...] = jnp.zeros_like(side)
    acc[...] = jnp.zeros_like(acc)

    def pool(x, ok):
        pre = params[2:3] * ((x * params[4:5] - params[0:1]) * params[1:2]) + params[3:4]
        return jnp.where(ok, jnp.maximum(pre, 0.0), 0.0).astype(bf16)

    own_at = 8 + cols
    far_at = 8 - last_row
    some = size // pairs

    def part_of(j):
        return pl.ds(j * some if isinstance(j, int) else pl.multiple_of(j * some, 16), some)

    def fill(s, j):
        zs = z[s, part_of(j), :]
        own = pool(zs, zs > -0.5 * BIG)
        pooled[s, part_of(j), :] = own
        source[part_of(j), :] = own.astype(f32)

    def fill_far(dst, s):
        far = edge_rows_of(edge, s, scenes, iota((EDGE, LANES), 1) < channels)
        flag = edge[edge.shape[0] - scenes : edge.shape[0] - scenes + 1, :]
        far = pool(far, (far > -0.5 * BIG) & (flag > 0.5))
        pooled[s, size:] = jnp.concatenate([far, jnp.zeros((LANES - EDGE, LANES), bf16)], axis=0)
        source[size : size + EDGE] = far.astype(f32)
        for p in range(EDGE):
            at = jnp.maximum(far_pix[s, p], last_row) + far_at
            dst[pl.ds(at, 1), :] = source[size + p : size + p + 1, :]

    def place(dst, s, j):
        rows = dst.at[pl.ds(own_at, 4 * pairs * cols), :]
        line = pix.at[s * pairs + j]
        values = source.at[part_of(j), :]
        for p in range(some):
            rows[pl.ds(line[0, p], 1), :] = values[p : p + 1, :]

    left = iota((out_cols, LANES), 1) < channels

    def convolve_pair(src, s, j):
        out = None
        for w in range(5):
            base = 8 + (4 * j + w) * cols
            even = src[pl.ds(base, out_cols, stride=2), :]
            odd = src[pl.ds(base + 1, out_cols, stride=2), :]
            part = dot_nn(jnp.where(left, even, odd).astype(bf16), taps[w])
            out = part if out is None else out + part
        side[8:, :] = out[:, LANES:]
        value = out[:, :LANES] + side[7 : 7 + out_cols, :]
        conv[s, j] = value
        acc[0:8] += jnp.sum(value.reshape(out_cols // 8, 8, LANES), axis=0)
        acc[8:16] += jnp.sum((value * value).reshape(out_cols // 8, 8, LANES), axis=0)
        used = (5 if j == pairs - 1 else 4) * cols
        base = 8 + 4 * j * cols
        src[base : base + used, :] = jnp.zeros((used, LANES), f32)

    copy_in(z_in, z, sems.at[0], 0).wait()
    fill_far(grid_a, 0)
    grid_b[:8, :] = jnp.zeros((8, LANES), f32)
    grid_b[8 + 4 * pairs * cols :, :] = jnp.zeros((grid_b.shape[0] - 8 - 4 * pairs * cols, LANES), f32)

    def start(j, _):
        grid_b[pl.ds(pl.multiple_of(8 + 4 * j * cols, 8), 4 * cols), :] = jnp.zeros((4 * cols, LANES), f32)
        fill(0, j)
        place(grid_a, 0, j)
        return 0

    lax.fori_loop(0, pairs, start, 0)

    def two_scenes(i, _):
        for k, (src, dst) in enumerate(((grid_a, grid_b), (grid_b, grid_a))):
            s = 2 * i + k
            ahead = jnp.minimum(s + 1, scenes - 1)

            @pl.when(s + 1 < scenes)
            def _():
                copy_in(z_in, z, sems.at[0], s + 1).wait()

            fill_far(dst, ahead)
            for j in range(pairs):
                fill(ahead, j)
                place(dst, ahead, j)
                convolve_pair(src, s, j)

            copy_in(conv, conv_out, sems.at[1], s).start()
            copy_in(pooled, pooled_out, sems.at[2], s).start()
        return 0

    lax.fori_loop(0, scenes // 2, two_scenes, 0)
    for s in range(scenes):
        copy_in(conv, conv_out, sems.at[1], s).wait()
        copy_in(pooled, pooled_out, sems.at[2], s).wait()
    sums[...] = jnp.broadcast_to(both_sums(acc, channels), sums.shape)


def both_sums(acc, channels):
    one = jnp.sum(acc[0:8], axis=0, keepdims=True)
    two = jnp.sum(acc[8:16], axis=0, keepdims=True)
    one = one + swap_halves(one)
    two = two + swap_halves(two)
    return jnp.where(iota((1, LANES), 1) < channels, one, two)


def convolve(devices, parts, pix, far_pix, got, z, edge, norm, pairs, out_cols):
    scenes, size, _ = z.shape
    peers = got.shape[0]
    channels = norm.shape[1]
    cells = 8 + (4 * pairs + 1) * 2 * out_cols + 8
    return pl.pallas_call(
        functools.partial(conv_body, devices, parts),
        in_specs=smem(2) + vmem(1) + hbm(1) + vmem(2),
        out_specs=hbm(2) + vmem(2),
        out_shape=[
            jax.ShapeDtypeStruct((scenes, pairs, out_cols, LANES), f32),
            jax.ShapeDtypeStruct((scenes, size + LANES, LANES), bf16),
            jax.ShapeDtypeStruct((peers, LANES), f32),
            jax.ShapeDtypeStruct((9 * channels, channels), bf16),
        ],
        scratch_shapes=[
            pltpu.VMEM((8, LANES), f32),
            pltpu.VMEM((size + LANES, LANES), f32),
            pltpu.VMEM((9 * channels, channels), f32),
            pltpu.VMEM((5, LANES, 2 * LANES), bf16),
            pltpu.VMEM((cells, LANES), f32),
            pltpu.VMEM((cells, LANES), f32),
            pltpu.VMEM((out_cols + 8, LANES), f32),
            pltpu.VMEM((16, LANES), f32),
            pltpu.VMEM((scenes, size, LANES), f32),
            pltpu.VMEM((scenes, pairs, out_cols, LANES), f32),
            pltpu.VMEM((scenes, size + LANES, LANES), bf16),
            pltpu.SemaphoreType.DMA((3, scenes)),
        ],
        name="convolve",
    )(pix, far_pix, got, z, edge, norm)


def split_sums(stats, channels):
    tot = jnp.sum(stats[...], axis=0)
    lower = iota((1, LANES), 1) < channels
    turned = swap_halves(tot)
    return jnp.where(lower, tot, turned), jnp.where(lower, turned, tot)


def conv_params(cells, stats, norm):
    one, two = split_sums(stats, norm.shape[1])
    mean = one / cells
    inv = lax.rsqrt(two / cells - mean * mean + norm_eps)
    nw = norm[...].astype(f32)
    return mean, inv, twice(nw[2:3]), twice(nw[3:4])


def turned_pair(block, j, k):
    _, _, channels, cols = block.shape
    return jnp.transpose(block[2 * j : 2 * j + 2, k].reshape(2 * channels, cols)).astype(f32)


def scene_copy(source, target, sems, s):
    return pltpu.make_async_copy(source.at[:, s], target.at[:, s], sems.at[s])


def norm_body(cells, stats, conv_in, cot_in, norm, result_out, sums, acc, conv, cot, result, sems):
    channels = norm.shape[1]
    scenes, pairs, out_cols, _ = conv.shape
    for s in range(scenes):
        copy_in(conv_in, conv, sems.at[0], s).start()
        scene_copy(cot_in, cot, sems.at[1], s).start()
    mean, inv, gain, bias = conv_params(cells, stats, norm)
    acc[...] = jnp.zeros_like(acc)

    def scene(k, _):
        copy_in(conv_in, conv, sems.at[0], k).wait()
        scene_copy(cot_in, cot, sems.at[1], k).wait()
        for j in range(pairs):
            xhat = (conv[k, j] - mean) * inv
            pre = gain * xhat + bias
            out = jnp.transpose(jnp.maximum(pre, 0.0).astype(bf16))
            result[2 * j : 2 * j + 2, k] = out.reshape(2, channels, out_cols)
            back = jnp.where(pre > 0, turned_pair(cot, j, k), 0.0)
            acc[0:8] += jnp.sum(back.reshape(out_cols // 8, 8, LANES), axis=0)
            acc[8:16] += jnp.sum((back * xhat).reshape(out_cols // 8, 8, LANES), axis=0)
        scene_copy(result, result_out, sems.at[2], k).start()
        return 0

    lax.fori_loop(0, scenes, scene, 0)
    sums[...] = jnp.broadcast_to(both_sums(acc, channels), sums.shape)
    for s in range(scenes):
        scene_copy(result, result_out, sems.at[2], s).wait()


def normalize(cells, stats, conv, cot, norm):
    peers = stats.shape[0]
    scenes = conv.shape[0]
    return pl.pallas_call(
        functools.partial(norm_body, cells),
        in_specs=vmem(1) + hbm(2) + vmem(1),
        out_specs=hbm(1) + vmem(1),
        out_shape=[
            jax.ShapeDtypeStruct(cot.shape, bf16),
            jax.ShapeDtypeStruct((peers, LANES), f32),
        ],
        scratch_shapes=[
            pltpu.VMEM((16, LANES), f32),
            pltpu.VMEM(conv.shape, f32),
            pltpu.VMEM(cot.shape, bf16),
            pltpu.VMEM(cot.shape, bf16),
            pltpu.SemaphoreType.DMA((3, scenes)),
        ],
        name="normalize",
    )(stats, conv, cot, norm)


def grad_body(
    cells, devices, parts, idx, stats, sums, conv_in, cot_in, norm, pooled_in, phase, kernel, slots_out, edge, far, kgrad,
    taps, field_a, field_b, taken_a, taken_b, turn, column_a, column_b, acc, rows_k, conv, cot, pooled, slots_a, slots_b, exact_a, exact_b, staged, sems,
):
    scenes, pairs, out_cols, _ = conv.shape
    channels = norm.shape[1]
    size = slots_a.shape[0]
    strip = out_cols + 8
    some = idx.shape[2]
    columns, slots, exact = (column_a, column_b), (slots_a, slots_b), (exact_a, exact_b)
    for s in range(scenes):
        copy_in(conv_in, conv, sems.at[0], s).start()
        scene_copy(cot_in, cot, sems.at[1], s).start()
        copy_in(pooled_in, pooled, sems.at[2], s).start()
    for hp in range(2):
        for up in range(2):
            line = []
            for dw in range(2):
                for dr in range(2):
                    a = ((1, None), (2, 0))[hp][dr]
                    b = ((1, None), (2, 0))[up][dw]
                    if a is None or b is None:
                        line.append(jnp.zeros((channels, channels), f32))
                    else:
                        at = (3 * a + b) * channels
                        line.append(kernel[at : at + channels, :].astype(f32))
            ph = 2 * hp + up
            taps[ph * channels : (ph + 1) * channels, :] = jnp.concatenate(line, axis=1).astype(bf16)
    for block in (field_a, field_b, taken_a, taken_b, acc):
        block[...] = jnp.zeros_like(block)

    def phases(column, s, j):
        chunks = column.shape[0] // LANES
        for c in range(j * chunks // pairs, (j + 1) * chunks // pairs):
            row = phase[s, :, c * LANES : (c + 1) * LANES]
            column[c * LANES : (c + 1) * LANES, :] = jnp.transpose(jnp.broadcast_to(row, (LANES, LANES)))

    mean, inv, gain, bias = conv_params(cells, stats, norm)
    bias_grad, gain_grad = split_sums(sums, channels)
    scale = gain * inv / cells
    left = iota((out_cols, LANES), 1) < channels
    half = (iota((some, LANES), 1) >= channels).astype(f32)

    def field(dst, s, j):
        xhat = (conv[s, j] - mean) * inv
        pre = gain * xhat + bias
        both = cot[2 * j : 2 * j + 2, s].reshape(2 * channels, out_cols)
        back = jnp.where(pre > 0, jnp.transpose(both).astype(f32), 0.0)
        grad = scale * (cells * back - bias_grad - xhat * gain_grad)
        grad = grad.astype(bf16).astype(f32)
        turned = swap_halves(grad)
        base = 2 * j * strip
        dst[base : base + out_cols, :] = jnp.where(left, turn[...], turned)
        dst[base + strip : base + strip + out_cols, :] = grad
        turn[...] = turned

    def take(dst, src, s, j):
        line = idx.at[s * pairs + j]
        for p in range(some):
            dst[2 * p : 2 * p + 2, :] = src[pl.ds(line[0, p], 2), :]

    def product(src, k, s, j):
        at = slice(j * some, (j + 1) * some)
        part = jnp.concatenate([src[pl.ds(0, some, stride=2), :], src[pl.ds(1, some, stride=2), :]], axis=1).astype(bf16)
        out = dot_nt(part, taps[...])
        ph = columns[k][at, :]
        is_even = ph == half
        is_odd = ph == half + 2.0
        value = jnp.where(is_even, out[:, :LANES], 0.0) + jnp.where(is_odd, out[:, LANES:], 0.0)
        value = value + swap_halves(value)
        pf = pooled[s, at, :].astype(f32)
        value = jnp.where(pf > 0, value, 0.0)
        exact[k][at, :] = value
        slots[k][at, :] = value.astype(bf16)
        split = jnp.concatenate([jnp.where(is_even, pf, 0.0), jnp.where(is_odd, pf, 0.0)], axis=1)
        acc[...] += dot_tn(split.astype(bf16), part)

    def copy_out(s):
        return copy_in(staged, slots_out, sems.at[3], s)

    def done(k, s):
        half_store(edge, s, scenes, exact[k][:EDGE, :])
        half_store(far, s, scenes, exact[k][size - LANES : size - LANES + EDGE, :])
        staged[s, :EDGE, :] = jnp.zeros((EDGE, LANES), bf16)
        staged[s, EDGE:, :] = slots[k][EDGE:, :]
        copy_out(s).start()

    def walk(dst, src, k, s):
        before = jnp.clip(s - 1, 0, scenes - 1)
        held = jnp.where(s > 0, s - 1, scenes)
        older = jnp.where(s > 1, s - 2, scenes)
        if dst is not None:
            copy_in(conv_in, conv, sems.at[0], s).wait()
            scene_copy(cot_in, cot, sems.at[1], s).wait()
            turn[...] = jnp.zeros_like(turn)

        @pl.when(s > 0)
        def _():
            copy_in(pooled_in, pooled, sems.at[2], before).wait()


        for j in range(pairs):
            to, of = ((taken_a, taken_b), (taken_b, taken_a))[j % 2]
            if dst is not None:
                phases(columns[k], s, j)
                field(dst, s, j)
            take(to, src, before, j)
            product(of, k if j == 0 else 1 - k, held if j > 0 else older, (j - 1) % pairs)

        @pl.when(s >= 2)
        def _():
            done(k, s - 2)

        if dst is not None:
            dst[2 * pairs * strip : 2 * pairs * strip + out_cols, :] = jnp.where(left, turn[...], 0.0)

    def two_scenes(i, _):
        walk(field_a, field_b, 0, 2 * i)
        walk(field_b, field_a, 1, 2 * i + 1)
        return 0

    far[...] = jnp.zeros_like(far)
    edge[...] = jnp.zeros_like(edge)
    for block in (column_a, column_b):
        block[...] = jnp.zeros_like(block)
    pooled[scenes] = jnp.zeros_like(pooled[scenes])
    lax.fori_loop(0, scenes // 2, two_scenes, 0)
    walk(None, field_b, 0, scenes)
    product(taken_b, 1, scenes - 1, pairs - 1)
    done(1, scenes - 1)
    for a in range(3):
        for b in range(3):
            hp, dr = ((1, 1), (0, 0), (1, 0))[a]
            up, dw = ((1, 1), (0, 0), (1, 0))[b]
            row, col = hp * 2 + up, dw * 2 + dr
            at = (3 * a + b) * channels
            rows_k[at : at + channels, :] = acc[
                row * channels : (row + 1) * channels, col * channels : (col + 1) * channels
            ]
    own = rows_k.shape[0] // devices
    share = own // parts
    for q in range(parts):
        for j in range(share):
            lanes = slice(j * channels, (j + 1) * channels)
            kgrad[q * devices : (q + 1) * devices, lanes] = rows_k[pl.ds(q * share + j, devices, stride=own), :]
    for s in range(scenes):
        copy_out(s).wait()


def gradients(cells, devices, parts, idx, stats, sums, conv, cot, norm, pooled, phase, kernel):
    scenes, pairs, out_cols, _ = conv.shape
    channels = norm.shape[1]
    rows = pooled.shape[1]
    return pl.pallas_call(
        functools.partial(grad_body, cells, devices, parts),
        in_specs=smem(1) + vmem(2) + hbm(2) + vmem(1) + hbm(1) + vmem(2),
        out_specs=hbm(1) + vmem(3),
        out_shape=[
            jax.ShapeDtypeStruct((scenes, rows, LANES), bf16),
            jax.ShapeDtypeStruct((scenes // 2 * EDGE, LANES), f32),
            jax.ShapeDtypeStruct((scenes // 2 * EDGE, LANES), f32),
            jax.ShapeDtypeStruct((parts * devices, 9 * channels * channels // devices // parts), f32),
        ],
        scratch_shapes=[
            pltpu.VMEM((4 * channels, 4 * channels), bf16),
            pltpu.VMEM(((2 * pairs + 1) * (out_cols + 8), LANES), f32),
            pltpu.VMEM(((2 * pairs + 1) * (out_cols + 8), LANES), f32),
            pltpu.VMEM((2 * idx.shape[2], LANES), f32),
            pltpu.VMEM((2 * idx.shape[2], LANES), f32),
            pltpu.VMEM((out_cols, LANES), f32),
            pltpu.VMEM((rows, LANES), f32),
            pltpu.VMEM((rows, LANES), f32),
            pltpu.VMEM((4 * channels, 4 * channels), f32),
            pltpu.VMEM((9 * channels, channels), f32),
            pltpu.VMEM(conv.shape, f32),
            pltpu.VMEM(cot.shape, bf16),
            pltpu.VMEM((scenes + 1, rows, LANES), bf16),
            pltpu.VMEM((rows, LANES), bf16),
            pltpu.VMEM((rows, LANES), bf16),
            pltpu.VMEM((rows, LANES), f32),
            pltpu.VMEM((rows, LANES), f32),
            pltpu.VMEM((scenes, rows, LANES), bf16),
            pltpu.SemaphoreType.DMA((4, scenes)),
        ],
        name="gradients",
    )(idx, stats, sums, conv, cot, norm, pooled, phase, kernel)


def fold(q, prod, channels):
    shape = (prod.shape[0], LANES)
    slot = iota(shape, 0) % PACK - 4 * q
    upper = (iota(shape, 1) >= channels).astype(jnp.int32)
    return jnp.where(slot == upper, prod[:, :LANES], 0.0) + jnp.where(slot == upper + 2, prod[:, LANES:], 0.0)


def single_winners(pts, who, grad, channels):
    size = who.shape[0]
    who = who.astype(f32) - (iota((size, LANES), 1) >= channels).astype(f32)
    total = None
    for part, x in enumerate(pts):
        for q in range(PACK // 4):
            n = part * PACK + q * 4
            one = jnp.where(who == float(n), grad, 0.0)
            two = jnp.where(who == float(n + 2), grad, 0.0)
            prod = fold(q, dot_nn(x, jnp.concatenate([one, two], axis=1).astype(bf16)), channels)
            total = prod if total is None else total + prod
    return total


def shared_winners(pts, count, table, who, grad, share, acc, depth, channels):
    feats = pts.shape[0]
    size = who.shape[0]

    def lifted(part, q):
        xin, _ = lift_inputs(pts[:, part * PACK : (part + 1) * PACK, :], count, part)
        l = dot_nn(jnp.transpose(xin), table[:, q * 256 : (q + 1) * 256])
        return xin[: feats * PACK], l[:, :LANES], l[:, LANES:]

    best = jnp.full((size, LANES), -3.0 * BIG, f32)
    times = jnp.zeros((size, LANES), f32)
    for part in range(depth // PACK):
        for q in range(PACK // 4):
            _, one, two = lifted(part, q)
            for l in (one, two):
                times = jnp.where(l > best, 1.0, jnp.where(l == best, times + 1.0, times))
                best = jnp.maximum(best, l)
    other, more = swap_halves(best), swap_halves(times)
    times = jnp.where(other > best, more, jnp.where(other == best, times + more, times))
    best = jnp.where(who < 0.0, jnp.maximum(best, other), BIG)
    share[...] = grad / times

    def add(of):
        total = None
        for part in range(depth // PACK):
            for q in range(PACK // 4):
                x, one, two = lifted(part, q)
                value = of(share[...])
                value = jnp.concatenate([jnp.where(one == best, value, 0.0), jnp.where(two == best, value, 0.0)], axis=1)
                part_sum = fold(q, dot_nn(x, value.astype(bf16)), channels)
                total = part_sum if total is None else total + part_sum
        acc[...] += total

    def rest(x):
        return x - x.astype(bf16).astype(f32)

    add(lambda x: x)

    @pl.when(jnp.max(jnp.where(who < 0.0, jnp.abs(rest(share[...])), 0.0)) > 0.0)
    def _():
        add(rest)
        add(lambda x: rest(rest(x)))


def unlift_body(
    ready, points, counts, weight, norm, winner_in, slots_in, acc, bias, table, pts, winner, slots, share, seen, sems
):
    feats, channels = weight.shape
    scenes, _, depth, size = points.shape
    rows = feats * PACK
    tiles = size // TILE
    for s in range(scenes):
        copy_in(points, pts, sems.at[0], s).start()
        copy_in(winner_in, winner, sems.at[1], s).start()
        copy_in(slots_in, slots, sems.at[2], s).start()
    acc[...] = jnp.zeros_like(acc)
    bias[...] = jnp.zeros_like(bias)

    def scene(s, _):
        copy_in(points, pts, sems.at[0], s).wait()
        copy_in(winner_in, winner, sems.at[1], s).wait()
        copy_in(slots_in, slots, sems.at[2], s).wait()
        total = None
        sums = None
        least = None
        for t in range(tiles):
            at = slice(t * TILE, (t + 1) * TILE)
            grad = slots[s, at, :].astype(f32)
            who = winner[s, at, :].astype(f32)
            one = jnp.sum(grad.reshape(TILE // 8, 8, LANES), axis=0)
            sums = one if sums is None else sums + one
            one = jnp.min(who.reshape(TILE // 8, 8, LANES), axis=0)
            least = one if least is None else jnp.minimum(least, one)
            x = [pts[s, :, part * PACK : (part + 1) * PACK, at].reshape(rows, TILE) for part in range(depth // PACK)]
            one = single_winners(x, who, grad, channels)
            total = one if total is None else total + one
        acc[...] += total
        bias[...] += sums
        seen[s] = least
        return 0

    lax.fori_loop(0, scenes, scene, 0)
    ready()

    @pl.when(jnp.min(seen[...]) < 0.0)
    def _():
        lift_table(weight, norm, table)

        def search(s, _):
            @pl.when(jnp.min(seen[s]) < 0.0)
            def _():
                def tile(t, _):
                    at = pl.ds(pl.multiple_of(t * LANES, LANES), LANES)
                    who = winner[s, at, :].astype(f32)

                    @pl.when(jnp.min(who) < 0.0)
                    def _():
                        count = counts[:, at]
                        count = jnp.sum(jnp.where(iota(count.shape, 0) == s, count, 0), axis=0, keepdims=True)
                        grad = slots[s, at, :].astype(f32)
                        shared_winners(pts.at[s, :, :, at], count, table, who, grad, share, acc, depth, channels)

                    return 0

                lax.fori_loop(0, size // LANES, tile, 0)

            return 0

        lax.fori_loop(0, scenes, search, 0)


def unlift(points, counts, weight, norm, winner, slots):
    scenes, feats, depth, size = points.shape
    channels = weight.shape[1]
    full = (feats + 2) * PACK
    inputs = (points, counts, weight, norm, winner, slots)
    small = (1, 2, 3)
    return pl.pallas_call(
        functools.partial(own_copies, unlift_body, small),
        in_specs=hbm(6),
        out_specs=vmem(2),
        out_shape=[
            jax.ShapeDtypeStruct((feats * PACK, LANES), f32),
            jax.ShapeDtypeStruct((8, LANES), f32),
        ],
        scratch_shapes=[
            pltpu.VMEM((full, PACK * channels), bf16),
            pltpu.VMEM(points.shape, bf16),
            pltpu.VMEM((scenes, size, LANES), bf16),
            pltpu.VMEM(slots.shape, bf16),
            pltpu.VMEM((LANES, LANES), f32),
            pltpu.VMEM((scenes, 8, LANES), f32),
            pltpu.SemaphoreType.DMA((3, scenes)),
        ]
        + places_of(inputs, small),
        cost_estimate=pl.CostEstimate(flops=40_000_000_000, bytes_accessed=16_000_000, transcendentals=0),
        name="unlift",
    )(*inputs)


def edges_body(
    devices, parts, pts, counts, weight, norm, winner, edge, far, moments, inner, inner_bias, kgrad, payload,
    table, acc, bias, share_of,
):
    feats, channels = weight.shape
    scenes, _, depth, _ = pts.shape
    rows = feats * PACK
    size = pts.shape[3]
    peers = payload.shape[0]
    share = kgrad.shape[1]
    for r in range(devices):
        row = kgrad[r : r + 1, :]
        for q in range(1, parts):
            row = row + kgrad[q * devices + r : q * devices + r + 1, :]
        each = peers // devices
        payload[r * each : (r + 1) * each, :, :share] = jnp.broadcast_to(row[:, None, :], (each, 1, share))

    lower = iota((EDGE, LANES), 1) < channels

    def whole(s):
        rows_of = edge_rows_of(edge, s, scenes, lower) + edge_rows_of(far, s, scenes, lower)
        return rows_of.astype(bf16).astype(f32)

    def padded(grad):
        return jnp.concatenate([grad, jnp.zeros((size - EDGE, LANES), f32)], axis=0)

    total, sums = inner[...], inner_bias[...]
    for s in range(scenes):
        grad = whole(s)
        sums = sums + jnp.sum(grad.reshape(EDGE // 8, 8, LANES), axis=0)
        x = [pts[s, :, part * PACK : (part + 1) * PACK, :].reshape(rows, size) for part in range(depth // PACK)]
        total = total + single_winners(x, winner[s], padded(grad), channels)
    acc[...] = total
    bias[...] = sums

    @pl.when(jnp.min(winner[:, :EDGE, :].astype(f32)) < 0.0)
    def _():
        lift_table(weight, norm, table)

        def scene(s, _):
            @pl.when(jnp.min(winner[s, :EDGE, :].astype(f32)) < 0.0)
            def _():
                count = counts[pl.ds(s, 1), :][:, :size]
                who = winner[s].astype(f32)
                grad = padded(whole(s))
                shared_winners(pts.at[s], count, table, who, grad, share_of, acc, depth, channels)

            return 0

        lax.fori_loop(0, scenes, scene, 0)

    out = exact_right(one_hot_cols(16, rows), acc[...])
    out = out + swap_halves(out)
    pieces = [out[i : i + 1, :channels] for i in range(feats)]
    pieces.append(jnp.sum(bias[...], axis=0, keepdims=True)[:, :channels])
    pieces += [moments[i : i + 1, :16] for i in range(feats + 1)]
    width = (feats + 1) * (channels + 16)
    pieces.append(jnp.zeros((1, payload.shape[2] - share - width), f32))
    row = jnp.concatenate(pieces, axis=1)
    payload[:, :, share:] = jnp.broadcast_to(row[:, None, :], (peers, 1, row.shape[1]))


def unlift_edges(devices, parts, peers, points, counts, weight, norm, winner, edge, far, moments, inner, bias, kgrad):
    scenes, feats, depth, _ = points.shape
    channels = weight.shape[1]
    full = (feats + 2) * PACK
    width = -(-(feats + 1) * (channels + 16) // LANES) * LANES
    return pl.pallas_call(
        functools.partial(edges_body, devices, parts),
        grid=(1,),
        in_specs=[
            pl.BlockSpec((scenes, feats, depth, LANES), lambda i: (0, 0, 0, 0)),
            pl.BlockSpec(counts.shape, lambda i: (0, 0)),
            pl.BlockSpec(weight.shape, lambda i: (0, 0)),
            pl.BlockSpec(norm.shape, lambda i: (0, 0)),
            pl.BlockSpec((scenes, LANES, LANES), lambda i: (0, 0, 0)),
        ]
        + [pl.BlockSpec(x.shape, lambda i: (0, 0)) for x in (edge, far, moments, inner, bias, kgrad)],
        out_specs=pl.BlockSpec((peers, 1, kgrad.shape[1] + width), lambda i: (0, 0, 0)),
        out_shape=jax.ShapeDtypeStruct((peers, 1, kgrad.shape[1] + width), f32),
        scratch_shapes=[
            pltpu.VMEM((full, PACK * channels), bf16),
            pltpu.VMEM((feats * PACK, LANES), f32),
            pltpu.VMEM((8, LANES), f32),
            pltpu.VMEM((LANES, LANES), f32),
        ],
        name="edges",
    )(points, counts, weight, norm, winner, edge, far, moments, inner, bias, kgrad)


def adam(fixes, w, states, grad, rate):
    moment = beta_one * states[0] + (1.0 - beta_one) * grad
    second = beta_two * states[1] + (1.0 - beta_two) * grad * grad
    new = w - rate * (moment / fixes[0] / (jnp.sqrt(second / fixes[1]) + adam_eps) + decay_rate * w)
    return new, moment, second, average_keep * states[2] + (1.0 - average_keep) * new


def step_body(devices, parts, fix, got, sums, weight, norm, pm, ps, nm, ns, km, ks, *refs):
    p_new, p_states, p_avg, p_copy, n_new, n_states, n_avg, n_copy, k_new, k_states, k_avg, k_copy, kgrad = refs
    feats, channels = weight.shape
    own = km.shape[1]
    share = own // parts
    peers = got.shape[0]
    scenes = peers // devices
    fixes = (fix[0], fix[1])

    width = share * channels
    kgrad[...] = jnp.zeros_like(kgrad)
    for q in range(parts):
        tot = got[q, :, :width]
        for r in range(1, devices):
            tot = tot + got[r * scenes + q, :, :width]
        for j in range(share):
            kgrad[q * share + j : q * share + j + 1, :channels] = tot[:, j * channels : (j + 1) * channels]
    grad = jnp.transpose(kgrad[...])[:channels, :own]
    new, moment, second, average = adam(fixes, km[...], (ks[0], ks[1], ks[2]), grad, rate_kernel)
    k_new[...] = new
    k_states[0] = moment
    k_states[1] = second
    k_avg[...] = average
    k_copy[...] = new.astype(bf16)

    row = jnp.sum(got[:, :, width:], axis=0)
    cross = jnp.concatenate([row[:, i * channels : (i + 1) * channels] for i in range(feats + 1)], axis=0)
    base = (feats + 1) * channels
    moments = jnp.concatenate([row[:, base + i * 16 : base + (i + 1) * 16] for i in range(feats + 1)], axis=0)
    w = weight[...].astype(f32)
    nw = norm[...].astype(f32)
    total = moments[feats : feats + 1, feats : feats + 1]
    firsts = moments[:feats, feats : feats + 1]
    mixed = None
    first_sum = None
    for i in range(feats):
        part = moments[:feats, i : i + 1] * w[i : i + 1]
        mixed = part if mixed is None else mixed + part
        part = moments[feats : feats + 1, i : i + 1] * w[i : i + 1]
        first_sum = part if first_sum is None else first_sum + part
    mean = first_sum / total
    inv = lax.rsqrt(jnp.sum(mixed * w, axis=0, keepdims=True) / total - mean * mean + norm_eps)
    bias_p = cross[feats : feats + 1]
    gain_p = inv * (jnp.sum(w * cross[:feats], axis=0, keepdims=True) - mean * bias_p)
    spread = inv * (mixed - firsts * mean)
    point_grad = (nw[0:1] * inv) * (cross[:feats] - (firsts * bias_p + spread * gain_p) / total)
    states = (ps[:, 0, :], ps[:, 1, :], ps[:, 2, :])
    new, moment, second, average = adam(fixes, pm[...], states, point_grad, rate_points)
    p_new[...] = new
    p_states[:, 0, :] = moment
    p_states[:, 1, :] = second
    p_avg[...] = average
    p_copy[...] = new.astype(bf16)

    both = jnp.sum(sums[...], axis=0)
    norm_grad = jnp.concatenate([gain_p, bias_p, both[:, channels:], both[:, :channels]], axis=0)
    new, moment, second, average = adam(fixes, nm[...], (ns[0], ns[1], ns[2]), norm_grad, rate_norms)
    n_new[...] = new
    n_states[0] = moment
    n_states[1] = second
    n_avg[...] = average
    n_copy[...] = new.astype(bf16)


def update(devices, parts, fix, got, sums, weight, norm, pm, ps, nm, ns, km, ks):
    feats, channels = weight.shape
    shapes = []
    for m, states in ((pm, (feats, 2, channels)), (nm, (2,) + nm.shape), (km, (2,) + km.shape)):
        shapes.append(jax.ShapeDtypeStruct(m.shape, f32))
        shapes.append(jax.ShapeDtypeStruct(states, f32))
        shapes.append(jax.ShapeDtypeStruct(m.shape, f32))
        shapes.append(jax.ShapeDtypeStruct(m.shape, bf16))
    return pl.pallas_call(
        functools.partial(step_body, devices, parts),
        in_specs=smem(1) + vmem(10),
        out_specs=vmem(12),
        out_shape=shapes,
        scratch_shapes=[pltpu.VMEM((LANES, LANES), f32)],
        name="update",
    )(fix, got, sums, weight, norm, pm, ps, nm, ns, km, ks)


def shifted(x, by):
    length = lax.axis_size("rows")
    pairs = [(i, i + by) for i in range(length) if 0 <= i + by < length]
    return lax.ppermute(x, "rows", pairs)


def exchange(x):
    return lax.all_to_all(x, ("rows", "scene"), 0, 0, tiled=True)


def body(
    points,
    pillar_counts,
    pillar_pixels,
    point_weight,
    point_master,
    point_states,
    norm_weight,
    norm_master,
    norm_states,
    kernel_weight,
    kernel_master,
    kernel_states,
    step_count,
    cotangent,
):
    size = points.shape[3]
    out_rows, scenes, channels, out_cols = cotangent.shape
    cols = 2 * out_cols
    devices = lax.axis_size("rows")
    scene_devices = lax.axis_size("scene")
    peers = devices * scene_devices
    cells = float(out_rows * scenes * out_cols * peers)
    own = kernel_weight.shape[0]
    parts = scene_devices if own % scene_devices == 0 else 1
    share = own // parts * channels
    mine = lax.axis_index("scene") if parts > 1 else jnp.int32(0)

    z, winner, edge, stats, moments = lift(
        mine.reshape(1, 1), points, pillar_counts, pillar_pixels, point_weight, norm_weight, kernel_weight.T, peers, share
    )
    edge = shifted(edge, 1)
    got = exchange(stats)
    held = scenes // 2 * EDGE
    far_pixels = edge[held : held + scenes].astype(jnp.int32)
    pairs = out_rows // 2
    own_pixels = pillar_pixels.reshape(scenes * pairs, 1, size // pairs)
    conv, pooled, sums, kernel = convolve(
        devices, parts, own_pixels, far_pixels, got, z, edge, norm_weight, pairs, out_cols
    )
    conv_stats = exchange(sums[:, None])

    far_pixels = far_pixels[:, :EDGE]
    at = (pillar_pixels % cols) // 2
    own_at = (pillar_pixels // (2 * cols) + 1) * (out_cols + 8) + at
    take_at = jnp.concatenate([own_at, (far_pixels % cols) // 2], axis=1)
    take_at = jnp.pad(take_at, ((0, 0), (0, -(size + EDGE) % (16 * pairs))))
    take_at = take_at.reshape(scenes * pairs, 1, take_at.shape[1] // pairs)
    own_phase = (pillar_pixels // cols % 2) * 2 + pillar_pixels % 2
    phase = jnp.concatenate([own_phase, 2 + far_pixels % 2], axis=1)
    phase = jnp.pad(phase, ((0, 0), (0, LANES - EDGE))).astype(f32)[:, None]

    result, sums = normalize(cells, conv_stats, conv, cotangent, norm_weight)
    grad_sums = exchange(sums[:, None])
    slots, own_edge, far, kgrad = gradients(
        cells, devices, parts, take_at, conv_stats, grad_sums, conv, cotangent, norm_weight, pooled, phase, kernel
    )
    far = shifted(far, -1)
    if parts > 1:
        kgrad = lax.all_to_all(kgrad, "scene", 0, 0, tiled=True)
    else:
        kgrad = lax.psum(kgrad, "scene")
    inner, bias = unlift(points, pillar_counts, point_weight, norm_weight, winner, slots)
    far, kgrad, inner, bias = lax.optimization_barrier((far, kgrad, inner, bias))
    payload = unlift_edges(
        devices, parts, peers, points, pillar_counts, point_weight, norm_weight, winner, own_edge, far, moments, inner, bias, kgrad
    )
    got = exchange(payload)
    steps_done = step_count[0].astype(f32)
    fix = jnp.stack([1.0 - beta_one**steps_done, 1.0 - beta_two**steps_done])
    outs = update(
        devices,
        parts,
        fix,
        got,
        grad_sums,
        point_weight,
        norm_weight,
        point_master,
        jnp.transpose(point_states, (1, 0, 2)),
        norm_master,
        norm_states,
        kernel_master.T,
        jnp.transpose(kernel_states, (0, 2, 1)),
    )
    outs = list(outs)
    outs[1] = jnp.transpose(outs[1], (1, 0, 2))
    outs[8], outs[10], outs[11] = outs[8].T, outs[10].T, outs[11].T
    outs[9] = jnp.transpose(outs[9], (0, 2, 1))
    return (result, *outs)


def solution(mesh):
    placed = (
        P("scene", None, None, "rows"),
        P("scene", "rows"),
        P("scene", "rows"),
        P(),
        P(),
        P(),
        P(),
        P(),
        P(),
        P("rows", None),
        P("rows", None),
        P(None, "rows", None),
        P(),
        P("rows", "scene", None, None),
    )
    return jax.shard_map(
        body,
        mesh=mesh,
        in_specs=placed,
        out_specs=(
            P("rows", "scene", None, None),
            P(),
            P(),
            P(),
            P(),
            P(),
            P(),
            P(),
            P(),
            P("rows", None),
            P(None, "rows", None),
            P("rows", None),
            P("rows", None),
        ),
        check_vma=False,
    )
```

```python
import functools

import jax
import jax.numpy as jnp
from jax import lax
from jax.experimental import pallas as pl
from jax.experimental.pallas import tpu as pltpu
from jax.sharding import PartitionSpec as P

beta_one = 0.9
beta_two = 0.999
adam_eps = 1e-08
decay_rate = 0.01
average_keep = 0.99
norm_eps = 1e-05
rate_points = 0.3
rate_norms = 0.2
rate_kernel = 0.04

EDGE = 48
BIG = 1e30
PACK = 8
ROWS = 128
TILE = 256
LANES = 128
f32 = jnp.float32
bf16 = jnp.bfloat16


def iota(shape, dim):
    return lax.broadcasted_iota(jnp.int32, shape, dim)


def dot_nn(a, b):
    return lax.dot_general(a, b, (((1,), (0,)), ((), ())), preferred_element_type=f32)


def dot_nt(a, b):
    return lax.dot_general(a, b, (((1,), (1,)), ((), ())), preferred_element_type=f32)


def dot_tn(a, b):
    return lax.dot_general(a, b, (((0,), (0,)), ((), ())), preferred_element_type=f32)


def split3(x):
    a = x.astype(bf16)
    r = x - a.astype(f32)
    b = r.astype(bf16)
    c = (r - b.astype(f32)).astype(bf16)
    return a, b, c


def exact_left(x, y):
    a, b, c = split3(x)
    return dot_nn(a, y) + (dot_nn(b, y) + dot_nn(c, y))


def exact_right(x, y):
    a, b, c = split3(y)
    return dot_nn(x, a) + (dot_nn(x, b) + dot_nn(x, c))


def swap_halves(x):
    return pltpu.roll(x, x.shape[1] // 2, axis=1)


def twice(row):
    return jnp.concatenate([row, row], axis=1)


def one_hot_rows(rows, cols):
    return (iota((rows, cols), 0) // PACK == iota((rows, cols), 1)).astype(f32).astype(bf16)


def one_hot_cols(rows, cols):
    return (iota((rows, cols), 1) // PACK == iota((rows, cols), 0)).astype(f32).astype(bf16)


def lift_table(weight, norm, table):
    feats, channels = weight.shape
    rows = table.shape[0]
    gain = norm[0:1, :].astype(f32)
    sign = jnp.where(gain > 0, 1.0, jnp.where(gain < 0, -1.0, 0.0))
    signed = weight[...].astype(f32) * sign
    full = jnp.concatenate([signed, jnp.zeros((1, channels), f32), jnp.ones((1, channels), f32)], axis=0)
    full = jnp.concatenate([full, jnp.zeros((16 - feats - 2, channels), f32)], axis=0)
    base = dot_nn(one_hot_rows(rows, 16), twice(full).astype(bf16))
    slot = iota(base.shape, 0) % PACK
    half = iota(base.shape, 1) // channels
    for m in range(PACK // 2):
        table[:, m * LANES : (m + 1) * LANES] = jnp.where(slot == 2 * m + half, base, 0.0).astype(bf16)


def lift_inputs(pts, count, part):
    feats, _, size = pts.shape
    live = (iota((PACK, size), 0) + part * PACK < count).astype(f32)
    low = live.astype(bf16)
    dead = ((live - 1.0) * BIG).astype(bf16)
    full = jnp.concatenate([pts.reshape(feats * PACK, size), low, dead], axis=0)
    kept = jnp.concatenate([(pts * low[None]).reshape(feats * PACK, size), low], axis=0)
    return full, kept


def copy_in(source, target, sems, s):
    return pltpu.make_async_copy(source.at[s], target.at[s], sems.at[s])


def half_store(block, s, scenes, value):
    channels = LANES // 2
    spot = pl.ds(pl.multiple_of((s % (scenes // 2)) * EDGE, 8), EDGE)
    lower = iota((EDGE, LANES), 1) < channels
    block[spot, :] = jnp.where(lower == (s < scenes // 2), value, block[spot, :])


def lift_body(
    mine, points, counts, pixels, weight, norm, kernel, z_out, winner_out, edge, payload, moments,
    table, gram, wide, pts, z, winner, low, high, sems,
):
    feats, channels = weight.shape
    scenes, _, depth, size = points.shape
    rows = (feats + 1) * PACK
    for s in range(scenes):
        copy_in(points, pts, sems.at[0], s).start()
    lift_table(weight, norm, table)
    gram[...] = jnp.zeros_like(gram)
    edge[...] = jnp.zeros_like(edge)

    def scene(s, _):
        copy_in(points, pts, sems.at[0], s).wait()
        count = counts[pl.ds(s, 1), :]
        total = None
        inputs = []
        for part in range(depth // PACK):
            xin, kept = lift_inputs(pts[s, :, part * PACK : (part + 1) * PACK, :], count, part)
            prod = dot_nt(kept, xin[:rows])
            total = prod if total is None else total + prod
            inputs.append(xin)
        for t in range(size // LANES):
            turned = [jnp.transpose(x[:, t * LANES : (t + 1) * LANES]) for x in inputs]
            for h in range(LANES // ROWS):
                at = slice(t * LANES + h * ROWS, t * LANES + (h + 1) * ROWS)
                best = None
                for part in range(depth // PACK):
                    lhs = turned[part][h * ROWS : (h + 1) * ROWS]
                    for q in range(PACK // 4):
                        l = dot_nn(lhs, table[:, q * 256 : (q + 1) * 256])
                        for k, piece in enumerate((l[:, :LANES], l[:, LANES:])):
                            n = jnp.full((ROWS, LANES), float(part * PACK + q * 4 + 2 * k), f32)
                            if best is None:
                                first = n
                                high[at, :] = n
                                best = piece
                            else:
                                first = jnp.where(piece > best, n, first)
                                pltpu.store(high.at[at, :], n, mask=piece >= best)
                                best = jnp.maximum(best, piece)
                last = high[at, :]
                upper = (iota((ROWS, LANES), 1) >= channels).astype(f32)
                first, last = first + upper, last + upper
                other = swap_halves(best)
                first = jnp.where(other > best, swap_halves(first), first)
                last = jnp.where(other >= best, swap_halves(last), last)
                best = jnp.maximum(best, other)
                only = jnp.where(first == last, first, -1.0)
                winner[s, at, :] = jnp.where(best > -0.5 * BIG, only, 99.0).astype(bf16)
                z[s, at, :] = best
        gram[...] += total
        copy_in(z, z_out, sems.at[1], s).start()
        copy_in(winner, winner_out, sems.at[2], s).start()
        half_store(edge, s, scenes, z[s, :EDGE, :])
        return 0

    lax.fori_loop(0, scenes, scene, 0)

    count_rows = edge.shape[0] - 2 * scenes
    edge[count_rows : count_rows + scenes, :] = pixels[:, :LANES].astype(f32)
    edge[count_rows + scenes :, :] = jnp.ones((scenes, LANES), f32)
    g = gram[...]
    g = jnp.where(iota(g.shape, 0) % PACK == iota(g.shape, 1) % PACK, g, 0.0)
    y = exact_left(g, one_hot_rows(rows, LANES))
    m = exact_right(one_hot_cols(16, rows), y)
    moments[...] = m
    w = jnp.concatenate([weight[...].astype(f32), jnp.zeros((16 - feats, channels), f32)], axis=0)
    aw = exact_left(m[:, :16], w.astype(bf16))
    two = jnp.sum(aw * w, axis=0, keepdims=True)
    one = aw[feats : feats + 1]
    own = kernel.shape[1]
    flat = jnp.concatenate([kernel[...].astype(f32), jnp.zeros((channels, LANES - own), f32)], axis=1)
    wide[...] = jnp.transpose(jnp.concatenate([flat, jnp.zeros((LANES - channels, LANES), f32)], axis=0))
    pieces = [one, two, m[feats : feats + 1]]
    share = (payload.shape[2] - 256) // channels
    for j in range(share):
        pieces.append(wide[pl.ds(mine[0, 0] * share + j, 1), :channels])
    row = jnp.concatenate(pieces, axis=1)
    payload[...] = jnp.broadcast_to(row[:, None, :], payload.shape)
    for s in range(scenes):
        copy_in(z, z_out, sems.at[1], s).wait()
        copy_in(winner, winner_out, sems.at[2], s).wait()


def vmem(count):
    return [pl.BlockSpec(memory_space=pltpu.VMEM)] * count


def smem(count):
    return [pl.BlockSpec(memory_space=pltpu.SMEM)] * count


def own_copies(body, small, *refs):
    refs = list(refs)
    count = len(small)
    places, sems = refs[-count - 1 : -1], refs[-1]
    refs = refs[: -count - 1]
    copies = []
    for i, (at, place) in enumerate(zip(small, places)):
        copies.append(pltpu.make_async_copy(refs[at], place, sems.at[i]))
        refs[at] = place
    for copy in copies:
        copy.start()

    def ready():
        for copy in copies:
            copy.wait()

    body(ready, *refs)


def places_of(inputs, small):
    return [pltpu.VMEM(inputs[at].shape, inputs[at].dtype) for at in small] + [pltpu.SemaphoreType.DMA((len(small),))]


def hbm(count):
    return [pl.BlockSpec(memory_space=pltpu.HBM)] * count


def lift(mine, points, counts, pixels, weight, norm, kernel, peers, share):
    scenes, feats, depth, size = points.shape
    channels = weight.shape[1]
    full = (feats + 2) * PACK
    rows = (feats + 1) * PACK
    edge_rows = scenes // 2 * EDGE + 2 * scenes
    return pl.pallas_call(
        lift_body,
        in_specs=smem(1) + hbm(1) + vmem(5),
        out_specs=hbm(2) + vmem(3),
        out_shape=[
            jax.ShapeDtypeStruct((scenes, size, LANES), f32),
            jax.ShapeDtypeStruct((scenes, size, LANES), bf16),
            jax.ShapeDtypeStruct((edge_rows, LANES), f32),
            jax.ShapeDtypeStruct((peers, 1, 256 + share), f32),
            jax.ShapeDtypeStruct((16, LANES), f32),
        ],
        scratch_shapes=[
            pltpu.VMEM((full, PACK * channels), bf16),
            pltpu.VMEM((rows, rows), f32),
            pltpu.VMEM((LANES, LANES), f32),
            pltpu.VMEM(points.shape, bf16),
            pltpu.VMEM((scenes, size, LANES), f32),
            pltpu.VMEM((scenes, size, LANES), bf16),
            pltpu.VMEM((size, LANES), f32),
            pltpu.VMEM((size, LANES), f32),
            pltpu.SemaphoreType.DMA((3, scenes)),
        ],
        name="lift",
    )(mine, points, counts, pixels, weight, norm, kernel)


def gather_kernel(got, kern, devices, parts):
    channels = kern.shape[1]
    share = kern.shape[0] // devices // parts
    peers = got.shape[0]
    for j in range(share):
        rows = got[:, 0, 256 + j * channels : 256 + (j + 1) * channels]
        if parts > 1:
            kern[pl.ds(j, peers, stride=share), :] = rows
        else:
            for r in range(devices):
                at = r * (peers // devices)
                kern[r * share + j : r * share + j + 1, :] = rows[at : at + 1]


def tap(kern, a, b):
    channels = kern.shape[1]
    if a is None or b is None:
        return jnp.zeros((channels, channels), f32)
    return kern[(3 * a + b) * channels : (3 * a + b + 1) * channels, :]


def edge_rows_of(block, s, scenes, lower):
    base = (s % (scenes // 2)) * EDGE
    spot = pl.ds(base if isinstance(base, int) else pl.multiple_of(base, 8), EDGE)
    rows = jnp.where(lower == (s < scenes // 2), block[spot, :], 0.0)
    return rows + swap_halves(rows)


def conv_body(
    devices, parts, pix, far_pix, got, z_in, edge, norm, conv_out, pooled_out, sums, kernel,
    params, source, kern, taps, grid_a, grid_b, side, acc, z, conv, pooled, sems,
):
    scenes, size, _ = z.shape
    for s in range(scenes):
        copy_in(z_in, z, sems.at[0], s).start()
    channels = norm.shape[1]
    _, pairs, out_cols, _ = conv.shape
    cols = 2 * out_cols
    last_row = (4 * pairs - 1) * cols
    tot = jnp.sum(got[:, :, :256], axis=0)
    count = tot[:, 2 * channels + 9 : 2 * channels + 10]
    mean = tot[:, :channels] / count
    inv = lax.rsqrt(tot[:, channels : 2 * channels] / count - mean * mean + norm_eps)
    nw = norm[...].astype(f32)
    gain = nw[0:1]
    sign = jnp.where(gain > 0, 1.0, jnp.where(gain < 0, -1.0, 0.0))
    params[0:1] = twice(mean)
    params[1:2] = twice(inv)
    params[2:3] = twice(gain)
    params[3:4] = twice(nw[1:2])
    params[4:5] = twice(sign)
    gather_kernel(got, kern, devices, parts)
    kernel[...] = kern[...].astype(bf16)
    for w, (low, high) in enumerate(((0, None), (1, None), (2, 0), (None, 1), (None, 2))):
        none = tap(kern, None, None)
        top = jnp.concatenate([tap(kern, low, 1), tap(kern, high, 1), none, none], axis=1)
        end = jnp.concatenate([tap(kern, low, 2), tap(kern, high, 2), tap(kern, low, 0), tap(kern, high, 0)], axis=1)
        taps[w] = jnp.concatenate([top, end], axis=0).astype(bf16)
    grid_a[...] = jnp.zeros_like(grid_a)
    side[...] = jnp.zeros_like(side)
    acc[...] = jnp.zeros_like(acc)

    def pool(x, ok):
        pre = params[2:3] * ((x * params[4:5] - params[0:1]) * params[1:2]) + params[3:4]
        return jnp.where(ok, jnp.maximum(pre, 0.0), 0.0).astype(bf16)

    own_at = 8 + cols
    far_at = 8 - last_row
    some = size // pairs

    def part_of(j):
        return pl.ds(j * some if isinstance(j, int) else pl.multiple_of(j * some, 16), some)

    def fill(s, j):
        zs = z[s, part_of(j), :]
        own = pool(zs, zs > -0.5 * BIG)
        pooled[s, part_of(j), :] = own
        source[part_of(j), :] = own.astype(f32)

    def fill_far(dst, s):
        far = edge_rows_of(edge, s, scenes, iota((EDGE, LANES), 1) < channels)
        flag = edge[edge.shape[0] - scenes : edge.shape[0] - scenes + 1, :]
        far = pool(far, (far > -0.5 * BIG) & (flag > 0.5))
        pooled[s, size:] = jnp.concatenate([far, jnp.zeros((LANES - EDGE, LANES), bf16)], axis=0)
        source[size : size + EDGE] = far.astype(f32)
        for p in range(EDGE):
            at = jnp.maximum(far_pix[s, p], last_row) + far_at
            dst[pl.ds(at, 1), :] = source[size + p : size + p + 1, :]

    def place(dst, s, j):
        rows = dst.at[pl.ds(own_at, 4 * pairs * cols), :]
        line = pix.at[s * pairs + j]
        values = source.at[part_of(j), :]
        for p in range(some):
            rows[pl.ds(line[0, p], 1), :] = values[p : p + 1, :]

    left = iota((out_cols, LANES), 1) < channels

    def convolve_pair(src, s, j):
        out = None
        for w in range(5):
            base = 8 + (4 * j + w) * cols
            even = src[pl.ds(base, out_cols, stride=2), :]
            odd = src[pl.ds(base + 1, out_cols, stride=2), :]
            part = dot_nn(jnp.where(left, even, odd).astype(bf16), taps[w])
            out = part if out is None else out + part
        side[8:, :] = out[:, LANES:]
        value = out[:, :LANES] + side[7 : 7 + out_cols, :]
        conv[s, j] = value
        acc[0:8] += jnp.sum(value.reshape(out_cols // 8, 8, LANES), axis=0)
        acc[8:16] += jnp.sum((value * value).reshape(out_cols // 8, 8, LANES), axis=0)
        used = (5 if j == pairs - 1 else 4) * cols
        base = 8 + 4 * j * cols
        src[base : base + used, :] = jnp.zeros((used, LANES), f32)

    copy_in(z_in, z, sems.at[0], 0).wait()
    fill_far(grid_a, 0)
    grid_b[:8, :] = jnp.zeros((8, LANES), f32)
    grid_b[8 + 4 * pairs * cols :, :] = jnp.zeros((grid_b.shape[0] - 8 - 4 * pairs * cols, LANES), f32)

    def start(j, _):
        grid_b[pl.ds(pl.multiple_of(8 + 4 * j * cols, 8), 4 * cols), :] = jnp.zeros((4 * cols, LANES), f32)
        fill(0, j)
        place(grid_a, 0, j)
        return 0

    lax.fori_loop(0, pairs, start, 0)

    def two_scenes(i, _):
        for k, (src, dst) in enumerate(((grid_a, grid_b), (grid_b, grid_a))):
            s = 2 * i + k
            ahead = jnp.minimum(s + 1, scenes - 1)

            @pl.when(s + 1 < scenes)
            def _():
                copy_in(z_in, z, sems.at[0], s + 1).wait()

            fill_far(dst, ahead)
            for j in range(pairs):
                fill(ahead, j)
                place(dst, ahead, j)
                convolve_pair(src, s, j)

            copy_in(conv, conv_out, sems.at[1], s).start()
            copy_in(pooled, pooled_out, sems.at[2], s).start()
        return 0

    lax.fori_loop(0, scenes // 2, two_scenes, 0)
    for s in range(scenes):
        copy_in(conv, conv_out, sems.at[1], s).wait()
        copy_in(pooled, pooled_out, sems.at[2], s).wait()
    sums[...] = jnp.broadcast_to(both_sums(acc, channels), sums.shape)


def both_sums(acc, channels):
    one = jnp.sum(acc[0:8], axis=0, keepdims=True)
    two = jnp.sum(acc[8:16], axis=0, keepdims=True)
    one = one + swap_halves(one)
    two = two + swap_halves(two)
    return jnp.where(iota((1, LANES), 1) < channels, one, two)


def convolve(devices, parts, pix, far_pix, got, z, edge, norm, pairs, out_cols):
    scenes, size, _ = z.shape
    peers = got.shape[0]
    channels = norm.shape[1]
    cells = 8 + (4 * pairs + 1) * 2 * out_cols + 8
    return pl.pallas_call(
        functools.partial(conv_body, devices, parts),
        in_specs=smem(2) + vmem(1) + hbm(1) + vmem(2),
        out_specs=hbm(2) + vmem(2),
        out_shape=[
            jax.ShapeDtypeStruct((scenes, pairs, out_cols, LANES), f32),
            jax.ShapeDtypeStruct((scenes, size + LANES, LANES), bf16),
            jax.ShapeDtypeStruct((peers, LANES), f32),
            jax.ShapeDtypeStruct((9 * channels, channels), bf16),
        ],
        scratch_shapes=[
            pltpu.VMEM((8, LANES), f32),
            pltpu.VMEM((size + LANES, LANES), f32),
            pltpu.VMEM((9 * channels, channels), f32),
            pltpu.VMEM((5, LANES, 2 * LANES), bf16),
            pltpu.VMEM((cells, LANES), f32),
            pltpu.VMEM((cells, LANES), f32),
            pltpu.VMEM((out_cols + 8, LANES), f32),
            pltpu.VMEM((16, LANES), f32),
            pltpu.VMEM((scenes, size, LANES), f32),
            pltpu.VMEM((scenes, pairs, out_cols, LANES), f32),
            pltpu.VMEM((scenes, size + LANES, LANES), bf16),
            pltpu.SemaphoreType.DMA((3, scenes)),
        ],
        name="convolve",
    )(pix, far_pix, got, z, edge, norm)


def split_sums(stats, channels):
    tot = jnp.sum(stats[...], axis=0)
    lower = iota((1, LANES), 1) < channels
    turned = swap_halves(tot)
    return jnp.where(lower, tot, turned), jnp.where(lower, turned, tot)


def conv_params(cells, stats, norm):
    one, two = split_sums(stats, norm.shape[1])
    mean = one / cells
    inv = lax.rsqrt(two / cells - mean * mean + norm_eps)
    nw = norm[...].astype(f32)
    return mean, inv, twice(nw[2:3]), twice(nw[3:4])


def turned_pair(block, j, k):
    _, _, channels, cols = block.shape
    return jnp.transpose(block[2 * j : 2 * j + 2, k].reshape(2 * channels, cols)).astype(f32)


def scene_copy(source, target, sems, s):
    return pltpu.make_async_copy(source.at[:, s], target.at[:, s], sems.at[s])


def norm_body(cells, stats, conv_in, cot_in, norm, result_out, sums, acc, conv, cot, result, sems):
    channels = norm.shape[1]
    scenes, pairs, out_cols, _ = conv.shape
    for s in range(scenes):
        copy_in(conv_in, conv, sems.at[0], s).start()
        scene_copy(cot_in, cot, sems.at[1], s).start()
    mean, inv, gain, bias = conv_params(cells, stats, norm)
    acc[...] = jnp.zeros_like(acc)

    def scene(k, _):
        copy_in(conv_in, conv, sems.at[0], k).wait()
        scene_copy(cot_in, cot, sems.at[1], k).wait()
        for j in range(pairs):
            xhat = (conv[k, j] - mean) * inv
            pre = gain * xhat + bias
            out = jnp.transpose(jnp.maximum(pre, 0.0).astype(bf16))
            result[2 * j : 2 * j + 2, k] = out.reshape(2, channels, out_cols)
            back = jnp.where(pre > 0, turned_pair(cot, j, k), 0.0)
            acc[0:8] += jnp.sum(back.reshape(out_cols // 8, 8, LANES), axis=0)
            acc[8:16] += jnp.sum((back * xhat).reshape(out_cols // 8, 8, LANES), axis=0)
        scene_copy(result, result_out, sems.at[2], k).start()
        return 0

    lax.fori_loop(0, scenes, scene, 0)
    sums[...] = jnp.broadcast_to(both_sums(acc, channels), sums.shape)
    for s in range(scenes):
        scene_copy(result, result_out, sems.at[2], s).wait()


def normalize(cells, stats, conv, cot, norm):
    peers = stats.shape[0]
    scenes = conv.shape[0]
    return pl.pallas_call(
        functools.partial(norm_body, cells),
        in_specs=vmem(1) + hbm(2) + vmem(1),
        out_specs=hbm(1) + vmem(1),
        out_shape=[
            jax.ShapeDtypeStruct(cot.shape, bf16),
            jax.ShapeDtypeStruct((peers, LANES), f32),
        ],
        scratch_shapes=[
            pltpu.VMEM((16, LANES), f32),
            pltpu.VMEM(conv.shape, f32),
            pltpu.VMEM(cot.shape, bf16),
            pltpu.VMEM(cot.shape, bf16),
            pltpu.SemaphoreType.DMA((3, scenes)),
        ],
        name="normalize",
    )(stats, conv, cot, norm)


def grad_body(
    cells, devices, parts, idx, stats, sums, conv_in, cot_in, norm, pooled_in, phase, kernel, slots_out, edge, far, kgrad,
    taps, field_a, field_b, taken_a, taken_b, turn, column_a, column_b, acc, rows_k, conv, cot, pooled, slots_a, slots_b, exact_a, exact_b, staged, sems,
):
    scenes, pairs, out_cols, _ = conv.shape
    channels = norm.shape[1]
    size = slots_a.shape[0]
    strip = out_cols + 8
    some = idx.shape[2]
    columns, slots, exact = (column_a, column_b), (slots_a, slots_b), (exact_a, exact_b)
    for s in range(scenes):
        copy_in(conv_in, conv, sems.at[0], s).start()
        scene_copy(cot_in, cot, sems.at[1], s).start()
        copy_in(pooled_in, pooled, sems.at[2], s).start()
    for hp in range(2):
        for up in range(2):
            line = []
            for dw in range(2):
                for dr in range(2):
                    a = ((1, None), (2, 0))[hp][dr]
                    b = ((1, None), (2, 0))[up][dw]
                    if a is None or b is None:
                        line.append(jnp.zeros((channels, channels), f32))
                    else:
                        at = (3 * a + b) * channels
                        line.append(kernel[at : at + channels, :].astype(f32))
            ph = 2 * hp + up
            taps[ph * channels : (ph + 1) * channels, :] = jnp.concatenate(line, axis=1).astype(bf16)
    for block in (field_a, field_b, taken_a, taken_b, acc):
        block[...] = jnp.zeros_like(block)

    def phases(column, s, j):
        chunks = column.shape[0] // LANES
        for c in range(j * chunks // pairs, (j + 1) * chunks // pairs):
            row = phase[s, :, c * LANES : (c + 1) * LANES]
            column[c * LANES : (c + 1) * LANES, :] = jnp.transpose(jnp.broadcast_to(row, (LANES, LANES)))

    mean, inv, gain, bias = conv_params(cells, stats, norm)
    bias_grad, gain_grad = split_sums(sums, channels)
    scale = gain * inv / cells
    left = iota((out_cols, LANES), 1) < channels
    half = (iota((some, LANES), 1) >= channels).astype(f32)

    def field(dst, s, j):
        xhat = (conv[s, j] - mean) * inv
        pre = gain * xhat + bias
        both = cot[2 * j : 2 * j + 2, s].reshape(2 * channels, out_cols)
        back = jnp.where(pre > 0, jnp.transpose(both).astype(f32), 0.0)
        grad = scale * (cells * back - bias_grad - xhat * gain_grad)
        grad = grad.astype(bf16).astype(f32)
        turned = swap_halves(grad)
        base = 2 * j * strip
        dst[base : base + out_cols, :] = jnp.where(left, turn[...], turned)
        dst[base + strip : base + strip + out_cols, :] = grad
        turn[...] = turned

    def take(dst, src, s, j):
        line = idx.at[s * pairs + j]
        for p in range(some):
            dst[2 * p : 2 * p + 2, :] = src[pl.ds(line[0, p], 2), :]

    def product(src, k, s, j):
        at = slice(j * some, (j + 1) * some)
        part = jnp.concatenate([src[pl.ds(0, some, stride=2), :], src[pl.ds(1, some, stride=2), :]], axis=1).astype(bf16)
        out = dot_nt(part, taps[...])
        ph = columns[k][at, :]
        is_even = ph == half
        is_odd = ph == half + 2.0
        value = jnp.where(is_even, out[:, :LANES], 0.0) + jnp.where(is_odd, out[:, LANES:], 0.0)
        value = value + swap_halves(value)
        pf = pooled[s, at, :].astype(f32)
        value = jnp.where(pf > 0, value, 0.0)
        exact[k][at, :] = value
        slots[k][at, :] = value.astype(bf16)
        split = jnp.concatenate([jnp.where(is_even, pf, 0.0), jnp.where(is_odd, pf, 0.0)], axis=1)
        acc[...] += dot_tn(split.astype(bf16), part)

    def copy_out(s):
        return copy_in(staged, slots_out, sems.at[3], s)

    def done(k, s):
        half_store(edge, s, scenes, exact[k][:EDGE, :])
        half_store(far, s, scenes, exact[k][size - LANES : size - LANES + EDGE, :])
        staged[s, :EDGE, :] = jnp.zeros((EDGE, LANES), bf16)
        staged[s, EDGE:, :] = slots[k][EDGE:, :]
        copy_out(s).start()

    def walk(dst, src, k, s):
        before = jnp.clip(s - 1, 0, scenes - 1)
        held = jnp.where(s > 0, s - 1, scenes)
        older = jnp.where(s > 1, s - 2, scenes)
        if dst is not None:
            copy_in(conv_in, conv, sems.at[0], s).wait()
            scene_copy(cot_in, cot, sems.at[1], s).wait()
            turn[...] = jnp.zeros_like(turn)

        @pl.when(s > 0)
        def _():
            copy_in(pooled_in, pooled, sems.at[2], before).wait()


        for j in range(pairs):
            to, of = ((taken_a, taken_b), (taken_b, taken_a))[j % 2]
            if dst is not None:
                phases(columns[k], s, j)
                field(dst, s, j)
            take(to, src, before, j)
            product(of, k if j == 0 else 1 - k, held if j > 0 else older, (j - 1) % pairs)

        @pl.when(s >= 2)
        def _():
            done(k, s - 2)

        if dst is not None:
            dst[2 * pairs * strip : 2 * pairs * strip + out_cols, :] = jnp.where(left, turn[...], 0.0)

    def two_scenes(i, _):
        walk(field_a, field_b, 0, 2 * i)
        walk(field_b, field_a, 1, 2 * i + 1)
        return 0

    far[...] = jnp.zeros_like(far)
    edge[...] = jnp.zeros_like(edge)
    for block in (column_a, column_b):
        block[...] = jnp.zeros_like(block)
    pooled[scenes] = jnp.zeros_like(pooled[scenes])
    lax.fori_loop(0, scenes // 2, two_scenes, 0)
    walk(None, field_b, 0, scenes)
    product(taken_b, 1, scenes - 1, pairs - 1)
    done(1, scenes - 1)
    for a in range(3):
        for b in range(3):
            hp, dr = ((1, 1), (0, 0), (1, 0))[a]
            up, dw = ((1, 1), (0, 0), (1, 0))[b]
            row, col = hp * 2 + up, dw * 2 + dr
            at = (3 * a + b) * channels
            rows_k[at : at + channels, :] = acc[
                row * channels : (row + 1) * channels, col * channels : (col + 1) * channels
            ]
    own = rows_k.shape[0] // devices
    share = own // parts
    for q in range(parts):
        for j in range(share):
            lanes = slice(j * channels, (j + 1) * channels)
            kgrad[q * devices : (q + 1) * devices, lanes] = rows_k[pl.ds(q * share + j, devices, stride=own), :]
    for s in range(scenes):
        copy_out(s).wait()


def gradients(cells, devices, parts, idx, stats, sums, conv, cot, norm, pooled, phase, kernel):
    scenes, pairs, out_cols, _ = conv.shape
    channels = norm.shape[1]
    rows = pooled.shape[1]
    return pl.pallas_call(
        functools.partial(grad_body, cells, devices, parts),
        in_specs=smem(1) + vmem(2) + hbm(2) + vmem(1) + hbm(1) + vmem(2),
        out_specs=hbm(1) + vmem(3),
        out_shape=[
            jax.ShapeDtypeStruct((scenes, rows, LANES), bf16),
            jax.ShapeDtypeStruct((scenes // 2 * EDGE, LANES), f32),
            jax.ShapeDtypeStruct((scenes // 2 * EDGE, LANES), f32),
            jax.ShapeDtypeStruct((parts * devices, 9 * channels * channels // devices // parts), f32),
        ],
        scratch_shapes=[
            pltpu.VMEM((4 * channels, 4 * channels), bf16),
            pltpu.VMEM(((2 * pairs + 1) * (out_cols + 8), LANES), f32),
            pltpu.VMEM(((2 * pairs + 1) * (out_cols + 8), LANES), f32),
            pltpu.VMEM((2 * idx.shape[2], LANES), f32),
            pltpu.VMEM((2 * idx.shape[2], LANES), f32),
            pltpu.VMEM((out_cols, LANES), f32),
            pltpu.VMEM((rows, LANES), f32),
            pltpu.VMEM((rows, LANES), f32),
            pltpu.VMEM((4 * channels, 4 * channels), f32),
            pltpu.VMEM((9 * channels, channels), f32),
            pltpu.VMEM(conv.shape, f32),
            pltpu.VMEM(cot.shape, bf16),
            pltpu.VMEM((scenes + 1, rows, LANES), bf16),
            pltpu.VMEM((rows, LANES), bf16),
            pltpu.VMEM((rows, LANES), bf16),
            pltpu.VMEM((rows, LANES), f32),
            pltpu.VMEM((rows, LANES), f32),
            pltpu.VMEM((scenes, rows, LANES), bf16),
            pltpu.SemaphoreType.DMA((4, scenes)),
        ],
        name="gradients",
    )(idx, stats, sums, conv, cot, norm, pooled, phase, kernel)


def fold(q, prod, channels):
    shape = (prod.shape[0], LANES)
    slot = iota(shape, 0) % PACK - 4 * q
    upper = (iota(shape, 1) >= channels).astype(jnp.int32)
    return jnp.where(slot == upper, prod[:, :LANES], 0.0) + jnp.where(slot == upper + 2, prod[:, LANES:], 0.0)


def single_winners(pts, who, grad, channels):
    size = who.shape[0]
    who = who.astype(f32) - (iota((size, LANES), 1) >= channels).astype(f32)
    total = None
    for part, x in enumerate(pts):
        for q in range(PACK // 4):
            n = part * PACK + q * 4
            one = jnp.where(who == float(n), grad, 0.0)
            two = jnp.where(who == float(n + 2), grad, 0.0)
            prod = fold(q, dot_nn(x, jnp.concatenate([one, two], axis=1).astype(bf16)), channels)
            total = prod if total is None else total + prod
    return total


def shared_winners(pts, count, table, who, grad, share, acc, depth, channels):
    feats = pts.shape[0]
    size = who.shape[0]

    def lifted(part, q):
        xin, _ = lift_inputs(pts[:, part * PACK : (part + 1) * PACK, :], count, part)
        l = dot_nn(jnp.transpose(xin), table[:, q * 256 : (q + 1) * 256])
        return xin[: feats * PACK], l[:, :LANES], l[:, LANES:]

    best = jnp.full((size, LANES), -3.0 * BIG, f32)
    times = jnp.zeros((size, LANES), f32)
    for part in range(depth // PACK):
        for q in range(PACK // 4):
            _, one, two = lifted(part, q)
            for l in (one, two):
                times = jnp.where(l > best, 1.0, jnp.where(l == best, times + 1.0, times))
                best = jnp.maximum(best, l)
    other, more = swap_halves(best), swap_halves(times)
    times = jnp.where(other > best, more, jnp.where(other == best, times + more, times))
    best = jnp.where(who < 0.0, jnp.maximum(best, other), BIG)
    share[...] = grad / times

    def add(of):
        total = None
        for part in range(depth // PACK):
            for q in range(PACK // 4):
                x, one, two = lifted(part, q)
                value = of(share[...])
                value = jnp.concatenate([jnp.where(one == best, value, 0.0), jnp.where(two == best, value, 0.0)], axis=1)
                part_sum = fold(q, dot_nn(x, value.astype(bf16)), channels)
                total = part_sum if total is None else total + part_sum
        acc[...] += total

    def rest(x):
        return x - x.astype(bf16).astype(f32)

    add(lambda x: x)

    @pl.when(jnp.max(jnp.where(who < 0.0, jnp.abs(rest(share[...])), 0.0)) > 0.0)
    def _():
        add(rest)
        add(lambda x: rest(rest(x)))


def unlift_body(
    ready, points, counts, weight, norm, winner_in, slots_in, acc, bias, table, pts, winner, slots, share, seen, sems
):
    feats, channels = weight.shape
    scenes, _, depth, size = points.shape
    rows = feats * PACK
    tiles = size // TILE
    for s in range(scenes):
        copy_in(points, pts, sems.at[0], s).start()
        copy_in(winner_in, winner, sems.at[1], s).start()
        copy_in(slots_in, slots, sems.at[2], s).start()
    acc[...] = jnp.zeros_like(acc)
    bias[...] = jnp.zeros_like(bias)

    def scene(s, _):
        copy_in(points, pts, sems.at[0], s).wait()
        copy_in(winner_in, winner, sems.at[1], s).wait()
        copy_in(slots_in, slots, sems.at[2], s).wait()
        total = None
        sums = None
        least = None
        for t in range(tiles):
            at = slice(t * TILE, (t + 1) * TILE)
            grad = slots[s, at, :].astype(f32)
            who = winner[s, at, :].astype(f32)
            one = jnp.sum(grad.reshape(TILE // 8, 8, LANES), axis=0)
            sums = one if sums is None else sums + one
            one = jnp.min(who.reshape(TILE // 8, 8, LANES), axis=0)
            least = one if least is None else jnp.minimum(least, one)
            x = [pts[s, :, part * PACK : (part + 1) * PACK, at].reshape(rows, TILE) for part in range(depth // PACK)]
            one = single_winners(x, who, grad, channels)
            total = one if total is None else total + one
        acc[...] += total
        bias[...] += sums
        seen[s] = least
        return 0

    lax.fori_loop(0, scenes, scene, 0)
    ready()

    @pl.when(jnp.min(seen[...]) < 0.0)
    def _():
        lift_table(weight, norm, table)

        def search(s, _):
            @pl.when(jnp.min(seen[s]) < 0.0)
            def _():
                def tile(t, _):
                    at = pl.ds(pl.multiple_of(t * LANES, LANES), LANES)
                    who = winner[s, at, :].astype(f32)

                    @pl.when(jnp.min(who) < 0.0)
                    def _():
                        count = counts[:, at]
                        count = jnp.sum(jnp.where(iota(count.shape, 0) == s, count, 0), axis=0, keepdims=True)
                        grad = slots[s, at, :].astype(f32)
                        shared_winners(pts.at[s, :, :, at], count, table, who, grad, share, acc, depth, channels)

                    return 0

                lax.fori_loop(0, size // LANES, tile, 0)

            return 0

        lax.fori_loop(0, scenes, search, 0)


def unlift(points, counts, weight, norm, winner, slots):
    scenes, feats, depth, size = points.shape
    channels = weight.shape[1]
    full = (feats + 2) * PACK
    inputs = (points, counts, weight, norm, winner, slots)
    small = (1, 2, 3)
    return pl.pallas_call(
        functools.partial(own_copies, unlift_body, small),
        in_specs=hbm(6),
        out_specs=vmem(2),
        out_shape=[
            jax.ShapeDtypeStruct((feats * PACK, LANES), f32),
            jax.ShapeDtypeStruct((8, LANES), f32),
        ],
        scratch_shapes=[
            pltpu.VMEM((full, PACK * channels), bf16),
            pltpu.VMEM(points.shape, bf16),
            pltpu.VMEM((scenes, size, LANES), bf16),
            pltpu.VMEM(slots.shape, bf16),
            pltpu.VMEM((LANES, LANES), f32),
            pltpu.VMEM((scenes, 8, LANES), f32),
            pltpu.SemaphoreType.DMA((3, scenes)),
        ]
        + places_of(inputs, small),
        cost_estimate=pl.CostEstimate(flops=40_000_000_000, bytes_accessed=16_000_000, transcendentals=0),
        name="unlift",
    )(*inputs)


def edges_body(
    devices, parts, pts, counts, weight, norm, winner, edge, far, moments, inner, inner_bias, kgrad, payload,
    table, acc, bias, share_of,
):
    feats, channels = weight.shape
    scenes, _, depth, _ = pts.shape
    rows = feats * PACK
    size = pts.shape[3]
    peers = payload.shape[0]
    share = kgrad.shape[1]
    for r in range(devices):
        row = kgrad[r : r + 1, :]
        for q in range(1, parts):
            row = row + kgrad[q * devices + r : q * devices + r + 1, :]
        each = peers // devices
        payload[r * each : (r + 1) * each, :, :share] = jnp.broadcast_to(row[:, None, :], (each, 1, share))

    lower = iota((EDGE, LANES), 1) < channels

    def whole(s):
        rows_of = edge_rows_of(edge, s, scenes, lower) + edge_rows_of(far, s, scenes, lower)
        return rows_of.astype(bf16).astype(f32)

    def padded(grad):
        return jnp.concatenate([grad, jnp.zeros((size - EDGE, LANES), f32)], axis=0)

    total, sums = inner[...], inner_bias[...]
    for s in range(scenes):
        grad = whole(s)
        sums = sums + jnp.sum(grad.reshape(EDGE // 8, 8, LANES), axis=0)
        x = [pts[s, :, part * PACK : (part + 1) * PACK, :].reshape(rows, size) for part in range(depth // PACK)]
        total = total + single_winners(x, winner[s], padded(grad), channels)
    acc[...] = total
    bias[...] = sums

    @pl.when(jnp.min(winner[:, :EDGE, :].astype(f32)) < 0.0)
    def _():
        lift_table(weight, norm, table)

        def scene(s, _):
            @pl.when(jnp.min(winner[s, :EDGE, :].astype(f32)) < 0.0)
            def _():
                count = counts[pl.ds(s, 1), :][:, :size]
                who = winner[s].astype(f32)
                grad = padded(whole(s))
                shared_winners(pts.at[s], count, table, who, grad, share_of, acc, depth, channels)

            return 0

        lax.fori_loop(0, scenes, scene, 0)

    out = exact_right(one_hot_cols(16, rows), acc[...])
    out = out + swap_halves(out)
    pieces = [out[i : i + 1, :channels] for i in range(feats)]
    pieces.append(jnp.sum(bias[...], axis=0, keepdims=True)[:, :channels])
    pieces += [moments[i : i + 1, :16] for i in range(feats + 1)]
    width = (feats + 1) * (channels + 16)
    pieces.append(jnp.zeros((1, payload.shape[2] - share - width), f32))
    row = jnp.concatenate(pieces, axis=1)
    payload[:, :, share:] = jnp.broadcast_to(row[:, None, :], (peers, 1, row.shape[1]))


def unlift_edges(devices, parts, peers, points, counts, weight, norm, winner, edge, far, moments, inner, bias, kgrad):
    scenes, feats, depth, _ = points.shape
    channels = weight.shape[1]
    full = (feats + 2) * PACK
    width = -(-(feats + 1) * (channels + 16) // LANES) * LANES
    return pl.pallas_call(
        functools.partial(edges_body, devices, parts),
        grid=(1,),
        in_specs=[
            pl.BlockSpec((scenes, feats, depth, LANES), lambda i: (0, 0, 0, 0)),
            pl.BlockSpec(counts.shape, lambda i: (0, 0)),
            pl.BlockSpec(weight.shape, lambda i: (0, 0)),
            pl.BlockSpec(norm.shape, lambda i: (0, 0)),
            pl.BlockSpec((scenes, LANES, LANES), lambda i: (0, 0, 0)),
        ]
        + [pl.BlockSpec(x.shape, lambda i: (0, 0)) for x in (edge, far, moments, inner, bias, kgrad)],
        out_specs=pl.BlockSpec((peers, 1, kgrad.shape[1] + width), lambda i: (0, 0, 0)),
        out_shape=jax.ShapeDtypeStruct((peers, 1, kgrad.shape[1] + width), f32),
        scratch_shapes=[
            pltpu.VMEM((full, PACK * channels), bf16),
            pltpu.VMEM((feats * PACK, LANES), f32),
            pltpu.VMEM((8, LANES), f32),
            pltpu.VMEM((LANES, LANES), f32),
        ],
        name="edges",
    )(points, counts, weight, norm, winner, edge, far, moments, inner, bias, kgrad)


def adam(fixes, w, states, grad, rate):
    moment = beta_one * states[0] + (1.0 - beta_one) * grad
    second = beta_two * states[1] + (1.0 - beta_two) * grad * grad
    new = w - rate * (moment / fixes[0] / (jnp.sqrt(second / fixes[1]) + adam_eps) + decay_rate * w)
    return new, moment, second, average_keep * states[2] + (1.0 - average_keep) * new


def step_body(devices, parts, fix, got, sums, weight, norm, pm, ps, nm, ns, km, ks, *refs):
    p_new, p_states, p_avg, p_copy, n_new, n_states, n_avg, n_copy, k_new, k_states, k_avg, k_copy, kgrad = refs
    feats, channels = weight.shape
    own = km.shape[1]
    share = own // parts
    peers = got.shape[0]
    scenes = peers // devices
    fixes = (fix[0], fix[1])

    width = share * channels
    kgrad[...] = jnp.zeros_like(kgrad)
    for q in range(parts):
        tot = got[q, :, :width]
        for r in range(1, devices):
            tot = tot + got[r * scenes + q, :, :width]
        for j in range(share):
            kgrad[q * share + j : q * share + j + 1, :channels] = tot[:, j * channels : (j + 1) * channels]
    grad = jnp.transpose(kgrad[...])[:channels, :own]
    new, moment, second, average = adam(fixes, km[...], (ks[0], ks[1], ks[2]), grad, rate_kernel)
    k_new[...] = new
    k_states[0] = moment
    k_states[1] = second
    k_avg[...] = average
    k_copy[...] = new.astype(bf16)

    row = jnp.sum(got[:, :, width:], axis=0)
    cross = jnp.concatenate([row[:, i * channels : (i + 1) * channels] for i in range(feats + 1)], axis=0)
    base = (feats + 1) * channels
    moments = jnp.concatenate([row[:, base + i * 16 : base + (i + 1) * 16] for i in range(feats + 1)], axis=0)
    w = weight[...].astype(f32)
    nw = norm[...].astype(f32)
    total = moments[feats : feats + 1, feats : feats + 1]
    firsts = moments[:feats, feats : feats + 1]
    mixed = None
    first_sum = None
    for i in range(feats):
        part = moments[:feats, i : i + 1] * w[i : i + 1]
        mixed = part if mixed is None else mixed + part
        part = moments[feats : feats + 1, i : i + 1] * w[i : i + 1]
        first_sum = part if first_sum is None else first_sum + part
    mean = first_sum / total
    inv = lax.rsqrt(jnp.sum(mixed * w, axis=0, keepdims=True) / total - mean * mean + norm_eps)
    bias_p = cross[feats : feats + 1]
    gain_p = inv * (jnp.sum(w * cross[:feats], axis=0, keepdims=True) - mean * bias_p)
    spread = inv * (mixed - firsts * mean)
    point_grad = (nw[0:1] * inv) * (cross[:feats] - (firsts * bias_p + spread * gain_p) / total)
    states = (ps[:, 0, :], ps[:, 1, :], ps[:, 2, :])
    new, moment, second, average = adam(fixes, pm[...], states, point_grad, rate_points)
    p_new[...] = new
    p_states[:, 0, :] = moment
    p_states[:, 1, :] = second
    p_avg[...] = average
    p_copy[...] = new.astype(bf16)

    both = jnp.sum(sums[...], axis=0)
    norm_grad = jnp.concatenate([gain_p, bias_p, both[:, channels:], both[:, :channels]], axis=0)
    new, moment, second, average = adam(fixes, nm[...], (ns[0], ns[1], ns[2]), norm_grad, rate_norms)
    n_new[...] = new
    n_states[0] = moment
    n_states[1] = second
    n_avg[...] = average
    n_copy[...] = new.astype(bf16)


def update(devices, parts, fix, got, sums, weight, norm, pm, ps, nm, ns, km, ks):
    feats, channels = weight.shape
    shapes = []
    for m, states in ((pm, (feats, 2, channels)), (nm, (2,) + nm.shape), (km, (2,) + km.shape)):
        shapes.append(jax.ShapeDtypeStruct(m.shape, f32))
        shapes.append(jax.ShapeDtypeStruct(states, f32))
        shapes.append(jax.ShapeDtypeStruct(m.shape, f32))
        shapes.append(jax.ShapeDtypeStruct(m.shape, bf16))
    return pl.pallas_call(
        functools.partial(step_body, devices, parts),
        in_specs=smem(1) + vmem(10),
        out_specs=vmem(12),
        out_shape=shapes,
        scratch_shapes=[pltpu.VMEM((LANES, LANES), f32)],
        name="update",
    )(fix, got, sums, weight, norm, pm, ps, nm, ns, km, ks)


def shifted(x, by):
    length = lax.axis_size("rows")
    pairs = [(i, i + by) for i in range(length) if 0 <= i + by < length]
    return lax.ppermute(x, "rows", pairs)


def exchange(x):
    return lax.all_to_all(x, ("rows", "scene"), 0, 0, tiled=True)


def body(
    points,
    pillar_counts,
    pillar_pixels,
    point_weight,
    point_master,
    point_states,
    norm_weight,
    norm_master,
    norm_states,
    kernel_weight,
    kernel_master,
    kernel_states,
    step_count,
    cotangent,
):
    size = points.shape[3]
    out_rows, scenes, channels, out_cols = cotangent.shape
    cols = 2 * out_cols
    devices = lax.axis_size("rows")
    scene_devices = lax.axis_size("scene")
    peers = devices * scene_devices
    cells = float(out_rows * scenes * out_cols * peers)
    own = kernel_weight.shape[0]
    parts = scene_devices if own % scene_devices == 0 else 1
    share = own // parts * channels
    mine = lax.axis_index("scene") if parts > 1 else jnp.int32(0)

    z, winner, edge, stats, moments = lift(
        mine.reshape(1, 1), points, pillar_counts, pillar_pixels, point_weight, norm_weight, kernel_weight.T, peers, share
    )
    edge = shifted(edge, 1)
    got = exchange(stats)
    held = scenes // 2 * EDGE
    far_pixels = edge[held : held + scenes].astype(jnp.int32)
    pairs = out_rows // 2
    own_pixels = pillar_pixels.reshape(scenes * pairs, 1, size // pairs)
    conv, pooled, sums, kernel = convolve(
        devices, parts, own_pixels, far_pixels, got, z, edge, norm_weight, pairs, out_cols
    )
    conv_stats = exchange(sums[:, None])

    far_pixels = far_pixels[:, :EDGE]
    at = (pillar_pixels % cols) // 2
    own_at = (pillar_pixels // (2 * cols) + 1) * (out_cols + 8) + at
    take_at = jnp.concatenate([own_at, (far_pixels % cols) // 2], axis=1)
    take_at = jnp.pad(take_at, ((0, 0), (0, -(size + EDGE) % (16 * pairs))))
    take_at = take_at.reshape(scenes * pairs, 1, take_at.shape[1] // pairs)
    own_phase = (pillar_pixels // cols % 2) * 2 + pillar_pixels % 2
    phase = jnp.concatenate([own_phase, 2 + far_pixels % 2], axis=1)
    phase = jnp.pad(phase, ((0, 0), (0, LANES - EDGE))).astype(f32)[:, None]

    result, sums = normalize(cells, conv_stats, conv, cotangent, norm_weight)
    grad_sums = exchange(sums[:, None])
    slots, own_edge, far, kgrad = gradients(
        cells, devices, parts, take_at, conv_stats, grad_sums, conv, cotangent, norm_weight, pooled, phase, kernel
    )
    far = shifted(far, -1)
    if parts > 1:
        kgrad = lax.all_to_all(kgrad, "scene", 0, 0, tiled=True)
    else:
        kgrad = lax.psum(kgrad, "scene")
    inner, bias = unlift(points, pillar_counts, point_weight, norm_weight, winner, slots)
    far, kgrad, inner, bias = lax.optimization_barrier((far, kgrad, inner, bias))
    payload = unlift_edges(
        devices, parts, peers, points, pillar_counts, point_weight, norm_weight, winner, own_edge, far, moments, inner, bias, kgrad
    )
    got = exchange(payload)
    steps_done = step_count[0].astype(f32)
    fix = jnp.stack([1.0 - beta_one**steps_done, 1.0 - beta_two**steps_done])
    outs = update(
        devices,
        parts,
        fix,
        got,
        grad_sums,
        point_weight,
        norm_weight,
        point_master,
        jnp.transpose(point_states, (1, 0, 2)),
        norm_master,
        norm_states,
        kernel_master.T,
        jnp.transpose(kernel_states, (0, 2, 1)),
    )
    outs = list(outs)
    outs[1] = jnp.transpose(outs[1], (1, 0, 2))
    outs[8], outs[10], outs[11] = outs[8].T, outs[10].T, outs[11].T
    outs[9] = jnp.transpose(outs[9], (0, 2, 1))
    return (result, *outs)


def solution(mesh):
    placed = (
        P("scene", None, None, "rows"),
        P("scene", "rows"),
        P("scene", "rows"),
        P(),
        P(),
        P(),
        P(),
        P(),
        P(),
        P("rows", None),
        P("rows", None),
        P(None, "rows", None),
        P(),
        P("rows", "scene", None, None),
    )
    return jax.shard_map(
        body,
        mesh=mesh,
        in_specs=placed,
        out_specs=(
            P("rows", "scene", None, None),
            P(),
            P(),
            P(),
            P(),
            P(),
            P(),
            P(),
            P(),
            P("rows", None),
            P(None, "rows", None),
            P("rows", None),
            P("rows", None),
        ),
        check_vma=False,
    )
```
